32 devices in a mesh: dp: 8 (over z, y), tensor: 4 (over x, core).
Axes of the slice: x: 2, y: 2, z: 4, core: 2. Of those that a mesh axis runs over, the one named last changes fastest.
Arguments:
- layer_input: bfloat16 [8192, 1024], P(('dp', 'tensor')), may hold values from -22 to 22
- out_grad: bfloat16 [8192, 1024], P(('dp', 'tensor')), may hold values from -6 to 6
- segment_ids: int32 [8192], P('dp'), may hold values from 0 to 24, as said below
- valid_mask: int32 [8192], P(('dp', 'tensor')), may hold values from 0 to 1, as said below
- doc_start: int32 [8192], P('dp'), may hold values from 0 to 1023, as said below
- norm_gains: bfloat16 [2, 1024], P(None, ('dp', 'tensor')), may hold values from 0.099609375 to 1.8984375
- conv_weight: bfloat16 [4, 1792], P(None, ('dp', 'tensor')), may hold values from -3 to 3
- conv_bias: bfloat16 [1792], P(('dp', 'tensor')), may hold values from -3 to 3
- mixer_gain: bfloat16 [1536], P(('dp', 'tensor')), may hold values from 0.099609375 to 1.8984375
- shared_proj: bfloat16 [1024, 512], P(('dp', 'tensor')), may hold values from -0.1875 to 0.1875
- step_bias: float32 [24], replicated, may hold values from -5 to -1
- decay_log: float32 [24], replicated, may hold values from -2 to 1.5
- skip_gain: float32 [24], replicated, may hold values from 0.5 to 1.5
- mamba_gate: bfloat16 [1024, 1536], P('dp', 'tensor'), may hold values from -0.1875 to 0.1875
- mamba_input: bfloat16 [1024, 1536], P('dp', 'tensor'), may hold values from -0.1875 to 0.1875
- mamba_step: bfloat16 [1024, 24], P('dp', 'tensor'), may hold values from -0.1875 to 0.1875
- query_proj: bfloat16 [1024, 512], P('dp', 'tensor'), may hold values from -0.1875 to 0.1875
- mamba_out: bfloat16 [1536, 1024], P('tensor', 'dp'), may hold values from -0.15625 to 0.15625
- attention_out: bfloat16 [512, 1024], P('tensor', 'dp'), may hold values from -2 to 2
- swiglu_gate: bfloat16 [1024, 2048], P('dp', 'tensor'), may hold values from -0.1875 to 0.1875
- swiglu_up: bfloat16 [1024, 2048], P('dp', 'tensor'), may hold values from -0.1875 to 0.1875
- swiglu_down: bfloat16 [2048, 1024], P('tensor', 'dp'), may hold values from -0.125 to 0.125
Outputs:
- layer_output: bfloat16 [8192, 1024], P(('dp', 'tensor'))
- input_grad: float32 [8192, 1024], P(('dp', 'tensor'))
- norm_gains_grad: float32 [2, 1024], P(None, ('dp', 'tensor'))
- conv_weight_grad: float32 [4, 1792], P(None, ('dp', 'tensor'))
- conv_bias_grad: float32 [1792], P(('dp', 'tensor'))
- mixer_gain_grad: float32 [1536], P(('dp', 'tensor'))
- shared_proj_grad: float32 [1024, 512], P(('dp', 'tensor'))
- step_bias_grad: float32 [24], replicated
- decay_log_grad: float32 [24], replicated
- skip_gain_grad: float32 [24], replicated
- mamba_gate_grad: float32 [1024, 1536], P('dp', 'tensor')
- mamba_input_grad: float32 [1024, 1536], P('dp', 'tensor')
- mamba_step_grad: float32 [1024, 24], P('dp', 'tensor')
- query_proj_grad: float32 [1024, 512], P('dp', 'tensor')
- mamba_out_grad: float32 [1536, 1024], P('tensor', 'dp')
- attention_out_grad: float32 [512, 1024], P('tensor', 'dp')
- swiglu_gate_grad: float32 [1024, 2048], P('dp', 'tensor')
- swiglu_up_grad: float32 [1024, 2048], P('dp', 'tensor')
- swiglu_down_grad: float32 [2048, 1024], P('tensor', 'dp')
- residual_rms: float32 [5], replicated
The draws below stay inside these ranges and needn't reach their ends.
Inputs may be any that keep to these rules, and one draw needn't show every extreme that they name: `segment_ids`: within each sequence of 1024 tokens the ids start at 0 and never fall; the padding at a sequence's end, 16 to 128 tokens, has id 24. `valid_mask`: 1 exactly where the segment id is below 24. `doc_start`: the position in its sequence of the token's first document token; for padding, the first padding position.
All inputs are finite; a program needn't handle non-finite values.
Results may differ from the reference program's by a relative error of at most 0.02.
Values may be sent and summed in bfloat16 or wider, within the bound.
No kernel may reach another device: no remote copies, remote signals or barrier semaphores. Data moves between devices by JAX's collectives and lax.ppermute only.
A program may use at most 192 MiB of HBM per device.

```python
import math
import jax
import jax.numpy as jnp
from jax import lax

D = 1024
MH = 24
HEAD_SIZE = 64
MAMBA_STATES = 128
CONV = 4
QUERY_HEADS = 8
KEY_VALUE_HEADS = 2
FF = 2048
SEQUENCE_TOKENS = 1024
NDOC = 24
DSSM = 1536
CH = 1792
NSH = 512
TOKENS = 8192
N_TENSOR = 4


def packing(key):
    seq_count = TOKENS // SEQUENCE_TOKENS
    length_key, pad_key = jax.random.split(jax.random.fold_in(key, 11))
    shortest = max(1, SEQUENCE_TOKENS * 60 // 1024)
    longest = max(shortest + 1, SEQUENCE_TOKENS * 800 // 1024 + 1)
    lengths = jax.random.randint(length_key, (seq_count, NDOC), shortest, longest, dtype=jnp.int32)
    doc_ends = jnp.cumsum(lengths, axis=1)
    padding = jax.random.randint(pad_key, (seq_count, 1), max(1, SEQUENCE_TOKENS // 64), SEQUENCE_TOKENS // 8 + 1, dtype=jnp.int32)
    live_len = SEQUENCE_TOKENS - padding
    positions = jnp.arange(SEQUENCE_TOKENS, dtype=jnp.int32)[None, :]
    document = jnp.sum((doc_ends[:, None, :] <= positions[:, :, None]).astype(jnp.int32), axis=2)
    document = jnp.minimum(document, NDOC - 1)
    starts = jnp.concatenate([jnp.zeros((seq_count, 1), jnp.int32), doc_ends[:, :-1]], axis=1)
    doc_begin = jnp.take_along_axis(starts, document, axis=1)
    is_valid = positions < live_len
    segment = jnp.where(is_valid, document, NDOC)
    doc_begin = jnp.where(is_valid, doc_begin, live_len)
    return (segment.reshape(-1).astype(jnp.int32), is_valid.astype(jnp.int32).reshape(-1), doc_begin.reshape(-1).astype(jnp.int32))


def draw_segment_ids(key, part):
    return packing(key)[0]


def draw_valid_mask(key, part):
    return packing(key)[1]


def draw_doc_start(key, part):
    return packing(key)[2]


def draw_layer_input(key, part):
    base_key, scale_key = jax.random.split(jax.random.fold_in(key, 5))
    base_draw = jnp.clip(jax.random.normal(base_key, (TOKENS, D), jnp.float32), -4.0, 4.0)
    spread = jnp.exp(jax.random.uniform(scale_key, (TOKENS, 1), jnp.float32, math.log(0.3), math.log(3.0)))
    rising = 0.6 + 1.2 * jnp.arange(TOKENS, dtype=jnp.float32)[:, None] / TOKENS
    return (base_draw * spread * rising).astype(jnp.bfloat16)


def level_of(own_key, dims, cuts, smallest, top_value):
    def one(dim, shards_of):
        steps = jax.random.uniform(jax.random.fold_in(jax.random.fold_in(own_key, 6), dim), (shards_of,), jnp.float32, smallest / len(cuts), top_value / len(cuts))
        return jnp.repeat(jnp.exp(steps), dims[dim] // shards_of).reshape((-1,) + (1,) * (len(dims) - dim - 1))

    level = one(*cuts[0])
    for cut in cuts[1:]:
        level = level * one(*cut)
    return level


def normal_values(key, extent, scale, bound, shards=(), kind=jnp.bfloat16):
    drawn = jax.random.normal(key, extent, jnp.float32) * scale
    if len(shards) > 0:
        drawn = level_of(key, extent, shards, -0.22, 0.18) * drawn
    return jnp.clip(drawn, min=-bound, max=bound).astype(kind)


def setup_inputs(seed: int = 0) -> dict:
    splits = jax.random.split(jax.random.key(seed), 23)
    return {
        "layer_input": draw_layer_input(jax.random.fold_in(splits[22], 71), 0),
        "out_grad": normal_values(splits[1], (TOKENS, D), 1.0, 6.0, ((0, 32),)),
        "segment_ids": draw_segment_ids(jax.random.fold_in(splits[22], 71), 0),
        "valid_mask": draw_valid_mask(jax.random.fold_in(splits[22], 71), 0),
        "doc_start": draw_doc_start(jax.random.fold_in(splits[22], 71), 0),
        "norm_gains": jnp.clip(1.0 + 0.18 * jax.random.normal(splits[5], (2, D), jnp.float32), 0.099609375, 1.8984375).astype(jnp.bfloat16),
        "conv_weight": normal_values(splits[6], (CONV, CH), CONV ** -0.5, 3.0, ((1, 32),)),
        "conv_bias": normal_values(splits[7], (CH,), 0.5, 3.0, ((0, 32),)),
        "mixer_gain": jnp.clip(1.0 + 0.18 * jax.random.normal(splits[8], (DSSM,), jnp.float32), 0.099609375, 1.8984375).astype(jnp.bfloat16),
        "shared_proj": normal_values(splits[9], (D, NSH), D ** -0.5, 0.1875, ((0, 32),)),
        "step_bias": jnp.clip(jax.random.uniform(splits[10], (MH,), jnp.float32, -5.0, -1.0), -5.0, -1.0),
        "decay_log": jnp.clip(jax.random.uniform(splits[11], (MH,), jnp.float32, -2.0, 1.5), -2.0, 1.5),
        "skip_gain": jnp.clip(jax.random.uniform(splits[12], (MH,), jnp.float32, 0.5, 1.5), 0.5, 1.5),
        "mamba_gate": normal_values(splits[13], (D, DSSM), D ** -0.5, 0.1875, ((0, 8), (1, 4))),
        "mamba_input": normal_values(splits[14], (D, DSSM), D ** -0.5, 0.1875, ((0, 8), (1, 4))),
        "mamba_step": normal_values(splits[15], (D, MH), D ** -0.5, 0.1875, ((0, 8), (1, 4))),
        "query_proj": normal_values(splits[16], (D, QUERY_HEADS * HEAD_SIZE), D ** -0.5, 0.1875, ((0, 8), (1, 4))),
        "mamba_out": normal_values(splits[17], (DSSM, D), DSSM ** -0.5, 0.15625, ((0, 4), (1, 8))),
        "attention_out": normal_values(splits[18], (QUERY_HEADS * HEAD_SIZE, D), (QUERY_HEADS * HEAD_SIZE // 64) ** -0.5, 2.0, ((0, 4), (1, 8))),
        "swiglu_gate": normal_values(splits[19], (D, FF), D ** -0.5, 0.1875, ((0, 8), (1, 4))),
        "swiglu_up": normal_values(splits[20], (D, FF), D ** -0.5, 0.1875, ((0, 8), (1, 4))),
        "swiglu_down": normal_values(splits[21], (FF, D), FF ** -0.5, 0.125, ((0, 4), (1, 8))),
    }


EPS = 1e-05
ROPE_BASE = 100000000000.0
NEG_FILL = -1e+30
HIGH = lax.Precision.HIGHEST

@jax.custom_vjp
def lower_bound(v):
    return lax.optimization_barrier(v.astype(jnp.bfloat16)).astype(jnp.float32)

@jax.custom_vjp
def low_back(v):
    return v

def low_keep(v):
    return (lower_bound(v), None)

def low_pass(kept, grad):
    return (grad,)

def back_keep(v):
    return (v, None)

def back_low(kept, grad):
    return (lower_bound(grad),)
lower_bound.defvjp(low_keep, low_pass)
low_back.defvjp(back_keep, back_low)

def matmul(left, right):
    return jnp.dot(left, right, precision=HIGH)

def rms_scale(values):
    return lax.rsqrt(lax.optimization_barrier(jnp.mean(values * values, axis=-1, keepdims=True)) + EPS)

def rope_tables(position):
    half_width = HEAD_SIZE // 2
    inverse = jnp.exp(jnp.arange(half_width, dtype=jnp.float32) * (-2.0 * math.log(ROPE_BASE) / HEAD_SIZE))
    angles = position.astype(jnp.float32)[:, None] * inverse[None, :]
    return (jnp.cos(angles), jnp.sin(angles))

def apply_rotary(values, cosine_table, sine_table):
    half_width = values.shape[-1] // 2
    first_half = values[..., :half_width]
    second_half = values[..., half_width:]
    cos_col = cosine_table[:, None, :]
    sin_col = sine_table[:, None, :]
    return jnp.concatenate([first_half * cos_col - second_half * sin_col, second_half * cos_col + first_half * sin_col], axis=-1)

def mamba_sequence(x_part, bc_part, raw_part, segments, conv_w, conv_b, bias_part, decay_part, skip_part):
    length = x_part.shape[0]
    head_count = raw_part.shape[1]
    head_width = x_part.shape[1] // head_count
    state_size = bc_part.shape[1] // 2
    conv_input = jnp.concatenate([x_part, bc_part], axis=1)
    tap_count = conv_w.shape[0]
    conv_sum = conv_b[None, :] + conv_w[tap_count - 1][None, :] * conv_input
    for lag_steps in range(1, tap_count):
        lagged = jnp.concatenate([jnp.zeros((lag_steps, conv_input.shape[1]), conv_input.dtype), conv_input[:-lag_steps]], axis=0)
        prior_seg = jnp.concatenate([jnp.full((lag_steps,), -1, jnp.int32), segments[:-lag_steps]], axis=0)
        same_doc = (prior_seg == segments).astype(conv_input.dtype)[:, None]
        conv_sum = conv_sum + conv_w[tap_count - 1 - lag_steps][None, :] * lagged * same_doc
    activated = jax.nn.silu(conv_sum)
    inner_width = head_count * head_width
    conv_x = activated[:, :inner_width].reshape(length, head_count, head_width)
    state_in = activated[:, inner_width:inner_width + state_size]
    state_out = activated[:, inner_width + state_size:]
    step_size = jax.nn.softplus(raw_part + bias_part[None, :])
    decay_rate = step_size * (-jnp.exp(decay_part))[None, :]
    log_decay = jnp.cumsum(decay_rate, axis=0).T
    pair_dot = jnp.dot(state_out, state_in.T, precision=HIGH)
    positions = jnp.arange(length, dtype=jnp.int32)
    allowed = (positions[:, None] >= positions[None, :]) & (segments[:, None] == segments[None, :])
    decay_gap = jnp.where(allowed[None], log_decay[:, :, None] - log_decay[:, None, :], 0.0)
    decay_mat = jnp.where(allowed[None], jnp.exp(decay_gap), 0.0) * pair_dot[None]
    driven = conv_x * step_size[:, :, None]
    mixing = jnp.einsum('hij,jhp->ihp', decay_mat, driven, precision=HIGH)
    return (mixing + skip_part[None, :, None] * conv_x).reshape(length, inner_width)

def sequence_mixer(params, pieces):
    conv_f, shift_f, gain_f, bias_f, decay_f, skip_f = params
    gate_z, mamba_x, step_raw, query_act, common_input, segments, starts = pieces
    head_local = MH // N_TENSOR
    query_slice = QUERY_HEADS // N_TENSOR
    local_width = head_local * HEAD_SIZE
    cosine_table, sine_table = rope_tables(jnp.arange(SEQUENCE_TOKENS, dtype=jnp.int32) - starts)
    token_index = jnp.arange(SEQUENCE_TOKENS, dtype=jnp.int32)
    allowed = (token_index[:, None] >= token_index[None, :]) & (segments[:, None] == segments[None, :])
    score_scale = 1.0 / math.sqrt(HEAD_SIZE)
    mamba_parts = []
    attend_parts = []
    for tensor_position in range(N_TENSOR):
        common_tensor_rank = low_back(common_input)
        channel_lo = tensor_position * local_width
        head_lo = tensor_position * head_local
        conv_rank = jnp.concatenate([conv_f[:, channel_lo:channel_lo + local_width], conv_f[:, DSSM:]], axis=1)
        shift_rank = jnp.concatenate([shift_f[channel_lo:channel_lo + local_width], shift_f[DSSM:]], axis=0)
        mamba_parts.append(mamba_sequence(mamba_x[:, channel_lo:channel_lo + local_width], common_tensor_rank[:, :2 * MAMBA_STATES], step_raw[:, head_lo:head_lo + head_local], segments, conv_rank, shift_rank, bias_f[head_lo:head_lo + head_local], decay_f[head_lo:head_lo + head_local], skip_f[head_lo:head_lo + head_local]))
        query_begin = tensor_position * query_slice
        query_rank = query_act[:, query_begin * HEAD_SIZE:(query_begin + query_slice) * HEAD_SIZE].reshape(SEQUENCE_TOKENS, query_slice, HEAD_SIZE)
        query_rot = lower_bound(apply_rotary(query_rank, cosine_table, sine_table))
        rotated_key = lower_bound(apply_rotary(common_tensor_rank[:, 2 * MAMBA_STATES:2 * MAMBA_STATES + KEY_VALUE_HEADS * HEAD_SIZE].reshape(SEQUENCE_TOKENS, KEY_VALUE_HEADS, HEAD_SIZE), cosine_table, sine_table))
        value_reduced = lower_bound(common_tensor_rank[:, 2 * MAMBA_STATES + KEY_VALUE_HEADS * HEAD_SIZE:].reshape(SEQUENCE_TOKENS, KEY_VALUE_HEADS, HEAD_SIZE))
        key_value_index = [(query_begin + head_total) // (QUERY_HEADS // KEY_VALUE_HEADS) for head_total in range(query_slice)]
        key_sel = jnp.stack([rotated_key[:, kv_num] for kv_num in key_value_index], axis=1)
        value_sel = jnp.stack([value_reduced[:, kv_num] for kv_num in key_value_index], axis=1)
        scores = low_back(jnp.einsum('ihd,jhd->hij', query_rot, key_sel, precision=HIGH) * score_scale)
        attn_probs = lower_bound(jax.nn.softmax(jnp.where(allowed[None], scores, NEG_FILL), axis=-1))
        attended = jnp.einsum('hij,jhd->ihd', attn_probs, value_sel, precision=HIGH)
        attend_parts.append(lower_bound(low_back(attended)).reshape(SEQUENCE_TOKENS, query_slice * HEAD_SIZE))
    mamba_y = jnp.concatenate(mamba_parts, axis=1)
    gated_y = mamba_y * jax.nn.silu(gate_z)
    normed = lower_bound(gated_y * rms_scale(gated_y) * gain_f)
    return (normed, jnp.concatenate(attend_parts, axis=1))

def reference(layer_input, out_grad, segment_ids, valid_mask, doc_start, norm_gains, conv_weight, conv_bias, mixer_gain, shared_proj, step_bias, decay_log, skip_gain, mamba_gate, mamba_input, mamba_step, query_proj, mamba_out, attention_out, swiglu_gate, swiglu_up, swiglu_down):
    floats = tuple((weight_arr.astype(jnp.float32) for weight_arr in (layer_input, norm_gains, conv_weight, conv_bias, mixer_gain, shared_proj, step_bias, decay_log, skip_gain, mamba_gate, mamba_input, mamba_step, query_proj, mamba_out, attention_out, swiglu_gate, swiglu_up, swiglu_down)))
    seq_count = TOKENS // SEQUENCE_TOKENS

    def stacked(values):
        return values.reshape((seq_count, SEQUENCE_TOKENS) + values.shape[1:])

    def forward(tokens_f, gains_f, conv_f, shift_f, mixer_f, shared_w, bias_f, decay_f, skip_f, gate_w, input_w, step_w, query_w, mamba_w, attend_w, ffn_gate_w, ffn_up_w, ffn_down_w):
        first_b = lower_bound(tokens_f * rms_scale(tokens_f) * gains_f[0])
        gate_z = low_back(matmul(first_b, gate_w))
        mamba_x = low_back(matmul(first_b, input_w))
        step_raw = low_back(matmul(first_b, step_w))
        query_act = low_back(matmul(first_b, query_w))
        common_input = matmul(first_b, shared_w)
        params = (conv_f, shift_f, mixer_f, bias_f, decay_f, skip_f)

        def one_sequence(pieces):
            return sequence_mixer(params, pieces)
        normed, attended = lax.map(jax.checkpoint(one_sequence), (stacked(gate_z), stacked(mamba_x), stacked(step_raw), stacked(query_act), stacked(common_input), stacked(segment_ids), stacked(doc_start)))
        mixer_sum = low_back(matmul(normed.reshape(TOKENS, DSSM), mamba_w) + matmul(attended.reshape(TOKENS, QUERY_HEADS * HEAD_SIZE), attend_w))
        middle = tokens_f + mixer_sum
        second_b = lower_bound(middle * rms_scale(middle) * gains_f[1])
        gate_act = low_back(matmul(second_b, ffn_gate_w))
        up_act = low_back(matmul(second_b, ffn_up_w))
        hidden_b = lower_bound(jax.nn.silu(gate_act) * up_act)
        ffn_out = low_back(matmul(hidden_b, ffn_down_w))
        result = middle + ffn_out
        return (result, (mixer_sum, middle, ffn_out))
    result, pullback, parts = jax.vjp(forward, *floats, has_aux=True)
    valid_f = valid_mask.astype(jnp.float32)
    out_cot = out_grad.astype(jnp.float32) * valid_f[:, None]
    grads = pullback(out_cot)
    count_all = jnp.sum(valid_f)
    tracked = (floats[0], parts[0], parts[1], parts[2], result)
    residual_rms = jnp.stack([jnp.sqrt(jnp.sum(valid_f * lax.optimization_barrier(jnp.sum(tracked_arr * tracked_arr, axis=1))) / (count_all * D)) for tracked_arr in tracked])
    return (result.astype(jnp.bfloat16), grads[0], grads[1], grads[2], grads[3], grads[4], grads[5], grads[6], grads[7], grads[8], grads[9], grads[10], grads[11], grads[12], grads[13], grads[14], grads[15], grads[16], grads[17], residual_rms)
```

```python
import functools
import math

import jax
import jax.numpy as jnp
from jax import lax
from jax.experimental import pallas as pl
from jax.experimental.pallas import tpu as pltpu
from jax.sharding import PartitionSpec as P

D = 1024
MH = 24
HEAD_SIZE = 64
MAMBA_STATES = 128
CONV = 4
QUERY_HEADS = 8
KEY_VALUE_HEADS = 2
SEQUENCE_TOKENS = 1024
DSSM = 1536


EPS = 1e-05
ROPE_BASE = 100000000000.0
NEG_FILL = -1e30
HIGH = lax.Precision.HIGHEST


def rms_scale(values):
    return lax.rsqrt(jnp.mean(values * values, axis=-1, keepdims=True) + EPS)


def norm_back(values, row_scale, gain_row, grad_in):
    scaled_grad = grad_in * gain_row
    gain_grad = jnp.sum(grad_in * values * row_scale, axis=0)
    value_grad = row_scale * scaled_grad - values * (row_scale * row_scale * row_scale) * jnp.mean(
        scaled_grad * values, axis=-1, keepdims=True
    )
    return (value_grad, gain_grad)


def product(left, right):
    return jnp.dot(left, right, preferred_element_type=jnp.float32)


def product_tn(left, right):
    return lax.dot_general(
        left, right, (((0,), (0,)), ((), ())), preferred_element_type=jnp.float32
    )


def product_nt(left, right):
    return lax.dot_general(
        left, right, (((1,), (1,)), ((), ())), preferred_element_type=jnp.float32
    )


def split_dot(values, selector, dims):
    high = values.astype(jnp.bfloat16)
    low = (values - high.astype(jnp.float32)).astype(jnp.bfloat16)
    left = lax.dot_general(high, selector, dims, preferred_element_type=jnp.float32)
    return left + lax.dot_general(low, selector, dims, preferred_element_type=jnp.float32)


NN = (((1,), (0,)), ((), ()))
NT = (((1,), (1,)), ((), ()))
TN = (((0,), (0,)), ((), ()))


def mxu(left, right, dims):
    return lax.dot_general(
        left.astype(jnp.bfloat16),
        right.astype(jnp.bfloat16),
        dims,
        preferred_element_type=jnp.float32,
    )


def iota(shape, dim):
    return lax.broadcasted_iota(jnp.int32, shape, dim)


def head_groups(width):
    return [(low, min(low + 2 * HEAD_SIZE, width)) for low in range(0, width, 2 * HEAD_SIZE)]


def chunk_common(chunk, start, width, x_ref, bc_ref, raw_ref, doc_ref, pad_ref, w_ref, par_ref):
    rows = pl.ds(start, chunk)
    doc = doc_ref[rows, :]
    age = start + iota((chunk, 1), 0) - doc
    span = pad_ref[pl.ds(start, chunk + 8), :]
    conv = w_ref[CONV : CONV + 1, :] + w_ref[CONV - 1 : CONV, :] * span[8:, :]
    lagged = [span[8:, :]]
    for lag in range(1, CONV):
        moved = jnp.where(age >= lag, span[8 - lag : 8 - lag + chunk, :], 0.0)
        lagged.append(moved)
        conv = conv + w_ref[CONV - 1 - lag : CONV - lag, :] * moved
    sig = jax.nn.sigmoid(conv)
    act = conv * sig
    raw = raw_ref[rows, :] + par_ref[0:1, :]
    step = jnp.maximum(raw, 0.0) + jnp.log1p(jnp.exp(-jnp.abs(raw)))
    rate = step * par_ref[1:2, :]
    lower = (iota((chunk, chunk), 0) >= iota((chunk, chunk), 1)).astype(jnp.bfloat16)
    high = rate.astype(jnp.bfloat16)
    low = (rate - high.astype(jnp.float32)).astype(jnp.bfloat16)
    total = mxu(lower, high, NN) + mxu(lower, low, NN)
    lanes = par_ref.shape[1]
    spread = (iota((lanes, width), 0) == iota((lanes, width), 1) // HEAD_SIZE).astype(jnp.bfloat16)
    key_pos = start + iota((chunk, chunk), 1)
    allowed = (key_pos <= start + iota((chunk, chunk), 0)) & (key_pos >= doc)
    doc_last = doc[chunk - 1 : chunk, :]
    ends = total[chunk - 1 : chunk, :]
    live = jnp.where(doc < start, jnp.exp(total), 0.0)
    keep = jnp.where(start + iota((chunk, 1), 0) >= doc_last, jnp.exp(ends - total), 0.0)
    carry = jnp.where(doc_last < start, jnp.exp(ends), 0.0)
    wide = split_dot(jnp.concatenate([step, live, keep, jnp.broadcast_to(carry, (8, lanes))], axis=0), spread, NN)
    return dict(
        conv=conv, sig=sig, act=act, raw=raw, step=step, total=total, turned=total.T, spread=spread, allowed=allowed,
        carry=carry, age=age, lagged=lagged, lower=lower,
        step_w=wide[:chunk], live_w=wide[chunk : 2 * chunk], keep_w=wide[2 * chunk : 3 * chunk],
        carry_w=wide[3 * chunk : 3 * chunk + 1],
    )


def decay_of(part, head):
    gap = part["total"][:, head : head + 1] - part["turned"][head : head + 1, :]
    return jnp.where(part["allowed"], jnp.exp(gap), 0.0)


def only(values, low, high):
    lane = iota(values.shape, 1)
    return jnp.where((lane >= low) & (lane < high), values, jnp.zeros_like(values))


def mamba_forward_kernel(
    chunk, width, x_ref, bc_ref, raw_ref, z_ref, doc_ref, w_ref, par_ref, skip_ref, y_ref, square_ref, kept_ref, pad_ref, state_ref
):
    length = x_ref.shape[0]
    pad_ref[0:8, :] = jnp.zeros((8, pad_ref.shape[1]), jnp.float32)
    pad_ref[8:, :width] = x_ref[:, :width]
    pad_ref[8:, width:] = bc_ref[...]
    state_ref[...] = jnp.zeros_like(state_ref)

    def one_chunk(index, _):
        start = pl.multiple_of(index * chunk, chunk)
        rows = pl.ds(start, chunk)
        part = chunk_common(chunk, start, width, x_ref, bc_ref, raw_ref, doc_ref, pad_ref, w_ref, par_ref)
        inner = part["act"][:, :width]
        bm = part["act"][:, width : width + MAMBA_STATES].astype(jnp.bfloat16)
        cm = part["act"][:, width + MAMBA_STATES :].astype(jnp.bfloat16)
        driven = (inner * part["step_w"]).astype(jnp.bfloat16)
        pair = mxu(cm, bm, NT)
        pieces = []
        for low, high in head_groups(width):
            heads = range(low // HEAD_SIZE, high // HEAD_SIZE)
            mats = [(decay_of(part, head) * pair).astype(jnp.bfloat16) for head in heads]
            piece = driven[:, low:high]
            right = [
                only(piece, HEAD_SIZE * k, HEAD_SIZE * (k + 1)) if len(mats) > 1 else piece
                for k in range(len(mats))
            ]
            pieces.append(
                mxu(jnp.concatenate(mats, axis=1), jnp.concatenate(right, axis=0), NN)
            )
        state = state_ref[...]
        kept_ref[pl.ds(pl.multiple_of(index * MAMBA_STATES, MAMBA_STATES), MAMBA_STATES), :] = state
        y = jnp.concatenate(pieces, axis=1) + part["live_w"] * mxu(cm, state, NN)
        y = y + skip_ref[0:1, :] * inner
        state_ref[...] = state * part["carry_w"] + mxu(
            bm, driven.astype(jnp.float32) * part["keep_w"], TN
        )
        y_ref[rows, :] = y
        z = z_ref[rows, :width]
        gated = y * z * jax.nn.sigmoid(z)
        square_ref[:, rows] = split_dot_left(gated * gated)
        return 0

    lax.fori_loop(0, length // chunk, one_chunk, 0)


def split_dot_left(values):
    ones = jnp.ones((8, values.shape[1]), jnp.bfloat16)
    high = values.astype(jnp.bfloat16)
    low = (values - high.astype(jnp.float32)).astype(jnp.bfloat16)
    return mxu(ones, high, NT) + mxu(ones, low, NT)


def mamba_backward_kernel(
    chunk, width, x_ref, bc_ref, raw_ref, z_ref, doc_ref, w_ref, par_ref, skip_ref, gain_ref, y_ref, mixed_ref, rows_ref,
    dq_ref, dkv_ref, kept_ref, din_ref, dcommon_ref, dw_ref, dpar_ref, dskip_ref, pad_ref, state_ref, halo_ref
):
    length = x_ref.shape[0]
    count = length // chunk
    wide = x_ref.shape[1]
    if wide > width:
        din_ref[...] = jnp.zeros_like(din_ref)
    din_ref[:, 2 * wide : 2 * wide + 2 * HEAD_SIZE] = dq_ref[...]
    dcommon_ref[:, 2 * MAMBA_STATES :] = dkv_ref[...]
    pad_ref[0:8, :] = jnp.zeros((8, pad_ref.shape[1]), jnp.float32)
    pad_ref[8:, :width] = x_ref[:, :width]
    pad_ref[8:, width:] = bc_ref[...]
    state_ref[...] = jnp.zeros_like(state_ref)
    halo_ref[...] = jnp.zeros_like(halo_ref)

    @pl.when(pl.program_id(0) == 0)
    def _():
        dw_ref[...] = jnp.zeros_like(dw_ref)
        dpar_ref[...] = jnp.zeros_like(dpar_ref)
        dskip_ref[...] = jnp.zeros_like(dskip_ref)

    def one_chunk(step_index, _):
        index = count - 1 - step_index
        start = pl.multiple_of(index * chunk, chunk)
        rows = pl.ds(start, chunk)
        part = chunk_common(chunk, start, width, x_ref, bc_ref, raw_ref, doc_ref, pad_ref, w_ref, par_ref)
        inner = part["act"][:, :width]
        bm = part["act"][:, width : width + MAMBA_STATES].astype(jnp.bfloat16)
        cm = part["act"][:, width + MAMBA_STATES :].astype(jnp.bfloat16)
        driven = (inner * part["step_w"]).astype(jnp.bfloat16)
        driven_f = driven.astype(jnp.float32)
        y = y_ref[rows, :]
        z = z_ref[rows, :width]
        z_sig = jax.nn.sigmoid(z)
        silu_z = z * z_sig
        gated = y * silu_z
        scale = rows_ref[rows, 0:1]
        normed_grad = mixed_ref[rows, :width]
        dskip_ref[1:2, :] += jnp.sum(normed_grad * gated * scale, axis=0, keepdims=True)
        gated_grad = scale * (normed_grad * gain_ref[0:1, :]) - gated * rows_ref[rows, 1:2]
        dy = gated_grad * silu_z
        din_ref[rows, :width] = (gated_grad * y * z_sig * (1.0 + z * (1.0 - z_sig))).astype(jnp.bfloat16)
        dy_b = dy.astype(jnp.bfloat16)
        pair = mxu(cm, bm, NT)
        pair_grad = jnp.zeros((chunk, chunk), jnp.float32)
        pieces = []
        for low, high in head_groups(width):
            heads = list(range(low // HEAD_SIZE, high // HEAD_SIZE))
            piece = driven[:, low:high]
            grads = [
                only(dy_b[:, low:high], HEAD_SIZE * k, HEAD_SIZE * (k + 1)) if len(heads) > 1 else dy_b[:, low:high]
                for k in range(len(heads))
            ]
            mats = []
            for k, head in enumerate(heads):
                decay = decay_of(part, head)
                mats.append((decay * pair).astype(jnp.bfloat16))
                pair_grad = pair_grad + decay * mxu(grads[k], piece, NT)
            pieces.append(mxu(jnp.concatenate(mats, axis=0), jnp.concatenate(grads, axis=0), TN))
        within = jnp.concatenate(pieces, axis=1)
        state = kept_ref[pl.ds(pl.multiple_of(index * MAMBA_STATES, MAMBA_STATES), MAMBA_STATES), :]
        state_grad = state_ref[...]
        pair_grad = pair_grad.astype(jnp.bfloat16)
        dy_live = (dy * part["live_w"]).astype(jnp.bfloat16)
        driven_keep = (driven_f * part["keep_w"]).astype(jnp.bfloat16)
        later = part["keep_w"] * mxu(bm, state_grad, NN)
        c_grad = mxu(pair_grad, bm, NN) + mxu(dy_live, state, NT)
        b_grad = mxu(pair_grad, cm, TN) + mxu(driven_keep, state_grad, NT)
        state_ref[...] = state_grad * part["carry_w"] + mxu(cm, dy_live, TN)
        driven_grad = within + later
        later_part = driven_f * later
        mixed = y - skip_ref[0:1, :] * inner
        sums = split_dot(
            jnp.concatenate(
                [
                    dy_b.astype(jnp.float32) * mixed - driven_f * within - later_part,
                    driven_grad * inner,
                    jnp.broadcast_to(
                        jnp.sum(later_part, axis=0, keepdims=True)
                        + part["carry_w"] * jnp.sum(state_grad * state, axis=0, keepdims=True),
                        (8, width),
                    ),
                ],
                axis=0,
            ),
            part["spread"],
            NT,
        )
        high = sums[:chunk].astype(jnp.bfloat16)
        low = (sums[:chunk] - high.astype(jnp.float32)).astype(jnp.bfloat16)
        rate_grad = (
            mxu(part["lower"], high, TN) + mxu(part["lower"], low, TN) + sums[2 * chunk : 2 * chunk + 1]
        )
        step_grad = rate_grad * par_ref[1:2, :] + sums[chunk : 2 * chunk]
        raw_grad = step_grad * jax.nn.sigmoid(part["raw"])
        din_ref[rows, 2 * wide + 2 * HEAD_SIZE :] = raw_grad.astype(jnp.bfloat16)
        dpar_ref[0:1, :] += jnp.sum(raw_grad, axis=0, keepdims=True)
        dpar_ref[1:2, :] += par_ref[1:2, :] * jnp.sum(rate_grad * part["step"], axis=0, keepdims=True)
        dskip_ref[0:1, :] += jnp.sum(dy * inner, axis=0, keepdims=True)
        inner_grad = driven_grad * part["step_w"] + skip_ref[0:1, :] * dy
        sig, conv = (part["sig"], part["conv"])
        conv_grad = jnp.concatenate([inner_grad, b_grad, c_grad], axis=1) * (
            sig * (1.0 + conv * (1.0 - sig))
        )
        dw_ref[CONV : CONV + 1, :] += jnp.sum(conv_grad, axis=0, keepdims=True)
        v_grad = w_ref[CONV - 1 : CONV, :] * conv_grad
        long = jnp.concatenate([conv_grad, halo_ref[...]], axis=0)
        next_start = jnp.minimum(start + chunk, length - 8)
        ages = jnp.concatenate([part["age"], start + chunk + iota((8, 1), 0) - doc_ref[pl.ds(pl.multiple_of(next_start, 8), 8), :]], axis=0)
        dw_ref[CONV - 1 : CONV, :] += jnp.sum(conv_grad * part["lagged"][0], axis=0, keepdims=True)
        for lag in range(1, CONV):
            dw_ref[CONV - 1 - lag : CONV - lag, :] += jnp.sum(
                conv_grad * part["lagged"][lag], axis=0, keepdims=True
            )
            masked = jnp.where(ages >= lag, long, 0.0)
            v_grad = v_grad + w_ref[CONV - 1 - lag : CONV - lag, :] * masked[lag : lag + chunk, :]
        halo_ref[...] = conv_grad[:8, :]
        din_ref[rows, wide : wide + width] = v_grad[:, :width].astype(jnp.bfloat16)
        dcommon_ref[rows, : 2 * MAMBA_STATES] = v_grad[:, width:].astype(jnp.bfloat16)
        return 0

    lax.fori_loop(0, count, one_chunk, 0)


CHUNK = 128
VMEM_LIMIT = 60 * 1024 * 1024


def columns_of(width, place=0):
    return pl.BlockSpec((SEQUENCE_TOKENS, width), lambda i: (i, place))


def whole_spec(shape):
    return pl.BlockSpec(shape, lambda i: (0,) * len(shape))


def mamba_forward(in_act, common, doc, taps, params, skip_row, chunk=CHUNK):
    tokens = in_act.shape[0]
    width = skip_row.shape[1]
    lanes = params.shape[1]
    wide = (in_act.shape[1] - 2 * lanes) // 2
    seq = SEQUENCE_TOKENS
    count = tokens // seq
    kept = seq // chunk * MAMBA_STATES
    return pl.pallas_call(
        functools.partial(mamba_forward_kernel, chunk, width),
        grid=(count,),
        in_specs=[
            columns_of(wide, 1),
            columns_of(2 * MAMBA_STATES),
            columns_of(lanes, 2 * wide // lanes + 1),
            columns_of(wide),
            columns_of(1),
            whole_spec(taps.shape),
            whole_spec(params.shape),
            whole_spec(skip_row.shape),
        ],
        out_specs=[
            columns_of(width),
            pl.BlockSpec((8, seq), lambda i: (0, i)),
            pl.BlockSpec((kept, width), lambda i: (i, 0)),
        ],
        out_shape=[
            jax.ShapeDtypeStruct((tokens, width), jnp.float32),
            jax.ShapeDtypeStruct((8, tokens), jnp.float32),
            jax.ShapeDtypeStruct((count * kept, width), jnp.float32),
        ],
        scratch_shapes=[
            pltpu.VMEM((seq + 8, width + 2 * MAMBA_STATES), jnp.float32),
            pltpu.VMEM((MAMBA_STATES, width), jnp.float32),
        ],
        compiler_params=pltpu.CompilerParams(vmem_limit_bytes=VMEM_LIMIT),
        cost_estimate=pl.CostEstimate(
            flops=tokens * width * 20000, bytes_accessed=tokens * width * 20, transcendentals=0
        ),
    )(in_act, common, in_act, in_act, doc, taps, params, skip_row)


def mamba_backward(
    in_act, common, doc, taps, params, skip_row, y, mixed_grad, rows_of, gain_row, dq, dkv, kept_states, chunk=CHUNK
):
    tokens = in_act.shape[0]
    width = skip_row.shape[1]
    lanes = params.shape[1]
    wide = (in_act.shape[1] - 2 * lanes) // 2
    seq = SEQUENCE_TOKENS
    count = tokens // seq
    kept = seq // chunk * MAMBA_STATES
    conv_width = width + 2 * MAMBA_STATES
    return pl.pallas_call(
        functools.partial(mamba_backward_kernel, chunk, width),
        grid=(count,),
        in_specs=[
            columns_of(wide, 1),
            columns_of(2 * MAMBA_STATES),
            columns_of(lanes, 2 * wide // lanes + 1),
            columns_of(wide),
            columns_of(1),
            whole_spec(taps.shape),
            whole_spec(params.shape),
            whole_spec(skip_row.shape),
            whole_spec(gain_row.shape),
            columns_of(width),
            columns_of(mixed_grad.shape[1]),
            columns_of(rows_of.shape[1]),
            columns_of(dq.shape[1]),
            columns_of(dkv.shape[1]),
            pl.BlockSpec((kept, width), lambda i: (i, 0)),
        ],
        out_specs=[
            columns_of(in_act.shape[1]),
            columns_of(common.shape[1]),
            whole_spec((8, conv_width)),
            whole_spec((8, lanes)),
            whole_spec((8, width)),
        ],
        out_shape=[
            jax.ShapeDtypeStruct(in_act.shape, jnp.bfloat16),
            jax.ShapeDtypeStruct(common.shape, jnp.bfloat16),
            jax.ShapeDtypeStruct((8, conv_width), jnp.float32),
            jax.ShapeDtypeStruct((8, lanes), jnp.float32),
            jax.ShapeDtypeStruct((8, width), jnp.float32),
        ],
        scratch_shapes=[
            pltpu.VMEM((seq + 8, conv_width), jnp.float32),
            pltpu.VMEM((MAMBA_STATES, width), jnp.float32),
            pltpu.VMEM((8, conv_width), jnp.float32),
        ],
        compiler_params=pltpu.CompilerParams(vmem_limit_bytes=VMEM_LIMIT),
        cost_estimate=pl.CostEstimate(
            flops=tokens * width * 60000, bytes_accessed=tokens * width * 20, transcendentals=0
        ),
    )(
        in_act, common, in_act, in_act, doc, taps, params, skip_row, gain_row, y, mixed_grad, rows_of, dq, dkv, kept_states
    )


NEGATIVE = -1e30
QUERY_BLOCK = 256


def swap_halves(values):
    half = HEAD_SIZE // 2
    lane = iota(values.shape, 1)
    width = values.shape[1]
    return jnp.where(
        lane % HEAD_SIZE < half,
        pltpu.roll(values, width - half, 1),
        pltpu.roll(values, half, 1),
    )


def attention_mask(start, rows, keys, doc):
    position = start + iota((rows, 1), 0)
    key_pos = iota((rows, keys), 1)
    return (key_pos <= position) & (key_pos >= doc)


def both_heads(values):
    return jnp.concatenate(
        [only(values, 0, HEAD_SIZE), only(values, HEAD_SIZE, 2 * HEAD_SIZE)], axis=0
    )


def chosen(values, kv):
    lane = iota(values.shape, 1)
    turned = pltpu.roll(values, HEAD_SIZE, 1)
    return jnp.where((lane < HEAD_SIZE) == (kv == 0), values, turned)


def attention_forward_kernel(
    kv_ref, q_ref, key_ref, value_ref, cos_ref, sin_ref, doc_ref, out_ref, qr_ref, kr_ref, vr_ref, log_ref
):
    length = q_ref.shape[0]
    kv = kv_ref[0]
    cos, sin = (cos_ref[...], sin_ref[...])
    query = q_ref[...]
    qr_ref[...] = ((query * cos + swap_halves(query) * sin).astype(jnp.bfloat16).astype(jnp.float32) * HEAD_SIZE**-0.5).astype(jnp.bfloat16)
    key = key_ref[...]
    kr_ref[...] = chosen(key * cos + swap_halves(key) * sin, kv).astype(jnp.bfloat16)
    vr_ref[...] = chosen(value_ref[...], kv).astype(jnp.bfloat16)
    rows = QUERY_BLOCK
    for start in range(0, length, rows):
        keys = start + rows
        block = slice(start, start + rows)
        mask = attention_mask(start, rows, keys, doc_ref[block, :])
        scores = mxu(both_heads(qr_ref[block, :]), kr_ref[0:keys, :], NT)
        outs = []
        logs = []
        for head in range(2):
            part = jnp.where(mask, scores[head * rows : (head + 1) * rows], NEGATIVE)
            peak = jnp.max(part, axis=1, keepdims=True)
            weight = jnp.exp(part - peak)
            total = jnp.sum(weight, axis=1, keepdims=True)
            outs.append(mxu(weight * (1.0 / total), vr_ref[0:keys, :], NN))
            logs.append(peak + jnp.log(total))
        lane = iota((rows, 2 * HEAD_SIZE), 1)
        out_ref[block, :] = jnp.where(lane < HEAD_SIZE, outs[0], outs[1]).astype(jnp.bfloat16)
        log_ref[block, :] = jnp.where(lane < HEAD_SIZE, logs[0], logs[1])


def attention_backward_kernel(
    kv_ref, qr_ref, kr_ref, vr_ref, cos_ref, sin_ref, doc_ref, log_ref, grad_ref, dq_ref, dkv_ref, dk_ref, dv_ref
):
    length = qr_ref.shape[0]
    kv = kv_ref[0]
    rows = QUERY_BLOCK
    dk_ref[...] = jnp.zeros_like(dk_ref)
    dv_ref[...] = jnp.zeros_like(dv_ref)
    for start in range(0, length, rows):
        keys = start + rows
        block = slice(start, start + rows)
        mask = attention_mask(start, rows, keys, doc_ref[block, :])
        query = both_heads(qr_ref[block, :])
        grad = both_heads(grad_ref[block, :])
        logs = log_ref[block, :]
        scores = mxu(query, kr_ref[0:keys, :], NT)
        prob_grad = mxu(grad, vr_ref[0:keys, :], NT)
        probs = []
        score_grads = []
        for head in range(2):
            mine = slice(head * rows, (head + 1) * rows)
            log = logs[:, head * HEAD_SIZE : head * HEAD_SIZE + 1]
            weight = jnp.where(mask, jnp.exp(scores[mine] - log), 0.0)
            product_grad = weight * prob_grad[mine]
            total = jnp.sum(product_grad, axis=1, keepdims=True)
            probs.append(weight.astype(jnp.bfloat16))
            score_grads.append((product_grad - weight * total).astype(jnp.bfloat16))
        lane = iota((rows, 2 * HEAD_SIZE), 1)
        dq = mxu(jnp.concatenate(score_grads, axis=0), kr_ref[0:keys, :], NN)
        dq = jnp.where(lane < HEAD_SIZE, dq[:rows], dq[rows:]) * HEAD_SIZE**-0.5
        dq = dq * cos_ref[block, :] - swap_halves(dq) * sin_ref[block, :]
        dq_ref[block, :] = dq.astype(jnp.bfloat16)
        dk_ref[0:keys, :] += mxu(jnp.concatenate(score_grads, axis=0), query, TN)
        dv_ref[0:keys, :] += mxu(jnp.concatenate(probs, axis=0), grad, TN)
    lane = iota((length, 2 * HEAD_SIZE), 1)
    mine = (lane < HEAD_SIZE) == (kv == 0)
    dk = dk_ref[...]
    dk = dk + pltpu.roll(dk, HEAD_SIZE, 1)
    dk = dk * cos_ref[...] - swap_halves(dk) * sin_ref[...]
    dv = dv_ref[...]
    dv = dv + pltpu.roll(dv, HEAD_SIZE, 1)
    dkv_ref[:, : 2 * HEAD_SIZE] = jnp.where(mine, dk, 0.0).astype(jnp.bfloat16)
    dkv_ref[:, 2 * HEAD_SIZE :] = jnp.where(mine, dv, 0.0).astype(jnp.bfloat16)


def attention_call(kernel, kv, tokens, ins, places, outs, scratch, flops):
    seq = SEQUENCE_TOKENS
    return pl.pallas_call(
        kernel,
        grid_spec=pltpu.PrefetchScalarGridSpec(
            num_scalar_prefetch=1,
            grid=(tokens // seq,),
            in_specs=[
                pl.BlockSpec((seq, columns), functools.partial(lambda place, i, kv: (i, place), place))
                for columns, place in places
            ],
            out_specs=[pl.BlockSpec((seq, columns), lambda i, kv: (i, 0)) for columns, _ in outs],
            scratch_shapes=scratch,
        ),
        out_shape=[jax.ShapeDtypeStruct((tokens, columns), kind) for columns, kind in outs],
        compiler_params=pltpu.CompilerParams(vmem_limit_bytes=VMEM_LIMIT),
        cost_estimate=pl.CostEstimate(flops=flops * tokens, bytes_accessed=tokens * 4096, transcendentals=0),
    )(kv, *ins)


def attention_forward(kv, in_act, common, cos, sin, doc):
    two = 2 * HEAD_SIZE
    low, full = (jnp.bfloat16, jnp.float32)
    return attention_call(
        attention_forward_kernel,
        kv,
        in_act.shape[0],
        (in_act, common, common, cos, sin, doc),
        (
            (two, in_act.shape[1] // two - 2),
            (two, 2 * MAMBA_STATES // two),
            (two, 2 * MAMBA_STATES // two + 1),
            (two, 0),
            (two, 0),
            (1, 0),
        ),
        ((two, low), (two, low), (two, low), (two, low), (two, full)),
        [],
        4000000,
    )


def attention_backward(kv, qr, kr, vr, cos, sin, doc, log, grad):
    two = 2 * HEAD_SIZE
    seq = SEQUENCE_TOKENS
    ins = (qr, kr, vr, cos, sin, doc, log, grad)
    return attention_call(
        attention_backward_kernel,
        kv,
        qr.shape[0],
        ins,
        [(a.shape[1], 0) for a in ins],
        ((two, jnp.bfloat16), (2 * two, jnp.bfloat16)),
        [pltpu.VMEM((seq, two), jnp.float32), pltpu.VMEM((seq, two), jnp.float32)],
        9000000,
    )


def rope_rows(position):
    lane = jnp.arange(2 * HEAD_SIZE, dtype=jnp.int32)
    half = HEAD_SIZE // 2
    inverse = jnp.exp(
        (lane % half).astype(jnp.float32) * (-2.0 * math.log(ROPE_BASE) / HEAD_SIZE)
    )
    angles = position.astype(jnp.float32)[:, None] * inverse[None, :]
    sign = jnp.where(lane % HEAD_SIZE < half, -1.0, 1.0)
    return (jnp.cos(angles), jnp.sin(angles) * sign[None, :])
def grid_of(count):
    rows = 1
    while 8 * rows * rows <= count:
        rows *= 2
    return (count // rows, rows)


def ring_cycle(count):
    depth, rows = grid_of(count)
    order = []
    for level in range(depth):
        inner = list(range(1, rows))
        if level % 2:
            inner.reverse()
        order += [level * rows + row for row in inner]
    return order + [level * rows for level in reversed(range(depth))]


class Ring:
    def __init__(self, count):
        self.count = count
        self.order = ring_cycle(count)
        place = [0] * count
        for spot, device in enumerate(self.order):
            place[device] = spot
        self.spot = jnp.asarray(place, jnp.int32)[lax.axis_index("dp")]
        self.table = jnp.asarray(self.order + self.order, jnp.int32)

    def device_at(self, offset):
        return self.table[(self.spot + offset + self.count) % self.count]

    def send(self, block, step):
        count, order = (self.count, self.order)
        return lax.ppermute(
            block, "dp", [(order[k], order[(k + step) % count]) for k in range(count)]
        )


def ring_gather(ring, block):
    count = ring.count
    rows = block.shape[0]
    half = rows // 2
    out = jnp.zeros((count * rows,) + block.shape[1:], block.dtype)

    def put(out, piece, offset, extra=0):
        return lax.dynamic_update_slice_in_dim(
            out, piece, ring.device_at(offset) * rows + extra, 0
        )

    out = put(out, block, 0)
    ahead = behind = block
    for step in range(1, count // 2):
        ahead = ring.send(ahead, 1)
        behind = ring.send(behind, -1)
        out = put(out, ahead, -step)
        out = put(out, behind, step)
    out = put(out, ring.send(ahead[:half], 1), -(count // 2))
    return put(out, ring.send(behind[half:], -1), count // 2, half)


def ring_scatter(ring, values):
    count = ring.count
    rows = values.shape[0] // count
    half = rows // 2

    def piece(offset, start=0, size=rows):
        return lax.dynamic_slice_in_dim(
            values, ring.device_at(offset) * rows + start, size, 0
        ).astype(jnp.float32)

    far = count // 2
    ahead = ring.send(piece(far, 0, half).astype(jnp.bfloat16), 1).astype(jnp.float32)
    behind = ring.send(piece(far, half, rows - half).astype(jnp.bfloat16), -1).astype(jnp.float32)
    ahead = jnp.concatenate([ahead, jnp.zeros_like(behind)], axis=0)
    behind = jnp.concatenate([jnp.zeros_like(ahead[:half]), behind], axis=0)
    for offset in range(far - 1, 0, -1):
        ahead = ring.send((ahead + piece(offset)).astype(jnp.bfloat16), 1).astype(jnp.float32)
        behind = ring.send((behind + piece(-offset)).astype(jnp.bfloat16), -1).astype(jnp.float32)
    return ahead + behind + piece(0)


def core_swap(block):
    count = lax.axis_size("tensor")
    return lax.ppermute(block, "tensor", [(k, k ^ 1) for k in range(count)])


def chip_shift(block, step):
    count = lax.axis_size("tensor")
    return lax.ppermute(block, "tensor", [(k, (k + 2 * step) % count) for k in range(count)])


def tensor_stack(block):
    count = lax.axis_size("tensor")
    mine = lax.axis_index("tensor")
    out = jnp.zeros((count,) + block.shape, block.dtype)
    put = lax.dynamic_update_index_in_dim
    out = put(out, block, mine, 0)
    others = [(chip_shift(block, step), (mine + count - 2 * step) % count) for step in range(1, count // 2)]
    out = put(out, core_swap(block), mine ^ 1, 0)
    for other, source in others:
        out = put(out, other, source, 0)
        out = put(out, core_swap(other), source ^ 1, 0)
    return out


def seq_gather(values):
    return tensor_stack(values).reshape((-1,) + values.shape[1:])


def tensor_scatter(pick, dtype):
    count = lax.axis_size("tensor")
    mine = lax.axis_index("tensor")
    received = []
    for step in range(1, count // 2):
        target = (mine + 2 * step) % count
        from_mate = core_swap(pick(target ^ 1).astype(dtype)).astype(jnp.float32)
        merged = (pick(target).astype(jnp.float32) + from_mate).astype(dtype)
        received.append(chip_shift(merged, step).astype(jnp.float32))
    total = pick(mine).astype(jnp.float32) + core_swap(pick(mine ^ 1).astype(dtype)).astype(jnp.float32)
    for other in received:
        total = total + other
    return total


def seq_reduce(values):
    rows = values.shape[0] // lax.axis_size("tensor")
    lowered = values.astype(jnp.bfloat16)
    return tensor_scatter(
        lambda index: lax.dynamic_slice_in_dim(lowered, index * rows, rows, 0), jnp.bfloat16
    )


def width_total(values):
    return jnp.sum(tensor_stack(values), axis=0)


def dp_exchange(pieces):
    count = lax.axis_size("dp")
    mine = lax.axis_index("dp")
    out = jnp.zeros_like(pieces)
    for step in range(count):
        piece = lax.dynamic_index_in_dim(pieces, (mine + step) % count, 0, False)
        if step:
            piece = lax.ppermute(piece, "dp", [(k, (k + step) % count) for k in range(count)])
        out = lax.dynamic_update_index_in_dim(out, piece, (mine + count - step) % count, 0)
    return out


def dp_stack(block):
    count = lax.axis_size("dp")
    mine = lax.axis_index("dp")
    out = jnp.zeros((count,) + block.shape, block.dtype)
    for step in range(count):
        piece = block
        if step:
            piece = lax.ppermute(block, "dp", [(k, (k + step) % count) for k in range(count)])
        out = lax.dynamic_update_index_in_dim(out, piece, (mine + count - step) % count, 0)
    return out


def after(value, *others):
    return lax.optimization_barrier((value,) + others)[0]


def local(
    layer_input,
    out_grad,
    segment_ids,
    valid_mask,
    doc_start,
    norm_gains,
    conv_weight,
    conv_bias,
    mixer_gain,
    shared_proj,
    step_bias,
    decay_log,
    skip_gain,
    mamba_gate,
    mamba_input,
    mamba_step,
    query_proj,
    mamba_out,
    attention_out,
    swiglu_gate,
    swiglu_up,
    swiglu_down,
):
    tensor_position = lax.axis_index("tensor")
    dp_count = lax.axis_size("dp")
    tensor_count = lax.axis_size("tensor")
    ring = Ring(dp_count)
    local_width = mamba_gate.shape[1]
    query_width = query_proj.shape[1]
    head_local = mamba_step.shape[1]
    hidden_width = swiglu_gate.shape[1]
    slab = 2 * HEAD_SIZE
    wide = -(-local_width // slab) * slab
    in_width = 2 * wide + slab

    def padded(values, columns):
        return jnp.pad(values, ((0, 0), (0, columns - values.shape[1])))

    x_full = seq_gather(layer_input)
    small = jnp.concatenate(
        [norm_gains.reshape(-1), conv_weight.reshape(-1), conv_bias, mixer_gain]
    )
    small = jnp.pad(small, (0, shared_proj.shape[1] - small.shape[0]))
    common = dp_stack(jnp.concatenate([shared_proj, small[None]], axis=0))
    common = tensor_stack(common)
    common = jnp.swapaxes(common, 0, 1)
    shared_w = common[:, :, :-1].reshape(-1, shared_proj.shape[1])
    small_all = common[:, :, -1].reshape(dp_count * tensor_count, -1)
    w_in = ring_gather(
        ring,
        jnp.concatenate(
            [
                padded(mamba_gate, wide),
                padded(mamba_input, wide),
                padded(query_proj, slab),
                padded(mamba_step, slab),
            ],
            axis=1,
        ),
    )
    w_out = ring_gather(
        ring, after(jnp.concatenate([mamba_out.T, attention_out.T], axis=1), w_in)
    )
    w_ffn = lax.all_gather(
        after(jnp.concatenate([swiglu_gate, swiglu_up, swiglu_down.T], axis=1), w_in),
        "dp",
        axis=0,
        tiled=True,
    )
    ffn_gate_up_w = w_ffn[:, : 2 * hidden_width]
    ffn_down_w = w_ffn[:, 2 * hidden_width :]
    cuts = []
    spot = 0
    for piece in (norm_gains, conv_weight, conv_bias, mixer_gain):
        size = piece.size
        cuts.append(small_all[:, spot : spot + size])
        spot += size
    gains_all = jnp.swapaxes(cuts[0].reshape(-1, 2, norm_gains.shape[1]), 0, 1).reshape(2, -1)
    conv_all = jnp.swapaxes(cuts[1].reshape(-1, CONV, conv_weight.shape[1]), 0, 1).reshape(CONV, -1)
    shift_all = cuts[2].reshape(-1)
    mixer_gain_all = cuts[3].reshape(-1)
    tokens_f = layer_input.astype(jnp.float32)
    gains_f = gains_all.astype(jnp.float32)
    scale_one = rms_scale(tokens_f)
    x_wide = x_full.astype(jnp.float32)
    first_full = (x_wide * rms_scale(x_wide) * gains_f[0]).astype(jnp.bfloat16)
    tokens_per_group = first_full.shape[0]
    seq_count = tokens_per_group // SEQUENCE_TOKENS
    query_slice = query_width // HEAD_SIZE
    channel_start = tensor_position * local_width
    head_start = tensor_position * head_local
    in_act = product(first_full, w_in)
    common_input = product(first_full, shared_w)
    conv_f = conv_all.astype(jnp.float32)
    shift_f = shift_all.astype(jnp.float32)
    own_conv = jnp.concatenate(
        [lax.dynamic_slice_in_dim(conv_f, channel_start, local_width, 1), conv_f[:, DSSM:]], axis=1
    )
    own_shift = jnp.concatenate(
        [lax.dynamic_slice_in_dim(shift_f, channel_start, local_width, 0), shift_f[DSSM:]], axis=0
    )
    own_bias = lax.dynamic_slice_in_dim(step_bias, head_start, head_local, 0)
    own_decay = lax.dynamic_slice_in_dim(decay_log, head_start, head_local, 0)
    own_skip = lax.dynamic_slice_in_dim(skip_gain, head_start, head_local, 0)
    own_gain = lax.dynamic_slice_in_dim(
        mixer_gain_all.astype(jnp.float32), channel_start, local_width, 0
    )
    doc = doc_start[:, None]
    taps = jnp.concatenate(
        [own_conv, own_shift[None], jnp.zeros((3, own_conv.shape[1]), jnp.float32)], axis=0
    )
    params = jnp.pad(
        jnp.stack([own_bias, -jnp.exp(own_decay)], axis=0), ((0, 6), (0, slab - head_local))
    )
    skip_row = jnp.broadcast_to(jnp.repeat(own_skip, HEAD_SIZE)[None], (8, local_width))
    gain_row = jnp.broadcast_to(own_gain[None], (8, local_width))
    position = jnp.tile(jnp.arange(SEQUENCE_TOKENS, dtype=jnp.int32), seq_count) - doc_start
    cosine_table, sine_table = rope_rows(position)
    kv = (tensor_position * query_slice // (QUERY_HEADS // KEY_VALUE_HEADS)).astype(jnp.int32)[None]
    mamba_y, square_rows, kept_states = mamba_forward(in_act, common_input, doc, taps, params, skip_row)
    attended, query_rot, key_rot, value_low, log_total = attention_forward(
        kv, in_act, common_input, cosine_table, sine_table, doc
    )
    square_sum = width_total(square_rows[0])
    gate_scale = lax.rsqrt(square_sum / DSSM + EPS)[:, None]
    gate_z = in_act[:, :local_width]
    gated_y = mamba_y * jax.nn.silu(gate_z)
    normed_b = (gated_y * gate_scale * own_gain).astype(jnp.bfloat16)
    attended_flat = attended[:, :query_width]
    mixed_b = jnp.concatenate([normed_b, attended_flat], axis=1)
    mixer_sum = seq_reduce(product_nt(mixed_b, w_out))
    middle = tokens_f + mixer_sum
    scale_two = rms_scale(middle)
    second_b = (middle * scale_two * gains_f[1]).astype(jnp.bfloat16)
    ffn_in = seq_gather(second_b)
    ffn_act = product(ffn_in, ffn_gate_up_w)
    gate_act = ffn_act[:, :hidden_width]
    up_act = ffn_act[:, hidden_width:]
    hidden_b = (jax.nn.silu(gate_act) * up_act).astype(jnp.bfloat16)
    ffn_part = product_nt(hidden_b, ffn_down_w)
    ffn_out = seq_reduce(ffn_part)
    result = middle + ffn_out
    valid_f = valid_mask.astype(jnp.float32)
    out_cot = out_grad.astype(jnp.float32) * valid_f[:, None]
    cot_b = out_cot.astype(jnp.bfloat16)
    ffn_grad_in = seq_gather(after(cot_b, w_in))
    hidden_grad = product(ffn_grad_in, ffn_down_w)
    sigmoid_gate = jax.nn.sigmoid(gate_act)
    gate_up_grad = jnp.concatenate(
        [
            hidden_grad * up_act * sigmoid_gate * (1.0 + gate_act * (1.0 - sigmoid_gate)),
            hidden_grad * jax.nn.silu(gate_act),
        ],
        axis=1,
    ).astype(jnp.bfloat16)
    second_grad = seq_reduce(product_nt(gate_up_grad, ffn_gate_up_w))
    ffn_w_grad = jnp.concatenate(
        [product_tn(ffn_in, gate_up_grad), product_tn(ffn_grad_in, hidden_b)], axis=1
    ).astype(jnp.bfloat16)
    ffn_w_grad = lax.psum_scatter(
        after(ffn_w_grad, second_grad), "dp", scatter_dimension=0, tiled=True
    ).astype(jnp.float32)
    gate_w_grad = ffn_w_grad[:, :hidden_width]
    up_w_grad = ffn_w_grad[:, hidden_width : 2 * hidden_width]
    down_w_grad = ffn_w_grad[:, 2 * hidden_width :].T
    second_value_grad, gain_two_grad = norm_back(middle, scale_two, gains_f[1], second_grad)
    middle_grad = out_cot + second_value_grad
    mixer_grad_full = seq_gather(middle_grad.astype(jnp.bfloat16))
    out_w_grad = product_tn(mixer_grad_full, mixed_b).astype(jnp.bfloat16)
    mixed_grad = product(mixer_grad_full, w_out)
    normed_grad = mixed_grad[:, :local_width]
    attended_grad = padded(mixed_grad[:, local_width:].astype(jnp.bfloat16), slab)
    inner_sum = width_total(jnp.sum(normed_grad * own_gain * gated_y, axis=1))
    dq, dkv = attention_backward(
        kv, query_rot, key_rot, value_low, cosine_table, sine_table, doc, log_total, attended_grad
    )
    row_terms = jnp.concatenate(
        [gate_scale, gate_scale * gate_scale * gate_scale * (inner_sum / DSSM)[:, None]], axis=1
    )
    in_grad, shared_grad, taps_grad, params_grad, rows_grad = mamba_backward(
        in_act, common_input, doc, taps, params, skip_row, mamba_y, mixed_grad, row_terms, gain_row, dq, dkv, kept_states
    )
    conv_grad = taps_grad[:CONV]
    shift_grad = taps_grad[CONV]
    bias_grad = params_grad[0, :head_local]
    decay_grad = params_grad[1, :head_local]
    skip_grad = jnp.sum(rows_grad[0].reshape(head_local, HEAD_SIZE), axis=1)
    own_gain_grad = rows_grad[1]
    first_part = product_nt(in_grad, w_in) + product_nt(shared_grad, shared_w)
    gain_one_grad = jnp.sum(first_part * x_wide * rms_scale(x_wide), axis=0)
    first_grad = seq_reduce(first_part)
    first_value_grad, _ = norm_back(tokens_f, scale_one, gains_f[0], first_grad)
    input_grad = middle_grad + first_value_grad
    out_w_grad = ring_scatter(ring, out_w_grad)
    mamba_out_grad = out_w_grad[:, :local_width].T
    attend_out_grad = out_w_grad[:, local_width:].T
    in_w_grad = ring_scatter(ring, product_tn(first_full, in_grad).astype(jnp.bfloat16))
    gate_proj_grad = in_w_grad[:, :local_width]
    input_proj_grad = in_w_grad[:, wide : wide + local_width]
    query_proj_grad = in_w_grad[:, 2 * wide : 2 * wide + query_width]
    step_proj_grad = in_w_grad[:, in_width : in_width + head_local]
    shared_w_grad = product_tn(first_full, shared_grad).reshape(
        dp_count, tensor_count, -1, shared_proj.shape[1]
    ).astype(jnp.bfloat16)
    shared_w_grad = tensor_scatter(
        lambda index: lax.dynamic_index_in_dim(shared_w_grad, index, 1, False), jnp.bfloat16
    )
    shared_proj_grad = jnp.sum(
        dp_exchange(shared_w_grad.astype(jnp.bfloat16)).astype(jnp.float32), axis=0
    )
    zero_row = jnp.zeros((DSSM,), jnp.float32)
    conv_rows = jnp.concatenate([conv_grad, shift_grad[None]], axis=0)
    conv_rows = jnp.concatenate(
        [
            lax.dynamic_update_slice_in_dim(
                jnp.zeros((CONV + 1, DSSM), jnp.float32), conv_rows[:, :local_width], channel_start, 1
            ),
            conv_rows[:, local_width:],
        ],
        axis=1,
    )
    gain_row = lax.dynamic_update_slice_in_dim(zero_row, own_gain_grad, channel_start, 0)
    gains_rows = jnp.stack([gain_one_grad, gain_two_grad], axis=0)
    device_count = dp_count * tensor_count

    def by_device(rows_in):
        return jnp.swapaxes(rows_in.reshape(rows_in.shape[0], device_count, -1), 0, 1).reshape(
            device_count, -1
        )

    scattered = jnp.concatenate(
        [by_device(gains_rows), by_device(conv_rows), by_device(gain_row[None])], axis=1
    ).reshape(dp_count, tensor_count, -1)
    scattered = tensor_scatter(
        lambda index: lax.dynamic_index_in_dim(scattered, index, 1, False), jnp.float32
    )
    bias_full = lax.dynamic_update_slice_in_dim(
        jnp.zeros((MH,), jnp.float32), bias_grad, head_start, 0
    )
    decay_full = lax.dynamic_update_slice_in_dim(
        jnp.zeros((MH,), jnp.float32), decay_grad, head_start, 0
    )
    skip_full = lax.dynamic_update_slice_in_dim(
        jnp.zeros((MH,), jnp.float32), skip_grad, head_start, 0
    )
    tracked = (tokens_f, mixer_sum, middle, ffn_out, result)
    stat_terms = jnp.stack(
        [jnp.sum(valid_f * jnp.sum(tracked_arr * tracked_arr, axis=1)) for tracked_arr in tracked]
    )
    everywhere = width_total(
        jnp.concatenate([stat_terms, jnp.sum(valid_f)[None], bias_full, decay_full, skip_full])
    )
    last = dp_exchange(
        jnp.concatenate(
            [
                scattered,
                jnp.broadcast_to(everywhere[None], (dp_count, everywhere.shape[0])),
            ],
            axis=1,
        )
    )
    last = jnp.sum(last, axis=0)
    gain_cols, conv_cols, mix_cols = (norm_gains.shape[1], conv_weight.shape[1], mixer_gain.shape[0])
    gains_grad = last[: 2 * gain_cols].reshape(2, gain_cols)
    spot = 2 * gain_cols
    conv_full_grad = last[spot : spot + CONV * conv_cols].reshape(CONV, conv_cols)
    spot += CONV * conv_cols
    shift_full_grad = last[spot : spot + conv_cols]
    spot += conv_cols
    gain_full_grad = last[spot : spot + mix_cols]
    spot += mix_cols
    stat_totals, count_all = (last[spot : spot + 5], last[spot + 5])
    bias_total = last[spot + 6 : spot + 6 + MH]
    decay_total = last[spot + 6 + MH : spot + 6 + 2 * MH]
    skip_total = last[spot + 6 + 2 * MH :]
    residual_rms = jnp.sqrt(stat_totals / (count_all * D))
    return (
        result.astype(jnp.bfloat16),
        input_grad,
        gains_grad,
        conv_full_grad,
        shift_full_grad,
        gain_full_grad,
        shared_proj_grad,
        bias_total,
        decay_total,
        skip_total,
        gate_proj_grad,
        input_proj_grad,
        step_proj_grad,
        query_proj_grad,
        mamba_out_grad,
        attend_out_grad,
        gate_w_grad,
        up_w_grad,
        down_w_grad,
        residual_rms,
    )


def solution(mesh):
    in_specs = (
        P(("dp", "tensor"), None),
        P(("dp", "tensor"), None),
        P("dp"),
        P(("dp", "tensor")),
        P("dp"),
        P(None, ("dp", "tensor")),
        P(None, ("dp", "tensor")),
        P(("dp", "tensor")),
        P(("dp", "tensor")),
        P(("dp", "tensor"), None),
        P(),
        P(),
        P(),
        P("dp", "tensor"),
        P("dp", "tensor"),
        P("dp", "tensor"),
        P("dp", "tensor"),
        P("tensor", "dp"),
        P("tensor", "dp"),
        P("dp", "tensor"),
        P("dp", "tensor"),
        P("tensor", "dp"),
    )
    out_specs = (
        P(("dp", "tensor"), None),
        P(("dp", "tensor"), None),
        P(None, ("dp", "tensor")),
        P(None, ("dp", "tensor")),
        P(("dp", "tensor")),
        P(("dp", "tensor")),
        P(("dp", "tensor"), None),
        P(),
        P(),
        P(),
        P("dp", "tensor"),
        P("dp", "tensor"),
        P("dp", "tensor"),
        P("dp", "tensor"),
        P("tensor", "dp"),
        P("tensor", "dp"),
        P("dp", "tensor"),
        P("dp", "tensor"),
        P("tensor", "dp"),
        P(),
    )
    return jax.shard_map(local, mesh=mesh, in_specs=in_specs, out_specs=out_specs, check_vma=False)
```

```python
import functools
import math

import jax
import jax.numpy as jnp
from jax import lax
from jax.experimental import pallas as pl
from jax.experimental.pallas import tpu as pltpu
from jax.sharding import PartitionSpec as P

D = 1024
MH = 24
HEAD_SIZE = 64
MAMBA_STATES = 128
CONV = 4
QUERY_HEADS = 8
KEY_VALUE_HEADS = 2
SEQUENCE_TOKENS = 1024
DSSM = 1536


EPS = 1e-05
ROPE_BASE = 100000000000.0
NEG_FILL = -1e30
HIGH = lax.Precision.HIGHEST


def rms_scale(values):
    return lax.rsqrt(jnp.mean(values * values, axis=-1, keepdims=True) + EPS)


def norm_back(values, row_scale, gain_row, grad_in):
    scaled_grad = grad_in * gain_row
    gain_grad = jnp.sum(grad_in * values * row_scale, axis=0)
    value_grad = row_scale * scaled_grad - values * (row_scale * row_scale * row_scale) * jnp.mean(
        scaled_grad * values, axis=-1, keepdims=True
    )
    return (value_grad, gain_grad)


def product(left, right):
    return jnp.dot(left, right, preferred_element_type=jnp.float32)


def product_tn(left, right):
    return lax.dot_general(
        left, right, (((0,), (0,)), ((), ())), preferred_element_type=jnp.float32
    )


def product_nt(left, right):
    return lax.dot_general(
        left, right, (((1,), (1,)), ((), ())), preferred_element_type=jnp.float32
    )


def split_dot(values, selector, dims):
    high = values.astype(jnp.bfloat16)
    low = (values - high.astype(jnp.float32)).astype(jnp.bfloat16)
    left = lax.dot_general(high, selector, dims, preferred_element_type=jnp.float32)
    return left + lax.dot_general(low, selector, dims, preferred_element_type=jnp.float32)


NN = (((1,), (0,)), ((), ()))
NT = (((1,), (1,)), ((), ()))
TN = (((0,), (0,)), ((), ()))


def mxu(left, right, dims):
    return lax.dot_general(
        left.astype(jnp.bfloat16),
        right.astype(jnp.bfloat16),
        dims,
        preferred_element_type=jnp.float32,
    )


def iota(shape, dim):
    return lax.broadcasted_iota(jnp.int32, shape, dim)


def head_groups(width):
    return [(low, min(low + 2 * HEAD_SIZE, width)) for low in range(0, width, 2 * HEAD_SIZE)]


def chunk_common(chunk, start, rows, width, raw_ref, doc_ref, pad_ref, w_ref, par_ref):
    doc = doc_ref[pl.ds(start, chunk), :]
    age = start + iota((chunk, 1), 0) - doc
    span = pad_ref[pl.ds(start, chunk + 8), :]
    conv = w_ref[CONV : CONV + 1, :] + w_ref[CONV - 1 : CONV, :] * span[8:, :]
    lagged = [span[8:, :]]
    for lag in range(1, CONV):
        moved = jnp.where(age >= lag, span[8 - lag : 8 - lag + chunk, :], 0.0)
        lagged.append(moved)
        conv = conv + w_ref[CONV - 1 - lag : CONV - lag, :] * moved
    sig = jax.nn.sigmoid(conv)
    act = conv * sig
    raw = raw_ref[rows, :] + par_ref[0:1, :]
    step = jnp.maximum(raw, 0.0) + jnp.log1p(jnp.exp(-jnp.abs(raw)))
    rate = step * par_ref[1:2, :]
    lower = (iota((chunk, chunk), 0) >= iota((chunk, chunk), 1)).astype(jnp.bfloat16)
    high = rate.astype(jnp.bfloat16)
    low = (rate - high.astype(jnp.float32)).astype(jnp.bfloat16)
    total = mxu(lower, high, NN) + mxu(lower, low, NN)
    lanes = par_ref.shape[1]
    spread = (iota((lanes, width), 0) == iota((lanes, width), 1) // HEAD_SIZE).astype(jnp.bfloat16)
    key_pos = start + iota((chunk, chunk), 1)
    allowed = (key_pos <= start + iota((chunk, chunk), 0)) & (key_pos >= doc)
    doc_last = doc[chunk - 1 : chunk, :]
    ends = total[chunk - 1 : chunk, :]
    live = jnp.where(doc < start, jnp.exp(total), 0.0)
    keep = jnp.where(start + iota((chunk, 1), 0) >= doc_last, jnp.exp(ends - total), 0.0)
    carry = jnp.where(doc_last < start, jnp.exp(ends), 0.0)
    wide = split_dot(jnp.concatenate([step, live, keep, jnp.broadcast_to(carry, (8, lanes))], axis=0), spread, NN)
    return dict(
        conv=conv, sig=sig, act=act, raw=raw, step=step, total=total, turned=total.T, spread=spread, allowed=allowed,
        carry=carry, age=age, lagged=lagged, lower=lower,
        step_w=wide[:chunk], live_w=wide[chunk : 2 * chunk], keep_w=wide[2 * chunk : 3 * chunk],
        carry_w=wide[3 * chunk : 3 * chunk + 1],
    )


def decay_of(part, head):
    gap = part["total"][:, head : head + 1] - part["turned"][head : head + 1, :]
    return jnp.where(part["allowed"], jnp.exp(gap), 0.0)


def only(values, low, high):
    lane = iota(values.shape, 1)
    return jnp.where((lane >= low) & (lane < high), values, jnp.zeros_like(values))


def place_of(order_ref, block_rows, length, start):
    token = pl.program_id(0) * length + start
    return pl.multiple_of(
        order_ref[token // block_rows] * block_rows + token % block_rows, 128
    )


def fill_conv_input(order_ref, block_rows, width, x_ref, bc_ref, pad_ref):
    length = pad_ref.shape[0] - 8
    pad_ref[0:8, :] = jnp.zeros((8, pad_ref.shape[1]), jnp.float32)
    for start in range(0, length, block_rows):
        rows = pl.ds(place_of(order_ref, block_rows, length, start), block_rows)
        pad_ref[8 + start : 8 + start + block_rows, :width] = x_ref[rows, :width]
        pad_ref[8 + start : 8 + start + block_rows, width:] = bc_ref[rows, :]


def mamba_forward_kernel(
    chunk, width, block_rows, order_ref, x_ref, bc_ref, raw_ref, z_ref, doc_ref, w_ref, par_ref, skip_ref, y_ref, square_ref, kept_ref, pad_ref, state_ref
):
    length = pad_ref.shape[0] - 8
    fill_conv_input(order_ref, block_rows, width, x_ref, bc_ref, pad_ref)
    state_ref[...] = jnp.zeros_like(state_ref)

    def one_chunk(index, _):
        start = pl.multiple_of(index * chunk, chunk)
        rows = pl.ds(place_of(order_ref, block_rows, length, start), chunk)
        part = chunk_common(chunk, start, rows, width, raw_ref, doc_ref, pad_ref, w_ref, par_ref)
        inner = part["act"][:, :width]
        bm = part["act"][:, width : width + MAMBA_STATES].astype(jnp.bfloat16)
        cm = part["act"][:, width + MAMBA_STATES :].astype(jnp.bfloat16)
        driven = (inner * part["step_w"]).astype(jnp.bfloat16)
        pair = mxu(cm, bm, NT)
        pieces = []
        for low, high in head_groups(width):
            heads = range(low // HEAD_SIZE, high // HEAD_SIZE)
            mats = [(decay_of(part, head) * pair).astype(jnp.bfloat16) for head in heads]
            piece = driven[:, low:high]
            right = [
                only(piece, HEAD_SIZE * k, HEAD_SIZE * (k + 1)) if len(mats) > 1 else piece
                for k in range(len(mats))
            ]
            pieces.append(
                mxu(jnp.concatenate(mats, axis=1), jnp.concatenate(right, axis=0), NN)
            )
        state = state_ref[...]
        kept_ref[pl.ds(pl.multiple_of(index * MAMBA_STATES, MAMBA_STATES), MAMBA_STATES), :] = state
        y = jnp.concatenate(pieces, axis=1) + part["live_w"] * mxu(cm, state, NN)
        y = y + skip_ref[0:1, :] * inner
        state_ref[...] = state * part["carry_w"] + mxu(
            bm, driven.astype(jnp.float32) * part["keep_w"], TN
        )
        y_ref[rows, :] = y
        z = z_ref[rows, :width]
        gated = y * z * jax.nn.sigmoid(z)
        square_ref[:, rows] = split_dot_left(gated * gated)
        return 0

    lax.fori_loop(0, length // chunk, one_chunk, 0)


def split_dot_left(values):
    ones = jnp.ones((8, values.shape[1]), jnp.bfloat16)
    high = values.astype(jnp.bfloat16)
    low = (values - high.astype(jnp.float32)).astype(jnp.bfloat16)
    return mxu(ones, high, NT) + mxu(ones, low, NT)


def mamba_backward_kernel(
    chunk, width, block_rows, order_ref, x_ref, bc_ref, raw_ref, doc_ref, w_ref, par_ref, skip_ref, y_ref, dy_ref,
    dkv_ref, kept_ref, din_ref, dw_ref, dpar_ref, pad_ref, state_ref, halo_ref, dskip_ref
):
    length = pad_ref.shape[0] - 8
    count = length // chunk
    wide = x_ref.shape[1]
    common_at = wide + 2 * HEAD_SIZE

    @pl.when(pl.program_id(0) == 0)
    def _():
        if wide > width:
            din_ref[...] = jnp.zeros_like(din_ref)
        din_ref[:, common_at + 2 * MAMBA_STATES :] = dkv_ref[...]

    fill_conv_input(order_ref, block_rows, width, x_ref, bc_ref, pad_ref)
    state_ref[...] = jnp.zeros_like(state_ref)
    halo_ref[...] = jnp.zeros_like(halo_ref)

    @pl.when(pl.program_id(0) == 0)
    def _():
        dw_ref[...] = jnp.zeros_like(dw_ref)
        dpar_ref[...] = jnp.zeros_like(dpar_ref)
        dskip_ref[...] = jnp.zeros_like(dskip_ref)

    def one_chunk(step_index, _):
        index = count - 1 - step_index
        start = pl.multiple_of(index * chunk, chunk)
        rows = pl.ds(place_of(order_ref, block_rows, length, start), chunk)
        part = chunk_common(chunk, start, rows, width, raw_ref, doc_ref, pad_ref, w_ref, par_ref)
        inner = part["act"][:, :width]
        bm = part["act"][:, width : width + MAMBA_STATES].astype(jnp.bfloat16)
        cm = part["act"][:, width + MAMBA_STATES :].astype(jnp.bfloat16)
        driven = (inner * part["step_w"]).astype(jnp.bfloat16)
        driven_f = driven.astype(jnp.float32)
        y = y_ref[rows, :]
        dy = dy_ref[rows, :]
        dy_b = dy.astype(jnp.bfloat16)
        pair = mxu(cm, bm, NT)
        pair_grad = jnp.zeros((chunk, chunk), jnp.float32)
        pieces = []
        for low, high in head_groups(width):
            heads = list(range(low // HEAD_SIZE, high // HEAD_SIZE))
            piece = driven[:, low:high]
            grads = [
                only(dy_b[:, low:high], HEAD_SIZE * k, HEAD_SIZE * (k + 1)) if len(heads) > 1 else dy_b[:, low:high]
                for k in range(len(heads))
            ]
            mats = []
            for k, head in enumerate(heads):
                decay = decay_of(part, head)
                mats.append((decay * pair).astype(jnp.bfloat16))
                pair_grad = pair_grad + decay * mxu(grads[k], piece, NT)
            pieces.append(mxu(jnp.concatenate(mats, axis=0), jnp.concatenate(grads, axis=0), TN))
        within = jnp.concatenate(pieces, axis=1)
        state = kept_ref[pl.ds(pl.multiple_of(index * MAMBA_STATES, MAMBA_STATES), MAMBA_STATES), :]
        state_grad = state_ref[...]
        pair_grad = pair_grad.astype(jnp.bfloat16)
        dy_live = (dy * part["live_w"]).astype(jnp.bfloat16)
        driven_keep = (driven_f * part["keep_w"]).astype(jnp.bfloat16)
        later = part["keep_w"] * mxu(bm, state_grad, NN)
        c_grad = mxu(pair_grad, bm, NN) + mxu(dy_live, state, NT)
        b_grad = mxu(pair_grad, cm, TN) + mxu(driven_keep, state_grad, NT)
        state_ref[...] = state_grad * part["carry_w"] + mxu(cm, dy_live, TN)
        driven_grad = within + later
        later_part = driven_f * later
        mixed = y - skip_ref[0:1, :] * inner
        sums = split_dot(
            jnp.concatenate(
                [
                    dy_b.astype(jnp.float32) * mixed - driven_f * within - later_part,
                    driven_grad * inner,
                    jnp.broadcast_to(
                        jnp.sum(later_part, axis=0, keepdims=True)
                        + part["carry_w"] * jnp.sum(state_grad * state, axis=0, keepdims=True),
                        (8, width),
                    ),
                ],
                axis=0,
            ),
            part["spread"],
            NT,
        )
        high = sums[:chunk].astype(jnp.bfloat16)
        low = (sums[:chunk] - high.astype(jnp.float32)).astype(jnp.bfloat16)
        rate_grad = (
            mxu(part["lower"], high, TN) + mxu(part["lower"], low, TN) + sums[2 * chunk : 2 * chunk + 1]
        )
        step_grad = rate_grad * par_ref[1:2, :] + sums[chunk : 2 * chunk]
        raw_grad = step_grad * jax.nn.sigmoid(part["raw"])
        din_ref[rows, wide:common_at] = raw_grad.astype(jnp.bfloat16)
        dpar_ref[0:1, :] += jnp.sum(raw_grad, axis=0, keepdims=True)
        dpar_ref[1:2, :] += par_ref[1:2, :] * jnp.sum(rate_grad * part["step"], axis=0, keepdims=True)
        dskip_ref[0:1, :] += jnp.sum(dy * inner, axis=0, keepdims=True)
        inner_grad = driven_grad * part["step_w"] + skip_ref[0:1, :] * dy
        sig, conv = (part["sig"], part["conv"])
        conv_grad = jnp.concatenate([inner_grad, b_grad, c_grad], axis=1) * (
            sig * (1.0 + conv * (1.0 - sig))
        )
        dw_ref[CONV : CONV + 1, :] += jnp.sum(conv_grad, axis=0, keepdims=True)
        v_grad = w_ref[CONV - 1 : CONV, :] * conv_grad
        long = jnp.concatenate([conv_grad, halo_ref[...]], axis=0)
        next_start = jnp.minimum(start + chunk, length - 8)
        ages = jnp.concatenate([part["age"], start + chunk + iota((8, 1), 0) - doc_ref[pl.ds(pl.multiple_of(next_start, 8), 8), :]], axis=0)
        dw_ref[CONV - 1 : CONV, :] += jnp.sum(conv_grad * part["lagged"][0], axis=0, keepdims=True)
        for lag in range(1, CONV):
            dw_ref[CONV - 1 - lag : CONV - lag, :] += jnp.sum(
                conv_grad * part["lagged"][lag], axis=0, keepdims=True
            )
            masked = jnp.where(ages >= lag, long, 0.0)
            v_grad = v_grad + w_ref[CONV - 1 - lag : CONV - lag, :] * masked[lag : lag + chunk, :]
        halo_ref[...] = conv_grad[:8, :]
        din_ref[rows, :width] = v_grad[:, :width].astype(jnp.bfloat16)
        din_ref[rows, common_at : common_at + 2 * MAMBA_STATES] = v_grad[:, width:].astype(jnp.bfloat16)
        return 0

    lax.fori_loop(0, count, one_chunk, 0)

    @pl.when(pl.program_id(0) == pl.num_programs(0) - 1)
    def _():
        lanes = dpar_ref.shape[1]
        spread = (iota((lanes, width), 0) == iota((lanes, width), 1) // HEAD_SIZE).astype(jnp.bfloat16)
        dpar_ref[2:3, :] = split_dot(dskip_ref[...], spread, NT)[0:1]


CHUNK = 128
VMEM_LIMIT = 60 * 1024 * 1024


def tokens_spec(tokens, width, place=0):
    return pl.BlockSpec((tokens, width), lambda i, *_: (0, place))


def whole_spec(shape):
    return pl.BlockSpec(shape, lambda i, *_: (0,) * len(shape))


def mamba_forward(order, block_rows, early, late, common, doc, taps, params, skip_row, chunk=CHUNK):
    tokens = late.shape[0]
    width = skip_row.shape[1]
    lanes = params.shape[1]
    wide = late.shape[1] - lanes
    seq = SEQUENCE_TOKENS
    count = tokens // seq
    kept = seq // chunk * MAMBA_STATES
    return pl.pallas_call(
        functools.partial(mamba_forward_kernel, chunk, width, block_rows),
        grid_spec=pltpu.PrefetchScalarGridSpec(
        num_scalar_prefetch=1,
        grid=(count,),
        in_specs=[
            tokens_spec(tokens, wide),
            tokens_spec(tokens, 2 * MAMBA_STATES),
            tokens_spec(tokens, lanes, wide // lanes),
            tokens_spec(tokens, wide),
            pl.BlockSpec((seq, 1), lambda i, *_: (i, 0)),
            whole_spec(taps.shape),
            whole_spec(params.shape),
            whole_spec(skip_row.shape),
        ],
        out_specs=[
            tokens_spec(tokens, width),
            whole_spec((8, tokens)),
            pl.BlockSpec((kept, width), lambda i, *_: (i, 0)),
        ],
        scratch_shapes=[
            pltpu.VMEM((seq + 8, width + 2 * MAMBA_STATES), jnp.float32),
            pltpu.VMEM((MAMBA_STATES, width), jnp.float32),
        ],
        ),
        out_shape=[
            jax.ShapeDtypeStruct((tokens, width), jnp.float32),
            jax.ShapeDtypeStruct((8, tokens), jnp.float32),
            jax.ShapeDtypeStruct((count * kept, width), jnp.float32),
        ],
        compiler_params=pltpu.CompilerParams(vmem_limit_bytes=VMEM_LIMIT),
        cost_estimate=pl.CostEstimate(
            flops=tokens * width * 20000, bytes_accessed=tokens * width * 20, transcendentals=0
        ),
    )(order, late, common, late, early, doc, taps, params, skip_row)


def mamba_backward(
    order, block_rows, late, common, doc, taps, params, skip_row, y, dy, dkv, kept_states, chunk=CHUNK
):
    tokens = late.shape[0]
    width = skip_row.shape[1]
    lanes = params.shape[1]
    wide = late.shape[1] - lanes
    seq = SEQUENCE_TOKENS
    count = tokens // seq
    kept = seq // chunk * MAMBA_STATES
    conv_width = width + 2 * MAMBA_STATES
    return pl.pallas_call(
        functools.partial(mamba_backward_kernel, chunk, width, block_rows),
        grid_spec=pltpu.PrefetchScalarGridSpec(
        num_scalar_prefetch=1,
        grid=(count,),
        in_specs=[
            tokens_spec(tokens, wide),
            tokens_spec(tokens, 2 * MAMBA_STATES),
            tokens_spec(tokens, lanes, wide // lanes),
            pl.BlockSpec((seq, 1), lambda i, *_: (i, 0)),
            whole_spec(taps.shape),
            whole_spec(params.shape),
            whole_spec(skip_row.shape),
            tokens_spec(tokens, width),
            tokens_spec(tokens, width),
            tokens_spec(tokens, dkv.shape[1]),
            pl.BlockSpec((kept, width), lambda i, *_: (i, 0)),
        ],
        out_specs=[
            tokens_spec(tokens, late.shape[1] + common.shape[1]),
            whole_spec((8, conv_width)),
            whole_spec((8, lanes)),
        ],
        scratch_shapes=[
            pltpu.VMEM((seq + 8, conv_width), jnp.float32),
            pltpu.VMEM((MAMBA_STATES, width), jnp.float32),
            pltpu.VMEM((8, conv_width), jnp.float32),
            pltpu.VMEM((8, width), jnp.float32),
        ],
        ),
        out_shape=[
            jax.ShapeDtypeStruct((tokens, late.shape[1] + common.shape[1]), jnp.bfloat16),
            jax.ShapeDtypeStruct((8, conv_width), jnp.float32),
            jax.ShapeDtypeStruct((8, lanes), jnp.float32),
        ],
        compiler_params=pltpu.CompilerParams(vmem_limit_bytes=VMEM_LIMIT),
        cost_estimate=pl.CostEstimate(
            flops=tokens * width * 60000, bytes_accessed=tokens * width * 20, transcendentals=0
        ),
    )(
        order, late, common, late, doc, taps, params, skip_row, y, dy, dkv, kept_states
    )


NEGATIVE = -1e30
QUERY_BLOCK = 256


def swap_halves(values):
    half = HEAD_SIZE // 2
    lane = iota(values.shape, 1)
    width = values.shape[1]
    return jnp.where(
        lane % HEAD_SIZE < half,
        pltpu.roll(values, width - half, 1),
        pltpu.roll(values, half, 1),
    )


def attention_mask(start, rows, keys, doc):
    position = start + iota((rows, 1), 0)
    key_pos = iota((rows, keys), 1)
    return (key_pos <= position) & (key_pos >= doc)


def both_heads(values):
    return jnp.concatenate(
        [only(values, 0, HEAD_SIZE), only(values, HEAD_SIZE, 2 * HEAD_SIZE)], axis=0
    )


def chosen(values, kv):
    lane = iota(values.shape, 1)
    turned = pltpu.roll(values, HEAD_SIZE, 1)
    return jnp.where((lane < HEAD_SIZE) == (kv == 0), values, turned)


def attention_forward_kernel(
    block_rows, kv_ref, order_ref, q_ref, key_ref, value_ref, cos_ref, sin_ref, doc_ref, out_ref, qr_ref, kr_ref, vr_ref, log_ref
):
    length = qr_ref.shape[0]
    kv = kv_ref[0]
    rows = block_rows
    for start in range(0, length, rows):
        block = slice(start, start + rows)
        place = pl.ds(place_of(order_ref, block_rows, length, start), rows)
        cos, sin = (cos_ref[block, :], sin_ref[block, :])
        query, key = (q_ref[place, :], key_ref[place, :])
        turned = (query * cos + swap_halves(query) * sin).astype(jnp.bfloat16)
        qr_ref[block, :] = (turned.astype(jnp.float32) * HEAD_SIZE**-0.5).astype(jnp.bfloat16)
        kr_ref[block, :] = chosen(key * cos + swap_halves(key) * sin, kv).astype(jnp.bfloat16)
        vr_ref[block, :] = chosen(value_ref[place, :], kv).astype(jnp.bfloat16)
        keys = start + rows
        mask = attention_mask(start, rows, keys, doc_ref[block, :])
        scores = mxu(both_heads(qr_ref[block, :]), kr_ref[0:keys, :], NT)
        outs = []
        logs = []
        for head in range(2):
            part = jnp.where(mask, scores[head * rows : (head + 1) * rows], NEGATIVE)
            peak = jnp.max(part, axis=1, keepdims=True)
            weight = jnp.exp(part - peak)
            total = jnp.sum(weight, axis=1, keepdims=True)
            outs.append(mxu(weight * (1.0 / total), vr_ref[0:keys, :], NN))
            logs.append(peak + jnp.log(total))
        lane = iota((rows, 2 * HEAD_SIZE), 1)
        out_ref[place, :] = jnp.where(lane < HEAD_SIZE, outs[0], outs[1]).astype(jnp.bfloat16)
        log_ref[block, :] = jnp.where(lane < HEAD_SIZE, logs[0], logs[1])


def attention_backward_kernel(
    block_rows, kv_ref, order_ref, qr_ref, kr_ref, vr_ref, cos_ref, sin_ref, doc_ref, log_ref, grad_ref, dq_ref, dkv_ref, dk_ref, dv_ref
):
    length = qr_ref.shape[0]
    kv = kv_ref[0]
    rows = block_rows
    lane = iota((rows, 2 * HEAD_SIZE), 1)
    mine = (lane < HEAD_SIZE) == (kv == 0)
    dk_ref[...] = jnp.zeros_like(dk_ref)
    dv_ref[...] = jnp.zeros_like(dv_ref)
    for start in reversed(range(0, length, rows)):
        keys = start + rows
        block = slice(start, start + rows)
        place = pl.ds(place_of(order_ref, block_rows, length, start), rows)
        mask = attention_mask(start, rows, keys, doc_ref[block, :])
        query = both_heads(qr_ref[block, :])
        grad = both_heads(grad_ref[place, :].astype(jnp.bfloat16))
        logs = log_ref[block, :]
        scores = mxu(query, kr_ref[0:keys, :], NT)
        prob_grad = mxu(grad, vr_ref[0:keys, :], NT)
        probs = []
        score_grads = []
        for head in range(2):
            part = slice(head * rows, (head + 1) * rows)
            log = logs[:, head * HEAD_SIZE : head * HEAD_SIZE + 1]
            weight = jnp.where(mask, jnp.exp(scores[part] - log), 0.0)
            product_grad = weight * prob_grad[part]
            total = jnp.sum(product_grad, axis=1, keepdims=True)
            probs.append(weight.astype(jnp.bfloat16))
            score_grads.append((product_grad - weight * total).astype(jnp.bfloat16))
        cos, sin = (cos_ref[block, :], sin_ref[block, :])
        dq = mxu(jnp.concatenate(score_grads, axis=0), kr_ref[0:keys, :], NN)
        dq = jnp.where(lane < HEAD_SIZE, dq[:rows], dq[rows:]) * HEAD_SIZE**-0.5
        dq = dq * cos - swap_halves(dq) * sin
        dq_ref[place, :] = dq.astype(jnp.bfloat16)
        dk_ref[0:keys, :] += mxu(jnp.concatenate(score_grads, axis=0), query, TN)
        dv_ref[0:keys, :] += mxu(jnp.concatenate(probs, axis=0), grad, TN)
        dk = dk_ref[block, :]
        dk = dk + pltpu.roll(dk, HEAD_SIZE, 1)
        dk = dk * cos - swap_halves(dk) * sin
        dv = dv_ref[block, :]
        dv = dv + pltpu.roll(dv, HEAD_SIZE, 1)
        dkv_ref[place, : 2 * HEAD_SIZE] = jnp.where(mine, dk, 0.0).astype(jnp.bfloat16)
        dkv_ref[place, 2 * HEAD_SIZE :] = jnp.where(mine, dv, 0.0).astype(jnp.bfloat16)


def attention_call(kernel, kv, order, block_rows, tokens, ins, outs, scratch, flops):
    seq = SEQUENCE_TOKENS

    def spec(columns, place):
        if place is None:
            return pl.BlockSpec((seq, columns), lambda i, *_: (i, 0))
        return tokens_spec(tokens, columns, place)

    return pl.pallas_call(
        functools.partial(kernel, block_rows),
        grid_spec=pltpu.PrefetchScalarGridSpec(
            num_scalar_prefetch=2,
            grid=(tokens // seq,),
            in_specs=[spec(columns, place) for _, columns, place in ins],
            out_specs=[spec(columns, place) for _, columns, place in outs],
            scratch_shapes=scratch,
        ),
        out_shape=[jax.ShapeDtypeStruct((tokens, columns), kind) for kind, columns, _ in outs],
        compiler_params=pltpu.CompilerParams(vmem_limit_bytes=VMEM_LIMIT),
        cost_estimate=pl.CostEstimate(
            flops=flops * tokens, bytes_accessed=tokens * 4096, transcendentals=0
        ),
    )(kv, order, *[value for value, _, _ in ins])


def attention_forward(kv, order, block_rows, early, common, cos, sin, doc):
    two = 2 * HEAD_SIZE
    low, full = (jnp.bfloat16, jnp.float32)
    query_at = early.shape[1] // two - 1
    key_at = 2 * MAMBA_STATES // two
    return attention_call(
        attention_forward_kernel,
        kv,
        order,
        block_rows,
        early.shape[0],
        (
            (early, two, query_at),
            (common, two, key_at),
            (common, two, key_at + 1),
            (cos, two, None),
            (sin, two, None),
            (doc, 1, None),
        ),
        ((low, two, 0), (low, two, None), (low, two, None), (low, two, None), (full, two, None)),
        [],
        4000000,
    )


def attention_backward(kv, order, block_rows, qr, kr, vr, cos, sin, doc, log, grad, grad_at):
    two = 2 * HEAD_SIZE
    seq = SEQUENCE_TOKENS
    return attention_call(
        attention_backward_kernel,
        kv,
        order,
        block_rows,
        qr.shape[0],
        (
            (qr, two, None),
            (kr, two, None),
            (vr, two, None),
            (cos, two, None),
            (sin, two, None),
            (doc, 1, None),
            (log, two, None),
            (grad, two, grad_at),
        ),
        ((jnp.bfloat16, two, 0), (jnp.bfloat16, 2 * two, 0)),
        [pltpu.VMEM((seq, two), jnp.float32), pltpu.VMEM((seq, two), jnp.float32)],
        9000000,
    )


def weight_grad_kernel(count, with_back, *refs):
    lefts, rights = (refs[:count], refs[count : 2 * count])
    rest = refs[2 * count :]
    out_ref = rest[-3] if with_back else rest[-1]
    spot = 0
    for left, right in zip(lefts, rights):
        grad = mxu(left[...], right[...], TN)
        columns = right.shape[1]
        out_ref[:, spot : spot + columns] = grad.astype(jnp.bfloat16)
        spot += columns
    if with_back:
        w_ref = rest[0]
        part = mxu(rights[-1][...], w_ref[...], NT)
        if len(rest) > 4:
            part = part + rest[1][...].astype(jnp.float32)
        rest[-2][...] = part.astype(rest[-2].dtype)
        rest[-1][...] = jnp.sum(grad * w_ref[...].astype(jnp.float32), axis=1, keepdims=True)


def weight_grads(pairs, back=None, base=None, kind=jnp.bfloat16):
    tokens, rows = pairs[0][0].shape
    total = sum(right.shape[1] for _, right in pairs)
    block = min(rows, 512)
    ins = [left for left, _ in pairs] + [right for _, right in pairs]
    specs = [pl.BlockSpec((tokens, block), lambda i: (0, i)) for _ in pairs]
    specs += [pl.BlockSpec((tokens, right.shape[1]), lambda i: (0, 0)) for _, right in pairs]
    outs = [jax.ShapeDtypeStruct((rows, total), jnp.bfloat16)]
    out_specs = [pl.BlockSpec((block, total), lambda i: (i, 0))]
    flops = 2 * tokens * rows * total
    if back is not None:
        weight, place = back
        ins.append(weight)
        specs.append(pl.BlockSpec((block, pairs[-1][1].shape[1]), lambda i: (i, place)))
        if base is not None:
            ins.append(base)
            specs.append(pl.BlockSpec((tokens, block), lambda i: (0, i)))
        outs += [
            jax.ShapeDtypeStruct((tokens, rows), kind),
            jax.ShapeDtypeStruct((rows, 1), jnp.float32),
        ]
        out_specs += [
            pl.BlockSpec((tokens, block), lambda i: (0, i)),
            pl.BlockSpec((block, 1), lambda i: (i, 0)),
        ]
        flops += 2 * tokens * rows * pairs[-1][1].shape[1]
    result = pl.pallas_call(
        functools.partial(weight_grad_kernel, len(pairs), back is not None),
        grid=(rows // block,),
        in_specs=specs,
        out_specs=out_specs,
        out_shape=outs,
        compiler_params=pltpu.CompilerParams(vmem_limit_bytes=VMEM_LIMIT),
        cost_estimate=pl.CostEstimate(
            flops=flops, bytes_accessed=4 * tokens * rows + 2 * rows * total, transcendentals=0
        ),
    )(*ins)
    return result if back is not None else result[0]


def feed_forward_kernel(hidden_width, x_ref, cot_ref, w_ref, grad_ref, hidden_ref, back_ref, out_ref):
    wide = 2 * hidden_width
    acts = mxu(x_ref[...], w_ref[:, :wide], NN)
    hidden_grad = mxu(cot_ref[...], w_ref[:, wide:], NN)
    gate, up = (acts[:, :hidden_width], acts[:, hidden_width:])
    sig = jax.nn.sigmoid(gate)
    silu = gate * sig
    grads = jnp.concatenate(
        [hidden_grad * up * (sig * (1.0 + gate * (1.0 - sig))), hidden_grad * silu], axis=1
    ).astype(jnp.bfloat16)
    grad_ref[...] = grads
    back_ref[...] = mxu(grads, w_ref[:, :wide], NT).astype(jnp.bfloat16)
    hidden = (silu * up).astype(jnp.bfloat16)
    hidden_ref[...] = hidden
    out_ref[...] = mxu(hidden, w_ref[:, wide:], NT).astype(jnp.bfloat16)


def feed_forward(x, cot, weights, rows):
    tokens, width = x.shape
    hidden_width = weights.shape[1] // 3
    by_rows = lambda columns: pl.BlockSpec((rows, columns), lambda i: (i, 0))
    sizes = (2 * hidden_width, hidden_width, width, width)
    return pl.pallas_call(
        functools.partial(feed_forward_kernel, hidden_width),
        grid=(tokens // rows,),
        in_specs=[by_rows(width), by_rows(width), pl.BlockSpec(weights.shape, lambda i: (0, 0))],
        out_specs=[by_rows(columns) for columns in sizes],
        out_shape=[jax.ShapeDtypeStruct((tokens, columns), jnp.bfloat16) for columns in sizes],
        compiler_params=pltpu.CompilerParams(vmem_limit_bytes=VMEM_LIMIT),
        cost_estimate=pl.CostEstimate(
            flops=12 * tokens * width * hidden_width,
            bytes_accessed=14 * tokens * width,
            transcendentals=0,
        ),
    )(x, cot, weights)


def finish_kernel(valid_ref, x_ref, mixer_ref, middle_ref, ffn_ref, out_ref, stat_ref):
    valid = valid_ref[...]
    middle, ffn = (middle_ref[...], ffn_ref[...])
    result = middle + ffn
    out_ref[...] = result.astype(jnp.bfloat16)
    tracked = (x_ref[...].astype(jnp.float32), mixer_ref[...], middle, ffn, result)
    stat_ref[...] = jnp.zeros_like(stat_ref)
    for k, values in enumerate(tracked):
        stat_ref[k : k + 1, 0:1] = jnp.sum(
            valid * jnp.sum(values * values, axis=1, keepdims=True), axis=0, keepdims=True
        )
    stat_ref[len(tracked) : len(tracked) + 1, 0:1] = jnp.sum(valid, axis=0, keepdims=True)


def finish(valid, x, mixer_sum, middle, ffn_out):
    return pl.pallas_call(
        finish_kernel,
        out_shape=[
            jax.ShapeDtypeStruct(x.shape, jnp.bfloat16),
            jax.ShapeDtypeStruct((8, 128), jnp.float32),
        ],
        compiler_params=pltpu.CompilerParams(vmem_limit_bytes=VMEM_LIMIT),
        cost_estimate=pl.CostEstimate(flops=16 * x.size, bytes_accessed=16 * x.size, transcendentals=0),
    )(valid, x, mixer_sum, middle, ffn_out)


def passengers(stages, *values):
    for _ in range(stages):
        yield []
    return (yield list(values))


def rope_rows(position):
    lane = jnp.arange(2 * HEAD_SIZE, dtype=jnp.int32)
    half = HEAD_SIZE // 2
    inverse = jnp.exp(
        (lane % half).astype(jnp.float32) * (-2.0 * math.log(ROPE_BASE) / HEAD_SIZE)
    )
    angles = position.astype(jnp.float32)[:, None] * inverse[None, :]
    sign = jnp.where(lane % HEAD_SIZE < half, -1.0, 1.0)
    return (jnp.cos(angles), jnp.sin(angles) * sign[None, :])
def grid_of(count):
    rows = 1
    while 8 * rows * rows <= count:
        rows *= 2
    return (count // rows, rows)


def ring_cycle(count):
    depth, rows = grid_of(count)
    order = []
    for level in range(depth):
        inner = list(range(1, rows))
        if level % 2:
            inner.reverse()
        order += [level * rows + row for row in inner]
    return order + [level * rows for level in reversed(range(depth))]


class Ring:
    def __init__(self, count):
        self.count = count
        self.order = ring_cycle(count)
        self.depth, self.rows = grid_of(count)
        inner = self.rows - 1
        mine = lax.axis_index("dp")
        level, row = (mine // self.rows, mine % self.rows)
        step = jnp.where(level % 2 == 0, row - 1, inner - row)
        self.spot = jnp.where(
            row > 0, level * inner + step, self.depth * inner + self.depth - 1 - level
        )

    def device_at(self, offset):
        inner = self.rows - 1
        spot = (self.spot + offset + self.count) % self.count
        level, step = (spot // inner, spot % inner)
        row = jnp.where(level % 2 == 0, step + 1, inner - step)
        back = self.count - 1 - spot
        return jnp.where(spot < self.depth * inner, level * self.rows + row, back * self.rows)

    def send(self, block, step):
        count, order = (self.count, self.order)
        return lax.ppermute(
            block, "dp", [(order[k], order[(k + step) % count]) for k in range(count)]
        )


def together(*values):
    return lax.optimization_barrier(values)


def lockstep(*chains):
    results = [None] * len(chains)
    waiting = {k: None for k in range(len(chains))}
    while waiting:
        sent = {}
        for k in list(waiting):
            try:
                sent[k] = chains[k].send(waiting[k])
            except StopIteration as stop:
                results[k] = stop.value
                del waiting[k]
        flat = [value for k in sent for value in sent[k]]
        if len(flat) > 1:
            flat = list(together(*flat))
        for k in sent:
            waiting[k] = flat[: len(sent[k])]
            flat = flat[len(sent[k]) :]
    return results


def after_stages(count, chain):
    for _ in range(count):
        yield []
    return (yield from chain)


def ring_gather(ring, block):
    count = ring.count
    rows = block.shape[0]
    half = rows // 2
    out = jnp.zeros((count * rows,) + block.shape[1:], block.dtype)

    def put(out, piece, offset, extra=0):
        return lax.dynamic_update_slice_in_dim(
            out, piece, ring.device_at(offset) * rows + extra, 0
        )

    out = put(out, block, 0)
    ahead = behind = block
    for step in range(1, count // 2):
        ahead, behind = yield [ring.send(ahead, 1), ring.send(behind, -1)]
        out = put(out, ahead, -step)
        out = put(out, behind, step)
    ahead, behind = yield [ring.send(ahead[:half], 1), ring.send(behind[half:], -1)]
    return put(put(out, ahead, -(count // 2)), behind, count // 2, half)


def ring_scatter(ring, *parts):
    count = ring.count
    rows = parts[0].shape[0] // count
    half = rows // 2

    def piece(offset, start=0, size=rows):
        first = ring.device_at(offset) * rows + start
        return jnp.concatenate(
            [lax.dynamic_slice_in_dim(part, first, size, 0).astype(jnp.float32) for part in parts],
            axis=1,
        )

    far = count // 2
    ahead = piece(far, 0, half).astype(jnp.bfloat16)
    behind = piece(far, half, rows - half).astype(jnp.bfloat16)
    for offset in range(far - 1, -1, -1):
        ahead, behind = yield [ring.send(ahead, 1), ring.send(behind, -1)]
        ahead, behind = (ahead.astype(jnp.float32), behind.astype(jnp.float32))
        if offset == far - 1:
            ahead, behind = (
                jnp.concatenate([ahead, jnp.zeros_like(behind)], axis=0),
                jnp.concatenate([jnp.zeros_like(ahead), behind], axis=0),
            )
        if offset:
            ahead = (ahead + piece(offset)).astype(jnp.bfloat16)
            behind = (behind + piece(-offset)).astype(jnp.bfloat16)
    return ahead + behind + piece(0)


def core_swap(block):
    count = lax.axis_size("tensor")
    return lax.ppermute(block, "tensor", [(k, k ^ 1) for k in range(count)])


def chip_shift(block, step):
    count = lax.axis_size("tensor")
    return lax.ppermute(block, "tensor", [(k, (k + 2 * step) % count) for k in range(count)])


def tensor_parts(block):
    chips = lax.axis_size("tensor") // 2
    mate, *others = yield [core_swap(block)] + [chip_shift(block, k) for k in range(1, chips)]
    mates = yield [core_swap(other) for other in others]
    parts = [block, mate]
    for other, beside in zip(others, mates):
        parts += [other, beside]
    return parts


def in_order(parts):
    chips = len(parts) // 2
    mine = lax.axis_index("tensor")
    flipped = mine % 2 == 1
    pairs = []
    for chip in range(chips):
        first, second = (parts[2 * chip], parts[2 * chip + 1])
        pairs.append((jnp.where(flipped, second, first), jnp.where(flipped, first, second)))
    out = []
    for chip in range(chips):
        back = (mine // 2 + chips - chip) % chips
        for core in range(2):
            value = pairs[0][core]
            for step in range(1, chips):
                value = jnp.where(back == step, pairs[step][core], value)
            out.append(value)
    return out


def seq_gather(values):
    parts = yield from tensor_parts(values)
    return jnp.concatenate(parts, axis=0)


def tensor_scatter(pick):
    chips = lax.axis_size("tensor") // 2
    places = [2 * (chips - step) for step in range(1, chips)]
    mate, *others = yield [core_swap(pick(place + 1)) for place in [0] + places]
    merged = [
        (pick(place).astype(jnp.float32) + other.astype(jnp.float32)).astype(jnp.bfloat16)
        for place, other in zip(places, others)
    ]
    received = yield [chip_shift(value, k + 1) for k, value in enumerate(merged)]
    total = pick(0).astype(jnp.float32) + mate.astype(jnp.float32)
    for other in received:
        total = total + other.astype(jnp.float32)
    return total


def seq_reduce(lowered):
    rows = lowered.shape[0] // lax.axis_size("tensor")
    return tensor_scatter(lambda place: lowered[place * rows : (place + 1) * rows])


def width_total(values):
    chips = lax.axis_size("tensor") // 2
    blocks = values.reshape(chips, 2, -1)
    blocks = blocks + core_swap(blocks)[:, ::-1]
    total = blocks
    for step in range(1, chips):
        total = total + jnp.roll(chip_shift(blocks, step), step, axis=0)
    return total.reshape(values.shape)


def exchange(blocks, axes):
    return lax.all_to_all(blocks, axes, 0, 0, tiled=False)


def dp_scatter(values):
    blocks = values.astype(jnp.bfloat16).reshape((lax.axis_size("dp"), -1) + values.shape[1:])
    return jnp.sum(exchange(blocks, "dp").astype(jnp.float32), axis=0)


def run(chain):
    return lockstep(chain)[0]


def local(
    layer_input,
    out_grad,
    segment_ids,
    valid_mask,
    doc_start,
    norm_gains,
    conv_weight,
    conv_bias,
    mixer_gain,
    shared_proj,
    step_bias,
    decay_log,
    skip_gain,
    mamba_gate,
    mamba_input,
    mamba_step,
    query_proj,
    mamba_out,
    attention_out,
    swiglu_gate,
    swiglu_up,
    swiglu_down,
):
    tensor_position = lax.axis_index("tensor")
    dp_count = lax.axis_size("dp")
    tensor_count = lax.axis_size("tensor")
    device = lax.axis_index("dp") * tensor_count + tensor_position
    ring = Ring(dp_count)
    local_width = mamba_gate.shape[1]
    query_width = query_proj.shape[1]
    head_local = mamba_step.shape[1]
    hidden_width = swiglu_gate.shape[1]
    query_slice = query_width // HEAD_SIZE
    slab = 2 * HEAD_SIZE
    wide = -(-local_width // slab) * slab
    early_width = wide + slab
    block_rows = layer_input.shape[0]
    tokens_per_group = block_rows * tensor_count
    seq_count = tokens_per_group // SEQUENCE_TOKENS
    channel_start = tensor_position * local_width
    head_start = tensor_position * head_local
    channels = conv_weight.shape[1] * dp_count * tensor_count

    def padded(values, columns):
        return jnp.pad(values, ((0, 0), (0, columns - values.shape[1])))

    def placed(rows_in, columns, start):
        whole = jnp.zeros((rows_in.shape[0], columns), rows_in.dtype)
        return lax.dynamic_update_slice_in_dim(whole, rows_in, start, 1)

    device_count = dp_count * tensor_count
    small = jnp.concatenate(
        [norm_gains.reshape(-1), conv_weight.reshape(-1), conv_bias, mixer_gain]
    )
    small_width = -(-small.shape[0] // 128) * 128
    small = jnp.pad(small, (0, small_width - small.shape[0]))
    small_all = exchange(
        jnp.broadcast_to(small[None], (device_count, small_width)), ("dp", "tensor")
    )
    shared_own = lax.all_gather(shared_proj, "tensor", axis=0, tiled=True)
    valid_f = valid_mask.astype(jnp.float32)
    out_cot = out_grad.astype(jnp.float32) * valid_f[:, None]
    layer_input, shared_own = together(layer_input, shared_own)
    x_full, w_in, ffn_grad_in, waited = lockstep(
        seq_gather(layer_input),
        ring_gather(
            ring,
            jnp.concatenate(
                [
                    padded(mamba_gate, wide),
                    padded(query_proj, slab),
                    mamba_out.T,
                    attention_out.T,
                    padded(mamba_input, wide),
                    padded(mamba_step, slab),
                    shared_own,
                ],
                axis=1,
            ),
        ),
        after_stages(2, seq_gather(out_cot.astype(jnp.bfloat16))),
        passengers(1, doc_start, swiglu_gate, swiglu_up, swiglu_down),
    )
    doc_start, swiglu_gate, swiglu_up, swiglu_down = waited
    ffn_block, w_in = together(
        jnp.concatenate([swiglu_gate, swiglu_up, swiglu_down.T], axis=1), w_in
    )
    shared_at = w_in.shape[1] - shared_proj.shape[1]
    late_at = early_width + local_width + query_width
    w_early, w_out, w_late, shared_w = (
        w_in[:, :early_width],
        w_in[:, early_width:late_at],
        w_in[:, late_at:shared_at],
        w_in[:, shared_at:],
    )
    w_ffn = lax.all_gather(ffn_block, "dp", axis=0, tiled=True)
    cuts = []
    spot = 0
    for piece in (norm_gains, conv_weight, conv_bias[None], mixer_gain[None]):
        taken = small_all[:, spot : spot + piece.size].astype(jnp.float32)
        cuts.append(jnp.swapaxes(taken.reshape((-1,) + piece.shape), 0, 1).reshape(piece.shape[0], -1))
        spot += piece.size
    gains_f = cuts[0]
    conv_f = jnp.concatenate(cuts[1:3], axis=0)
    mixer_gain_f = cuts[3][0]
    tokens_f = layer_input.astype(jnp.float32)
    scale_one = rms_scale(tokens_f)
    x_wide = x_full.astype(jnp.float32)
    first_full = (x_wide * rms_scale(x_wide) * gains_f[0]).astype(jnp.bfloat16)
    taps = jnp.concatenate(
        [lax.dynamic_slice_in_dim(conv_f, channel_start, local_width, 1), conv_f[:, DSSM:]], axis=1
    )
    taps = jnp.pad(taps, ((0, 3), (0, 0)))
    own_gain = lax.dynamic_slice_in_dim(mixer_gain_f, channel_start, local_width, 0)
    own_bias = lax.dynamic_slice_in_dim(step_bias, head_start, head_local, 0)
    own_decay = lax.dynamic_slice_in_dim(decay_log, head_start, head_local, 0)
    own_skip = lax.dynamic_slice_in_dim(skip_gain, head_start, head_local, 0)
    params = jnp.pad(
        jnp.stack([own_bias, -jnp.exp(own_decay)], axis=0), ((0, 6), (0, slab - head_local))
    )
    skip_row = jnp.broadcast_to(jnp.repeat(own_skip, HEAD_SIZE)[None], (8, local_width))
    doc = doc_start[:, None]
    position = jnp.tile(jnp.arange(SEQUENCE_TOKENS, dtype=jnp.int32), seq_count) - doc_start
    cosine_table, sine_table = rope_rows(position)
    kv = (tensor_position * query_slice // (QUERY_HEADS // KEY_VALUE_HEADS)).astype(jnp.int32)[None]
    device_ids = jnp.arange(tensor_count, dtype=jnp.int32)
    chip_count = tensor_count // 2
    block_order = (tensor_position // 2 + chip_count - device_ids // 2) % chip_count * 2 + (
        tensor_position + device_ids
    ) % 2

    late_act = product(first_full, w_late)
    common_act = product(first_full, shared_w)
    early_act = product(first_full, w_early)
    mamba_y, square_rows, kept_states = mamba_forward(
        block_order, block_rows, early_act, late_act, common_act, doc, taps, params, skip_row
    )
    attended, query_rot, key_rot, value_low, log_total = attention_forward(
        kv, block_order, block_rows, early_act, common_act, cosine_table, sine_table, doc
    )
    square_sum = width_total(square_rows[0])
    gate_scale = lax.rsqrt(square_sum / DSSM + EPS)[:, None]
    gate_z = early_act[:, :local_width]
    sigmoid_z = jax.nn.sigmoid(gate_z)
    silu_z = gate_z * sigmoid_z
    gated_y = mamba_y * silu_z
    normed_b = (gated_y * gate_scale * own_gain).astype(jnp.bfloat16)
    mixed_b = jnp.concatenate([normed_b, attended[:, :query_width]], axis=1)
    mixer_sum = run(seq_reduce(product_nt(mixed_b, w_out).astype(jnp.bfloat16)))

    middle = tokens_f + mixer_sum
    scale_two = rms_scale(middle)
    second_b = (middle * scale_two * gains_f[1]).astype(jnp.bfloat16)
    ffn_in = run(seq_gather(second_b))
    gate_up_grad, hidden_b, second_part, ffn_part = feed_forward(
        ffn_in, ffn_grad_in, w_ffn, block_rows
    )
    ffn_in, ffn_grad_in, second_part = together(ffn_in, ffn_grad_in, second_part)
    second_grad = run(seq_reduce(second_part))
    ffn_w_grad = weight_grads(((ffn_in, gate_up_grad), (ffn_grad_in, hidden_b)))
    second_value_grad, gain_two_grad = norm_back(middle, scale_two, gains_f[1], second_grad)
    middle_grad = out_cot + second_value_grad
    middle_grad, ffn_w_grad = together(middle_grad, ffn_w_grad)
    ffn_w_grad = lax.psum_scatter(ffn_w_grad, "dp", scatter_dimension=0, tiled=True).astype(
        jnp.float32
    )
    gate_w_grad = ffn_w_grad[:, :hidden_width]
    up_w_grad = ffn_w_grad[:, hidden_width : 2 * hidden_width]
    down_w_grad = ffn_w_grad[:, 2 * hidden_width :].T

    mixer_grad_full = run(seq_gather(middle_grad.astype(jnp.bfloat16)))
    ffn_part, mixer_grad_full = together(ffn_part, mixer_grad_full)
    mixed_grad = product(mixer_grad_full, w_out)
    normed_grad = mixed_grad[:, :local_width]
    scaled_normed = normed_grad * own_gain
    inner_sum = width_total(jnp.sum(scaled_normed * gated_y, axis=1))
    attended_grad, attended_at = (mixed_grad, local_width // slab)
    if local_width % slab or query_width != slab:
        attended_grad, attended_at = (padded(mixed_grad[:, local_width:], slab), 0)
    out_total = dp_scatter(weight_grads(((mixer_grad_full, mixed_b),)))
    dq, dkv = attention_backward(
        kv,
        block_order,
        block_rows,
        query_rot,
        key_rot,
        value_low,
        cosine_table,
        sine_table,
        doc,
        log_total,
        attended_grad,
        attended_at,
    )
    own_gain_grad = jnp.sum(normed_grad * gated_y * gate_scale, axis=0)
    gated_grad = (
        gate_scale * scaled_normed
        - gated_y * (gate_scale * gate_scale * gate_scale) * (inner_sum / DSSM)[:, None]
    )
    mamba_y_grad = gated_grad * silu_z
    gate_z_grad = (gated_grad * mamba_y * sigmoid_z * (1.0 + gate_z * (1.0 - sigmoid_z))).astype(
        jnp.bfloat16
    )
    early_grad = jnp.concatenate([padded(gate_z_grad, wide), dq], axis=1)
    early_w_grad, first_early, gain_one_early = weight_grads(
        ((first_full, early_grad),), (w_in, 0), kind=jnp.float32
    )
    early_w_grad, out_total = together(early_w_grad, out_total)
    early_total = dp_scatter(early_w_grad)
    ffn_out = run(seq_reduce(ffn_part))
    result_b, stat_terms = finish(valid_f[:, None], layer_input, mixer_sum, middle, ffn_out)
    mamba_y_grad, first_early = together(mamba_y_grad, first_early)
    late_grad, taps_grad, params_grad = mamba_backward(
        block_order,
        block_rows,
        late_act,
        common_act,
        doc,
        taps,
        params,
        skip_row,
        mamba_y,
        mamba_y_grad,
        dkv,
        kept_states,
    )

    back = (w_in, late_at // late_grad.shape[1])
    if late_at % late_grad.shape[1]:
        back = (w_in[:, late_at:], 0)
    late_w_grad, first_part, gain_one_late = weight_grads(
        ((first_full, late_grad),), back, first_early
    )
    gain_one_grad = (gain_one_early + gain_one_late)[:, 0] / gains_f[0]
    def by_device(rows_in):
        return jnp.swapaxes(rows_in.reshape(rows_in.shape[0], device_count, -1), 0, 1).reshape(
            device_count, -1
        )

    heads = jnp.concatenate(
        [placed(params_grad[:3, :head_local], MH, head_start).reshape(-1), stat_terms[:6, 0]]
    )
    sums = jnp.concatenate(
        [
            by_device(jnp.stack([gain_one_grad, gain_two_grad], axis=0)),
            by_device(
                jnp.concatenate(
                    [
                        placed(taps_grad[: CONV + 1, :local_width], DSSM, channel_start),
                        taps_grad[: CONV + 1, local_width:],
                    ],
                    axis=1,
                )
            ),
            by_device(placed(own_gain_grad[None], DSSM, channel_start)),
            jnp.broadcast_to(heads[None], (device_count, heads.shape[0])),
        ],
        axis=1,
    )
    sums = padded(sums, -(-sums.shape[1] // 128) * 128)
    sums, early_total = together(sums, early_total)

    def exchanged(blocks):
        (got,) = yield [exchange(blocks, ("dp", "tensor"))]
        return jnp.sum(got, axis=0)

    late_total, first_grad, sums = lockstep(
        ring_scatter(ring, late_w_grad),
        seq_reduce(first_part),
        after_stages(1, exchanged(sums)),
    )
    shared_total = late_total[:, early_width:].astype(jnp.bfloat16)
    shared_rows = shared_proj.shape[0]
    places = [
        ((tensor_position // 2 + chip_count - place // 2) % chip_count) * 2
        + (tensor_position + place) % 2
        for place in range(tensor_count)
    ]
    shared_proj_grad = run(
        tensor_scatter(
            lambda place: lax.dynamic_slice_in_dim(
                shared_total, places[place] * shared_rows, shared_rows, 0
            )
        )
    )
    mamba_out_grad = out_total[:, :local_width].T
    attend_out_grad = out_total[:, local_width:].T
    gate_proj_grad = early_total[:, :local_width]
    query_proj_grad = early_total[:, wide : wide + query_width]
    input_proj_grad = late_total[:, :local_width]
    step_proj_grad = late_total[:, wide : wide + head_local]
    first_value_grad, _ = norm_back(tokens_f, scale_one, gains_f[0], first_grad)
    input_grad = middle_grad + first_value_grad

    gain_cols, conv_cols, mix_cols = (
        norm_gains.shape[1],
        conv_weight.shape[1],
        mixer_gain.shape[0],
    )
    gains_grad = sums[: 2 * gain_cols].reshape(2, gain_cols)
    spot = 2 * gain_cols
    conv_grads = sums[spot : spot + (CONV + 1) * conv_cols].reshape(CONV + 1, conv_cols)
    spot += (CONV + 1) * conv_cols
    gain_full_grad = sums[spot : spot + mix_cols]
    spot += mix_cols
    heads_total = sums[spot : spot + 3 * MH].reshape(3, MH)
    spot += 3 * MH
    residual_rms = jnp.sqrt(sums[spot : spot + 5] / (sums[spot + 5] * D))
    return (
        result_b,
        input_grad,
        gains_grad,
        conv_grads[:CONV],
        conv_grads[CONV],
        gain_full_grad,
        shared_proj_grad,
        heads_total[0],
        heads_total[1],
        heads_total[2],
        gate_proj_grad,
        input_proj_grad,
        step_proj_grad,
        query_proj_grad,
        mamba_out_grad,
        attend_out_grad,
        gate_w_grad,
        up_w_grad,
        down_w_grad,
        residual_rms,
    )


def solution(mesh):
    in_specs = (
        P(("dp", "tensor"), None),
        P(("dp", "tensor"), None),
        P("dp"),
        P(("dp", "tensor")),
        P("dp"),
        P(None, ("dp", "tensor")),
        P(None, ("dp", "tensor")),
        P(("dp", "tensor")),
        P(("dp", "tensor")),
        P(("dp", "tensor"), None),
        P(),
        P(),
        P(),
        P("dp", "tensor"),
        P("dp", "tensor"),
        P("dp", "tensor"),
        P("dp", "tensor"),
        P("tensor", "dp"),
        P("tensor", "dp"),
        P("dp", "tensor"),
        P("dp", "tensor"),
        P("tensor", "dp"),
    )
    out_specs = (
        P(("dp", "tensor"), None),
        P(("dp", "tensor"), None),
        P(None, ("dp", "tensor")),
        P(None, ("dp", "tensor")),
        P(("dp", "tensor")),
        P(("dp", "tensor")),
        P(("dp", "tensor"), None),
        P(),
        P(),
        P(),
        P("dp", "tensor"),
        P("dp", "tensor"),
        P("dp", "tensor"),
        P("dp", "tensor"),
        P("tensor", "dp"),
        P("tensor", "dp"),
        P("dp", "tensor"),
        P("dp", "tensor"),
        P("tensor", "dp"),
        P(),
    )
    return jax.shard_map(local, mesh=mesh, in_specs=in_specs, out_specs=out_specs, check_vma=False)
```

```python
import functools
import math

import jax
import jax.numpy as jnp
from jax import lax
from jax.experimental import pallas as pl
from jax.experimental.pallas import tpu as pltpu
from jax.sharding import PartitionSpec as P

D = 1024
MH = 24
HEAD_SIZE = 64
MAMBA_STATES = 128
CONV = 4
QUERY_HEADS = 8
KEY_VALUE_HEADS = 2
SEQUENCE_TOKENS = 1024
DSSM = 1536


EPS = 1e-05
ROPE_BASE = 100000000000.0
NEG_FILL = -1e30
HIGH = lax.Precision.HIGHEST


def rms_scale(values):
    return lax.rsqrt(jnp.mean(values * values, axis=-1, keepdims=True) + EPS)


def norm_back(values, row_scale, gain_row, grad_in):
    scaled_grad = grad_in * gain_row
    gain_grad = jnp.sum(grad_in * values * row_scale, axis=0)
    value_grad = row_scale * scaled_grad - values * (row_scale * row_scale * row_scale) * jnp.mean(
        scaled_grad * values, axis=-1, keepdims=True
    )
    return (value_grad, gain_grad)


def product(left, right):
    return jnp.dot(left, right, preferred_element_type=jnp.float32)


def product_tn(left, right):
    return lax.dot_general(
        left, right, (((0,), (0,)), ((), ())), preferred_element_type=jnp.float32
    )


def product_nt(left, right):
    return lax.dot_general(
        left, right, (((1,), (1,)), ((), ())), preferred_element_type=jnp.float32
    )


def split_dot(values, selector, dims):
    high = values.astype(jnp.bfloat16)
    low = (values - high.astype(jnp.float32)).astype(jnp.bfloat16)
    left = lax.dot_general(high, selector, dims, preferred_element_type=jnp.float32)
    return left + lax.dot_general(low, selector, dims, preferred_element_type=jnp.float32)


def estimate(flops, size):
    return pl.CostEstimate(flops=int(flops * 0.05), bytes_accessed=int(size * 0.05), transcendentals=0)


NN = (((1,), (0,)), ((), ()))
NT = (((1,), (1,)), ((), ()))
TN = (((0,), (0,)), ((), ()))


def mxu(left, right, dims):
    return lax.dot_general(
        left.astype(jnp.bfloat16),
        right.astype(jnp.bfloat16),
        dims,
        preferred_element_type=jnp.float32,
    )


def iota(shape, dim):
    return lax.broadcasted_iota(jnp.int32, shape, dim)


def head_groups(width):
    return [(low, min(low + 2 * HEAD_SIZE, width)) for low in range(0, width, 2 * HEAD_SIZE)]


def chunk_common(chunk, start, rows, width, raw_ref, doc_ref, pad_ref, w_ref, par_ref):
    doc = doc_ref[pl.ds(start, chunk), :]
    age = start + iota((chunk, 1), 0) - doc
    span = pad_ref[pl.ds(start, chunk + 8), :]
    conv = w_ref[CONV : CONV + 1, :] + w_ref[CONV - 1 : CONV, :] * span[8:, :]
    lagged = [span[8:, :]]
    for lag in range(1, CONV):
        moved = jnp.where(age >= lag, span[8 - lag : 8 - lag + chunk, :], 0.0)
        lagged.append(moved)
        conv = conv + w_ref[CONV - 1 - lag : CONV - lag, :] * moved
    sig = jax.nn.sigmoid(conv)
    act = conv * sig
    raw = raw_ref[rows, :] + par_ref[0:1, :]
    step = jnp.maximum(raw, 0.0) + jnp.log1p(jnp.exp(-jnp.abs(raw)))
    rate = step * par_ref[1:2, :]
    lower = (iota((chunk, chunk), 0) >= iota((chunk, chunk), 1)).astype(jnp.bfloat16)
    high = rate.astype(jnp.bfloat16)
    low = (rate - high.astype(jnp.float32)).astype(jnp.bfloat16)
    total = mxu(lower, high, NN) + mxu(lower, low, NN)
    lanes = par_ref.shape[1]
    spread = (iota((lanes, width), 0) == iota((lanes, width), 1) // HEAD_SIZE).astype(jnp.bfloat16)
    key_pos = start + iota((chunk, chunk), 1)
    allowed = (key_pos <= start + iota((chunk, chunk), 0)) & (key_pos >= doc)
    doc_last = doc[chunk - 1 : chunk, :]
    ends = total[chunk - 1 : chunk, :]
    live = jnp.where(doc < start, jnp.exp(total), 0.0)
    keep = jnp.where(start + iota((chunk, 1), 0) >= doc_last, jnp.exp(ends - total), 0.0)
    carry = jnp.where(doc_last < start, jnp.exp(ends), 0.0)
    wide = split_dot(jnp.concatenate([step, live, keep, jnp.broadcast_to(carry, (8, lanes))], axis=0), spread, NN)
    return dict(
        conv=conv, sig=sig, act=act, raw=raw, step=step, total=total, turned=total.T, spread=spread, allowed=allowed,
        carry=carry, age=age, lagged=lagged, lower=lower,
        step_w=wide[:chunk], live_w=wide[chunk : 2 * chunk], keep_w=wide[2 * chunk : 3 * chunk],
        carry_w=wide[3 * chunk : 3 * chunk + 1],
    )


def decay_of(part, head):
    gap = part["total"][:, head : head + 1] - part["turned"][head : head + 1, :]
    return jnp.where(part["allowed"], jnp.exp(gap), 0.0)


def only(values, low, high):
    lane = iota(values.shape, 1)
    return jnp.where((lane >= low) & (lane < high), values, jnp.zeros_like(values))


def place_of(order_ref, block_rows, length, start):
    token = pl.program_id(0) * length + start
    return pl.multiple_of(
        order_ref[token // block_rows] * block_rows + token % block_rows, 128
    )


def fill_conv_input(order_ref, block_rows, width, x_ref, bc_ref, pad_ref):
    length = pad_ref.shape[0] - 8
    pad_ref[0:8, :] = jnp.zeros((8, pad_ref.shape[1]), jnp.float32)
    for start in range(0, length, block_rows):
        rows = pl.ds(place_of(order_ref, block_rows, length, start), block_rows)
        pad_ref[8 + start : 8 + start + block_rows, :width] = x_ref[rows, :width]
        pad_ref[8 + start : 8 + start + block_rows, width:] = bc_ref[rows, :]


def mamba_forward_kernel(
    chunk, width, block_rows, order_ref, x_ref, bc_ref, raw_ref, z_ref, doc_ref, w_ref, par_ref, skip_ref, y_ref, square_ref, kept_ref, pad_ref, state_ref
):
    length = pad_ref.shape[0] - 8
    fill_conv_input(order_ref, block_rows, width, x_ref, bc_ref, pad_ref)
    state_ref[...] = jnp.zeros_like(state_ref)

    def one_chunk(index, _):
        start = pl.multiple_of(index * chunk, chunk)
        rows = pl.ds(place_of(order_ref, block_rows, length, start), chunk)
        part = chunk_common(chunk, start, rows, width, raw_ref, doc_ref, pad_ref, w_ref, par_ref)
        inner = part["act"][:, :width]
        bm = part["act"][:, width : width + MAMBA_STATES].astype(jnp.bfloat16)
        cm = part["act"][:, width + MAMBA_STATES :].astype(jnp.bfloat16)
        driven = (inner * part["step_w"]).astype(jnp.bfloat16)
        pair = mxu(cm, bm, NT)
        pieces = []
        for low, high in head_groups(width):
            heads = range(low // HEAD_SIZE, high // HEAD_SIZE)
            mats = [(decay_of(part, head) * pair).astype(jnp.bfloat16) for head in heads]
            piece = driven[:, low:high]
            right = [
                only(piece, HEAD_SIZE * k, HEAD_SIZE * (k + 1)) if len(mats) > 1 else piece
                for k in range(len(mats))
            ]
            pieces.append(
                mxu(jnp.concatenate(mats, axis=1), jnp.concatenate(right, axis=0), NN)
            )
        state = state_ref[...]
        kept_ref[pl.ds(pl.multiple_of(index * MAMBA_STATES, MAMBA_STATES), MAMBA_STATES), :] = state
        y = jnp.concatenate(pieces, axis=1) + part["live_w"] * mxu(cm, state, NN)
        y = y + skip_ref[0:1, :] * inner
        state_ref[...] = state * part["carry_w"] + mxu(
            bm, driven.astype(jnp.float32) * part["keep_w"], TN
        )
        y_ref[rows, :] = y
        z = z_ref[rows, :width]
        gated = y * z * jax.nn.sigmoid(z)
        square_ref[:, rows] = split_dot_left(gated * gated)
        return 0

    lax.fori_loop(0, length // chunk, one_chunk, 0)


def split_dot_left(values):
    ones = jnp.ones((8, values.shape[1]), jnp.bfloat16)
    high = values.astype(jnp.bfloat16)
    low = (values - high.astype(jnp.float32)).astype(jnp.bfloat16)
    return mxu(ones, high, NT) + mxu(ones, low, NT)


def mamba_backward_kernel(
    chunk, width, block_rows, order_ref, x_ref, bc_ref, raw_ref, doc_ref, w_ref, par_ref, skip_ref, y_ref, dy_ref,
    dkv_ref, kept_ref, din_ref, dw_ref, dpar_ref, pad_ref, state_ref, halo_ref, dskip_ref
):
    length = pad_ref.shape[0] - 8
    count = length // chunk
    wide = x_ref.shape[1]
    common_at = wide + 2 * HEAD_SIZE

    @pl.when(pl.program_id(0) == 0)
    def _():
        if wide > width:
            din_ref[...] = jnp.zeros_like(din_ref)
        din_ref[:, common_at + 2 * MAMBA_STATES :] = dkv_ref[...]

    fill_conv_input(order_ref, block_rows, width, x_ref, bc_ref, pad_ref)
    state_ref[...] = jnp.zeros_like(state_ref)
    halo_ref[...] = jnp.zeros_like(halo_ref)

    @pl.when(pl.program_id(0) == 0)
    def _():
        dw_ref[...] = jnp.zeros_like(dw_ref)
        dpar_ref[...] = jnp.zeros_like(dpar_ref)
        dskip_ref[...] = jnp.zeros_like(dskip_ref)

    def one_chunk(step_index, _):
        index = count - 1 - step_index
        start = pl.multiple_of(index * chunk, chunk)
        rows = pl.ds(place_of(order_ref, block_rows, length, start), chunk)
        part = chunk_common(chunk, start, rows, width, raw_ref, doc_ref, pad_ref, w_ref, par_ref)
        inner = part["act"][:, :width]
        bm = part["act"][:, width : width + MAMBA_STATES].astype(jnp.bfloat16)
        cm = part["act"][:, width + MAMBA_STATES :].astype(jnp.bfloat16)
        driven = (inner * part["step_w"]).astype(jnp.bfloat16)
        driven_f = driven.astype(jnp.float32)
        y = y_ref[rows, :]
        dy = dy_ref[rows, :]
        dy_b = dy.astype(jnp.bfloat16)
        pair = mxu(cm, bm, NT)
        pair_grad = jnp.zeros((chunk, chunk), jnp.float32)
        pieces = []
        for low, high in head_groups(width):
            heads = list(range(low // HEAD_SIZE, high // HEAD_SIZE))
            piece = driven[:, low:high]
            grads = [
                only(dy_b[:, low:high], HEAD_SIZE * k, HEAD_SIZE * (k + 1)) if len(heads) > 1 else dy_b[:, low:high]
                for k in range(len(heads))
            ]
            mats = []
            for k, head in enumerate(heads):
                decay = decay_of(part, head)
                mats.append((decay * pair).astype(jnp.bfloat16))
                pair_grad = pair_grad + decay * mxu(grads[k], piece, NT)
            pieces.append(mxu(jnp.concatenate(mats, axis=0), jnp.concatenate(grads, axis=0), TN))
        within = jnp.concatenate(pieces, axis=1)
        state = kept_ref[pl.ds(pl.multiple_of(index * MAMBA_STATES, MAMBA_STATES), MAMBA_STATES), :]
        state_grad = state_ref[...]
        pair_grad = pair_grad.astype(jnp.bfloat16)
        dy_live = (dy * part["live_w"]).astype(jnp.bfloat16)
        driven_keep = (driven_f * part["keep_w"]).astype(jnp.bfloat16)
        later = part["keep_w"] * mxu(bm, state_grad, NN)
        c_grad = mxu(pair_grad, bm, NN) + mxu(dy_live, state, NT)
        b_grad = mxu(pair_grad, cm, TN) + mxu(driven_keep, state_grad, NT)
        state_ref[...] = state_grad * part["carry_w"] + mxu(cm, dy_live, TN)
        driven_grad = within + later
        later_part = driven_f * later
        mixed = y - skip_ref[0:1, :] * inner
        sums = split_dot(
            jnp.concatenate(
                [
                    dy_b.astype(jnp.float32) * mixed - driven_f * within - later_part,
                    driven_grad * inner,
                    jnp.broadcast_to(
                        jnp.sum(later_part, axis=0, keepdims=True)
                        + part["carry_w"] * jnp.sum(state_grad * state, axis=0, keepdims=True),
                        (8, width),
                    ),
                ],
                axis=0,
            ),
            part["spread"],
            NT,
        )
        high = sums[:chunk].astype(jnp.bfloat16)
        low = (sums[:chunk] - high.astype(jnp.float32)).astype(jnp.bfloat16)
        rate_grad = (
            mxu(part["lower"], high, TN) + mxu(part["lower"], low, TN) + sums[2 * chunk : 2 * chunk + 1]
        )
        step_grad = rate_grad * par_ref[1:2, :] + sums[chunk : 2 * chunk]
        raw_grad = step_grad * jax.nn.sigmoid(part["raw"])
        din_ref[rows, wide:common_at] = raw_grad.astype(jnp.bfloat16)
        dpar_ref[0:1, :] += jnp.sum(raw_grad, axis=0, keepdims=True)
        dpar_ref[1:2, :] += par_ref[1:2, :] * jnp.sum(rate_grad * part["step"], axis=0, keepdims=True)
        dskip_ref[0:1, :] += jnp.sum(dy * inner, axis=0, keepdims=True)
        inner_grad = driven_grad * part["step_w"] + skip_ref[0:1, :] * dy
        sig, conv = (part["sig"], part["conv"])
        conv_grad = jnp.concatenate([inner_grad, b_grad, c_grad], axis=1) * (
            sig * (1.0 + conv * (1.0 - sig))
        )
        dw_ref[CONV : CONV + 1, :] += jnp.sum(conv_grad, axis=0, keepdims=True)
        v_grad = w_ref[CONV - 1 : CONV, :] * conv_grad
        long = jnp.concatenate([conv_grad, halo_ref[...]], axis=0)
        next_start = jnp.minimum(start + chunk, length - 8)
        ages = jnp.concatenate([part["age"], start + chunk + iota((8, 1), 0) - doc_ref[pl.ds(pl.multiple_of(next_start, 8), 8), :]], axis=0)
        dw_ref[CONV - 1 : CONV, :] += jnp.sum(conv_grad * part["lagged"][0], axis=0, keepdims=True)
        for lag in range(1, CONV):
            dw_ref[CONV - 1 - lag : CONV - lag, :] += jnp.sum(
                conv_grad * part["lagged"][lag], axis=0, keepdims=True
            )
            masked = jnp.where(ages >= lag, long, 0.0)
            v_grad = v_grad + w_ref[CONV - 1 - lag : CONV - lag, :] * masked[lag : lag + chunk, :]
        halo_ref[...] = conv_grad[:8, :]
        din_ref[rows, :width] = v_grad[:, :width].astype(jnp.bfloat16)
        din_ref[rows, common_at : common_at + 2 * MAMBA_STATES] = v_grad[:, width:].astype(jnp.bfloat16)
        return 0

    lax.fori_loop(0, count, one_chunk, 0)

    @pl.when(pl.program_id(0) == pl.num_programs(0) - 1)
    def _():
        lanes = dpar_ref.shape[1]
        spread = (iota((lanes, width), 0) == iota((lanes, width), 1) // HEAD_SIZE).astype(jnp.bfloat16)
        dpar_ref[2:3, :] = split_dot(dskip_ref[...], spread, NT)[0:1]


CHUNK = 256
VMEM_LIMIT = 60 * 1024 * 1024


def tokens_spec(tokens, width, place=0):
    return pl.BlockSpec((tokens, width), lambda i, *_: (0, place))


def whole_spec(shape):
    return pl.BlockSpec(shape, lambda i, *_: (0,) * len(shape))


def mamba_forward(order, block_rows, early, late, common, doc, taps, params, skip_row, chunk=CHUNK):
    tokens = late.shape[0]
    width = skip_row.shape[1]
    lanes = params.shape[1]
    wide = late.shape[1] - lanes
    seq = SEQUENCE_TOKENS
    count = tokens // seq
    kept = seq // chunk * MAMBA_STATES
    return pl.pallas_call(
        functools.partial(mamba_forward_kernel, chunk, width, block_rows),
        grid_spec=pltpu.PrefetchScalarGridSpec(
        num_scalar_prefetch=1,
        grid=(count,),
        in_specs=[
            tokens_spec(tokens, wide),
            tokens_spec(tokens, 2 * MAMBA_STATES),
            tokens_spec(tokens, lanes, wide // lanes),
            tokens_spec(tokens, wide),
            pl.BlockSpec((seq, 1), lambda i, *_: (i, 0)),
            whole_spec(taps.shape),
            whole_spec(params.shape),
            whole_spec(skip_row.shape),
        ],
        out_specs=[
            tokens_spec(tokens, width),
            whole_spec((8, tokens)),
            pl.BlockSpec((kept, width), lambda i, *_: (i, 0)),
        ],
        scratch_shapes=[
            pltpu.VMEM((seq + 8, width + 2 * MAMBA_STATES), jnp.float32),
            pltpu.VMEM((MAMBA_STATES, width), jnp.float32),
        ],
        ),
        out_shape=[
            jax.ShapeDtypeStruct((tokens, width), jnp.float32),
            jax.ShapeDtypeStruct((8, tokens), jnp.float32),
            jax.ShapeDtypeStruct((count * kept, width), jnp.float32),
        ],
        compiler_params=pltpu.CompilerParams(vmem_limit_bytes=VMEM_LIMIT),
        cost_estimate=estimate(tokens * width * 20000, tokens * width * 20),
    )(order, late, common, late, early, doc, taps, params, skip_row)


def mamba_backward(
    order, block_rows, late, common, doc, taps, params, skip_row, y, dy, dkv, kept_states, chunk=CHUNK
):
    tokens = late.shape[0]
    width = skip_row.shape[1]
    lanes = params.shape[1]
    wide = late.shape[1] - lanes
    seq = SEQUENCE_TOKENS
    count = tokens // seq
    kept = seq // chunk * MAMBA_STATES
    conv_width = width + 2 * MAMBA_STATES
    return pl.pallas_call(
        functools.partial(mamba_backward_kernel, chunk, width, block_rows),
        grid_spec=pltpu.PrefetchScalarGridSpec(
        num_scalar_prefetch=1,
        grid=(count,),
        in_specs=[
            tokens_spec(tokens, wide),
            tokens_spec(tokens, 2 * MAMBA_STATES),
            tokens_spec(tokens, lanes, wide // lanes),
            pl.BlockSpec((seq, 1), lambda i, *_: (i, 0)),
            whole_spec(taps.shape),
            whole_spec(params.shape),
            whole_spec(skip_row.shape),
            tokens_spec(tokens, width),
            tokens_spec(tokens, width),
            tokens_spec(tokens, dkv.shape[1]),
            pl.BlockSpec((kept, width), lambda i, *_: (i, 0)),
        ],
        out_specs=[
            tokens_spec(tokens, late.shape[1] + common.shape[1]),
            whole_spec((8, conv_width)),
            whole_spec((8, lanes)),
        ],
        scratch_shapes=[
            pltpu.VMEM((seq + 8, conv_width), jnp.float32),
            pltpu.VMEM((MAMBA_STATES, width), jnp.float32),
            pltpu.VMEM((8, conv_width), jnp.float32),
            pltpu.VMEM((8, width), jnp.float32),
        ],
        ),
        out_shape=[
            jax.ShapeDtypeStruct((tokens, late.shape[1] + common.shape[1]), jnp.bfloat16),
            jax.ShapeDtypeStruct((8, conv_width), jnp.float32),
            jax.ShapeDtypeStruct((8, lanes), jnp.float32),
        ],
        compiler_params=pltpu.CompilerParams(vmem_limit_bytes=VMEM_LIMIT),
        cost_estimate=estimate(tokens * width * 60000, tokens * width * 20),
    )(
        order, late, common, late, doc, taps, params, skip_row, y, dy, dkv, kept_states
    )


NEGATIVE = -1e30
QUERY_BLOCK = 256


def swap_halves(values):
    half = HEAD_SIZE // 2
    lane = iota(values.shape, 1)
    width = values.shape[1]
    return jnp.where(
        lane % HEAD_SIZE < half,
        pltpu.roll(values, width - half, 1),
        pltpu.roll(values, half, 1),
    )


def attention_mask(start, rows, keys, doc):
    position = start + iota((rows, 1), 0)
    key_pos = iota((rows, keys), 1)
    return (key_pos <= position) & (key_pos >= doc)


def both_heads(values):
    return jnp.concatenate(
        [only(values, 0, HEAD_SIZE), only(values, HEAD_SIZE, 2 * HEAD_SIZE)], axis=0
    )


def chosen(values, kv):
    lane = iota(values.shape, 1)
    turned = pltpu.roll(values, HEAD_SIZE, 1)
    return jnp.where((lane < HEAD_SIZE) == (kv == 0), values, turned)


def attention_forward_kernel(
    block_rows, kv_ref, order_ref, q_ref, key_ref, value_ref, cos_ref, sin_ref, doc_ref, out_ref, qr_ref, kr_ref, vr_ref, log_ref
):
    length = qr_ref.shape[0]
    kv = kv_ref[0]
    rows = block_rows
    for start in range(0, length, rows):
        block = slice(start, start + rows)
        place = pl.ds(place_of(order_ref, block_rows, length, start), rows)
        cos, sin = (cos_ref[block, :], sin_ref[block, :])
        query, key = (q_ref[place, :], key_ref[place, :])
        turned = (query * cos + swap_halves(query) * sin).astype(jnp.bfloat16)
        qr_ref[block, :] = (turned.astype(jnp.float32) * HEAD_SIZE**-0.5).astype(jnp.bfloat16)
        kr_ref[block, :] = chosen(key * cos + swap_halves(key) * sin, kv).astype(jnp.bfloat16)
        vr_ref[block, :] = chosen(value_ref[place, :], kv).astype(jnp.bfloat16)
        keys = start + rows
        mask = attention_mask(start, rows, keys, doc_ref[block, :])
        scores = mxu(both_heads(qr_ref[block, :]), kr_ref[0:keys, :], NT)
        outs = []
        logs = []
        for head in range(2):
            part = jnp.where(mask, scores[head * rows : (head + 1) * rows], NEGATIVE)
            peak = jnp.max(part, axis=1, keepdims=True)
            weight = jnp.exp(part - peak)
            total = jnp.sum(weight, axis=1, keepdims=True)
            outs.append(mxu(weight * (1.0 / total), vr_ref[0:keys, :], NN))
            logs.append(peak + jnp.log(total))
        lane = iota((rows, 2 * HEAD_SIZE), 1)
        out_ref[place, :] = jnp.where(lane < HEAD_SIZE, outs[0], outs[1]).astype(jnp.bfloat16)
        log_ref[block, :] = jnp.where(lane < HEAD_SIZE, logs[0], logs[1])


def attention_backward_kernel(
    block_rows, kv_ref, order_ref, qr_ref, kr_ref, vr_ref, cos_ref, sin_ref, doc_ref, log_ref, grad_ref, dq_ref, dkv_ref, dk_ref, dv_ref
):
    length = qr_ref.shape[0]
    kv = kv_ref[0]
    rows = block_rows
    lane = iota((rows, 2 * HEAD_SIZE), 1)
    mine = (lane < HEAD_SIZE) == (kv == 0)
    dk_ref[...] = jnp.zeros_like(dk_ref)
    dv_ref[...] = jnp.zeros_like(dv_ref)
    for start in reversed(range(0, length, rows)):
        keys = start + rows
        block = slice(start, start + rows)
        place = pl.ds(place_of(order_ref, block_rows, length, start), rows)
        mask = attention_mask(start, rows, keys, doc_ref[block, :])
        query = both_heads(qr_ref[block, :])
        grad = both_heads(grad_ref[place, :].astype(jnp.bfloat16))
        logs = log_ref[block, :]
        scores = mxu(query, kr_ref[0:keys, :], NT)
        prob_grad = mxu(grad, vr_ref[0:keys, :], NT)
        probs = []
        score_grads = []
        for head in range(2):
            part = slice(head * rows, (head + 1) * rows)
            log = logs[:, head * HEAD_SIZE : head * HEAD_SIZE + 1]
            weight = jnp.where(mask, jnp.exp(scores[part] - log), 0.0)
            product_grad = weight * prob_grad[part]
            total = jnp.sum(product_grad, axis=1, keepdims=True)
            probs.append(weight.astype(jnp.bfloat16))
            score_grads.append((product_grad - weight * total).astype(jnp.bfloat16))
        cos, sin = (cos_ref[block, :], sin_ref[block, :])
        dq = mxu(jnp.concatenate(score_grads, axis=0), kr_ref[0:keys, :], NN)
        dq = jnp.where(lane < HEAD_SIZE, dq[:rows], dq[rows:]) * HEAD_SIZE**-0.5
        dq = dq * cos - swap_halves(dq) * sin
        dq_ref[place, :] = dq.astype(jnp.bfloat16)
        dk_ref[0:keys, :] += mxu(jnp.concatenate(score_grads, axis=0), query, TN)
        dv_ref[0:keys, :] += mxu(jnp.concatenate(probs, axis=0), grad, TN)
        dk = dk_ref[block, :]
        dk = dk + pltpu.roll(dk, HEAD_SIZE, 1)
        dk = dk * cos - swap_halves(dk) * sin
        dv = dv_ref[block, :]
        dv = dv + pltpu.roll(dv, HEAD_SIZE, 1)
        dkv_ref[place, : 2 * HEAD_SIZE] = jnp.where(mine, dk, 0.0).astype(jnp.bfloat16)
        dkv_ref[place, 2 * HEAD_SIZE :] = jnp.where(mine, dv, 0.0).astype(jnp.bfloat16)


def attention_call(kernel, kv, order, block_rows, tokens, ins, outs, scratch, flops):
    seq = SEQUENCE_TOKENS

    def spec(columns, place):
        if place is None:
            return pl.BlockSpec((seq, columns), lambda i, *_: (i, 0))
        return tokens_spec(tokens, columns, place)

    return pl.pallas_call(
        functools.partial(kernel, block_rows),
        grid_spec=pltpu.PrefetchScalarGridSpec(
            num_scalar_prefetch=2,
            grid=(tokens // seq,),
            in_specs=[spec(columns, place) for _, columns, place in ins],
            out_specs=[spec(columns, place) for _, columns, place in outs],
            scratch_shapes=scratch,
        ),
        out_shape=[jax.ShapeDtypeStruct((tokens, columns), kind) for kind, columns, _ in outs],
        compiler_params=pltpu.CompilerParams(vmem_limit_bytes=VMEM_LIMIT),
        cost_estimate=estimate(flops * tokens, tokens * 4096),
    )(kv, order, *[value for value, _, _ in ins])


def attention_forward(kv, order, block_rows, early, common, cos, sin, doc):
    two = 2 * HEAD_SIZE
    low, full = (jnp.bfloat16, jnp.float32)
    query_at = early.shape[1] // two - 1
    key_at = 2 * MAMBA_STATES // two
    return attention_call(
        attention_forward_kernel,
        kv,
        order,
        block_rows,
        early.shape[0],
        (
            (early, two, query_at),
            (common, two, key_at),
            (common, two, key_at + 1),
            (cos, two, None),
            (sin, two, None),
            (doc, 1, None),
        ),
        ((low, two, 0), (low, two, None), (low, two, None), (low, two, None), (full, two, None)),
        [],
        4000000,
    )


def attention_backward(kv, order, block_rows, qr, kr, vr, cos, sin, doc, log, grad, grad_at):
    two = 2 * HEAD_SIZE
    seq = SEQUENCE_TOKENS
    return attention_call(
        attention_backward_kernel,
        kv,
        order,
        block_rows,
        qr.shape[0],
        (
            (qr, two, None),
            (kr, two, None),
            (vr, two, None),
            (cos, two, None),
            (sin, two, None),
            (doc, 1, None),
            (log, two, None),
            (grad, two, grad_at),
        ),
        ((jnp.bfloat16, two, 0), (jnp.bfloat16, 2 * two, 0)),
        [pltpu.VMEM((seq, two), jnp.float32), pltpu.VMEM((seq, two), jnp.float32)],
        9000000,
    )


def pack_kernel(widths, turned, *refs):
    spot = 0
    out_ref = refs[-1]
    for ref, width, turn in zip(refs, widths, turned):
        value = ref[...].T if turn else ref[...]
        have = value.shape[1]
        out_ref[:, spot : spot + have] = value
        if width > have:
            out_ref[:, spot + have : spot + width] = jnp.zeros(
                (value.shape[0], width - have), value.dtype
            )
        spot += width


def pack(rows, pieces):
    widths = [width for _, width, _ in pieces]
    turned = [turn for _, _, turn in pieces]
    arrays = [value for value, _, _ in pieces]
    size = rows * sum(widths)
    return pl.pallas_call(
        functools.partial(pack_kernel, widths, turned),
        out_shape=jax.ShapeDtypeStruct((rows, sum(widths)), arrays[0].dtype),
        compiler_params=pltpu.CompilerParams(vmem_limit_bytes=VMEM_LIMIT),
        cost_estimate=estimate(size, 4 * size),
    )(*arrays)


def unpack_kernel(groups, size, pieces, small_ref, *out_refs):
    spot = 0
    for out_ref, (rows, width) in zip(out_refs, pieces):
        total = out_ref.shape[1]
        column = iota((width, total), 1)
        owner = iota((small_ref.shape[0], total), 1) // (width * groups)
        mine = owner == iota((small_ref.shape[0], total), 0)
        for row in range(rows):
            found = jnp.zeros((small_ref.shape[0], total), jnp.float32)
            for group in range(groups):
                pick = (column % width == iota((width, total), 0)) & (
                    column // width % groups == group
                )
                start = group * size + spot
                found = found + mxu(
                    small_ref[:, start : start + width], pick.astype(jnp.bfloat16), NN
                )
            out_ref[row : row + 1, :] = jnp.sum(
                jnp.where(mine, found, 0.0), axis=0, keepdims=True
            )
            spot += width
        if rows < out_ref.shape[0]:
            out_ref[rows:, :] = jnp.zeros((out_ref.shape[0] - rows, total), jnp.float32)


def unpack(small, groups, size, pieces):
    count = small.shape[0] * groups
    return pl.pallas_call(
        functools.partial(unpack_kernel, groups, size, pieces),
        out_shape=[
            jax.ShapeDtypeStruct((8, count * width), jnp.float32) for _, width in pieces
        ],
        compiler_params=pltpu.CompilerParams(vmem_limit_bytes=VMEM_LIMIT),
        cost_estimate=estimate(1 << 26, 1 << 18),
    )(small)


def project_kernel(count, x_ref, gain_ref, *refs):
    x = x_ref[...].astype(jnp.float32)
    scale = lax.rsqrt(jnp.mean(x * x, axis=1, keepdims=True) + EPS)
    first = (x * scale * gain_ref[0:1, :]).astype(jnp.bfloat16)
    refs[count][...] = first
    for w_ref, out_ref in zip(refs[:count], refs[count + 1 :]):
        out_ref[...] = mxu(first, w_ref[...], NN)


def project(x, gains, weights, rows):
    tokens, width = x.shape
    arrays, specs = ([], [])
    for array, columns, start in weights:
        if start % columns:
            array, start = (array[:, start : start + columns], 0)
        arrays.append(array)
        specs.append(
            pl.BlockSpec(
                (width, columns), functools.partial(lambda place, i: (0, place), start // columns)
            )
        )
    by_rows = lambda columns: pl.BlockSpec((rows, columns), lambda i: (i, 0))
    total = sum(columns for _, columns, _ in weights)
    return pl.pallas_call(
        functools.partial(project_kernel, len(weights)),
        grid=(tokens // rows,),
        in_specs=[by_rows(width), pl.BlockSpec(gains.shape, lambda i: (0, 0))] + specs,
        out_specs=[by_rows(width)] + [by_rows(columns) for _, columns, _ in weights],
        out_shape=[jax.ShapeDtypeStruct((tokens, width), jnp.bfloat16)]
        + [jax.ShapeDtypeStruct((tokens, columns), jnp.float32) for _, columns, _ in weights],
        compiler_params=pltpu.CompilerParams(vmem_limit_bytes=VMEM_LIMIT),
        cost_estimate=estimate(2 * tokens * width * total, 2 * width * total + 4 * tokens * (width + total)),
    )(x, gains, *arrays)


def gather_kernel(pieces, extra, *refs):
    out_ref = refs[-1]
    count = out_ref.shape[0]
    out_ref[...] = jnp.zeros_like(out_ref)
    spot = 0
    for ref, (rows, width) in zip(refs, pieces):
        total = ref.shape[1]
        pick = (iota((total, width), 0) % width == iota((total, width), 1)).astype(jnp.bfloat16)
        mine = iota((count, total), 1) // width == iota((count, total), 0)
        for row in range(rows):
            rest = jnp.where(mine, ref[row : row + 1, :], 0.0)
            found = jnp.zeros((count, width), jnp.float32)
            for _ in range(3):
                low = rest.astype(jnp.bfloat16)
                found = found + mxu(low, pick, NN)
                rest = rest - low.astype(jnp.float32)
            out_ref[:, spot : spot + width] = found
            spot += width
    for row in range(refs[-2].shape[0]):
        width = extra[row]
        out_ref[:, spot : spot + width] = jnp.broadcast_to(
            refs[-2][row : row + 1, :width], (count, width)
        )
        spot += width


def gather_sums(count, arrays, pieces, everywhere, extra):
    columns = sum(rows * width for rows, width in pieces) + sum(extra)
    columns = -(-columns // 128) * 128
    return pl.pallas_call(
        functools.partial(gather_kernel, pieces, extra),
        out_shape=jax.ShapeDtypeStruct((count, columns), jnp.float32),
        compiler_params=pltpu.CompilerParams(vmem_limit_bytes=VMEM_LIMIT),
        cost_estimate=estimate(1 << 26, 1 << 18),
    )(*arrays, everywhere)


def spread_kernel(shapes, got_ref, *out_refs):
    sums = jnp.sum(got_ref[...], axis=0, keepdims=True)
    spot = 0
    for out_ref, (rows, width) in zip(out_refs, shapes):
        for row in range(rows):
            out_ref[row : row + 1, :] = sums[:, spot : spot + width]
            spot += width


def spread_sums(got, shapes):
    return pl.pallas_call(
        functools.partial(spread_kernel, shapes),
        out_shape=[jax.ShapeDtypeStruct(shape, jnp.float32) for shape in shapes],
        compiler_params=pltpu.CompilerParams(vmem_limit_bytes=VMEM_LIMIT),
        cost_estimate=estimate(1 << 16, 1 << 17),
    )(got)


def weight_grad_kernel(count, with_back, *refs):
    lefts, rights = (refs[:count], refs[count : 2 * count])
    rest = refs[2 * count :]
    out_ref = rest[-3] if with_back else rest[-1]
    spot = 0
    for left, right in zip(lefts, rights):
        grad = mxu(left[...], right[...], TN)
        columns = right.shape[1]
        out_ref[:, spot : spot + columns] = grad.astype(jnp.bfloat16)
        spot += columns
    if with_back:
        w_ref = rest[0]
        part = mxu(rights[-1][...], w_ref[...], NT)
        if len(rest) > 4:
            part = part + rest[1][...].astype(jnp.float32)
        rest[-2][...] = part.astype(rest[-2].dtype)
        rest[-1][...] = jnp.sum(grad * w_ref[...].astype(jnp.float32), axis=1, keepdims=True)


def weight_grads(pairs, back=None, base=None, kind=jnp.bfloat16):
    tokens, rows = pairs[0][0].shape
    total = sum(right.shape[1] for _, right in pairs)
    block = min(rows, 512)
    ins = [left for left, _ in pairs] + [right for _, right in pairs]
    specs = [pl.BlockSpec((tokens, block), lambda i: (0, i)) for _ in pairs]
    specs += [pl.BlockSpec((tokens, right.shape[1]), lambda i: (0, 0)) for _, right in pairs]
    outs = [jax.ShapeDtypeStruct((rows, total), jnp.bfloat16)]
    out_specs = [pl.BlockSpec((block, total), lambda i: (i, 0))]
    flops = 2 * tokens * rows * total
    if back is not None:
        weight, place = back
        ins.append(weight)
        specs.append(pl.BlockSpec((block, pairs[-1][1].shape[1]), lambda i: (i, place)))
        if base is not None:
            ins.append(base)
            specs.append(pl.BlockSpec((tokens, block), lambda i: (0, i)))
        outs += [
            jax.ShapeDtypeStruct((tokens, rows), kind),
            jax.ShapeDtypeStruct((rows, 1), jnp.float32),
        ]
        out_specs += [
            pl.BlockSpec((tokens, block), lambda i: (0, i)),
            pl.BlockSpec((block, 1), lambda i: (i, 0)),
        ]
        flops += 2 * tokens * rows * pairs[-1][1].shape[1]
    result = pl.pallas_call(
        functools.partial(weight_grad_kernel, len(pairs), back is not None),
        grid=(rows // block,),
        in_specs=specs,
        out_specs=out_specs,
        out_shape=outs,
        compiler_params=pltpu.CompilerParams(vmem_limit_bytes=VMEM_LIMIT),
        cost_estimate=estimate(flops, 4 * tokens * rows + 2 * rows * total),
    )(*ins)
    return result if back is not None else result[0]


def feed_forward_kernel(hidden_width, x_ref, cot_ref, w_ref, grad_ref, hidden_ref, back_ref, out_ref):
    wide = 2 * hidden_width
    acts = mxu(x_ref[...], w_ref[:, :wide], NN)
    hidden_grad = mxu(cot_ref[...], w_ref[:, wide:], NN)
    gate, up = (acts[:, :hidden_width], acts[:, hidden_width:])
    sig = jax.nn.sigmoid(gate)
    silu = gate * sig
    grads = jnp.concatenate(
        [hidden_grad * up * (sig * (1.0 + gate * (1.0 - sig))), hidden_grad * silu], axis=1
    ).astype(jnp.bfloat16)
    grad_ref[...] = grads
    back_ref[...] = mxu(grads, w_ref[:, :wide], NT).astype(jnp.bfloat16)
    hidden = (silu * up).astype(jnp.bfloat16)
    hidden_ref[...] = hidden
    out_ref[...] = mxu(hidden, w_ref[:, wide:], NT).astype(jnp.bfloat16)


def feed_forward(x, cot, weights, rows):
    tokens, width = x.shape
    hidden_width = weights.shape[1] // 3
    by_rows = lambda columns: pl.BlockSpec((rows, columns), lambda i: (i, 0))
    sizes = (2 * hidden_width, hidden_width, width, width)
    return pl.pallas_call(
        functools.partial(feed_forward_kernel, hidden_width),
        grid=(tokens // rows,),
        in_specs=[by_rows(width), by_rows(width), pl.BlockSpec(weights.shape, lambda i: (0, 0))],
        out_specs=[by_rows(columns) for columns in sizes],
        out_shape=[jax.ShapeDtypeStruct((tokens, columns), jnp.bfloat16) for columns in sizes],
        compiler_params=pltpu.CompilerParams(vmem_limit_bytes=VMEM_LIMIT),
        cost_estimate=estimate(12 * tokens * width * hidden_width, 14 * tokens * width),
    )(x, cot, weights)


def finish_kernel(valid_ref, x_ref, mixer_ref, middle_ref, ffn_ref, out_ref, stat_ref):
    valid = valid_ref[...]
    middle, ffn = (middle_ref[...], ffn_ref[...])
    result = middle + ffn
    out_ref[...] = result.astype(jnp.bfloat16)
    tracked = (x_ref[...].astype(jnp.float32), mixer_ref[...], middle, ffn, result)
    stat_ref[...] = jnp.zeros_like(stat_ref)
    for k, values in enumerate(tracked):
        stat_ref[k : k + 1, 0:1] = jnp.sum(
            valid * jnp.sum(values * values, axis=1, keepdims=True), axis=0, keepdims=True
        )
    stat_ref[len(tracked) : len(tracked) + 1, 0:1] = jnp.sum(valid, axis=0, keepdims=True)


def finish(valid, x, mixer_sum, middle, ffn_out):
    return pl.pallas_call(
        finish_kernel,
        out_shape=[
            jax.ShapeDtypeStruct(x.shape, jnp.bfloat16),
            jax.ShapeDtypeStruct((8, 128), jnp.float32),
        ],
        compiler_params=pltpu.CompilerParams(vmem_limit_bytes=VMEM_LIMIT),
        cost_estimate=estimate(16 * x.size, 16 * x.size),
    )(valid, x, mixer_sum, middle, ffn_out)


def resumed(chain, sent):
    while True:
        got = yield sent
        try:
            sent = chain.send(got)
        except StopIteration as stop:
            return stop.value


def passengers(stages, *values):
    for _ in range(stages):
        yield []
    return (yield list(values))


def rope_rows(position):
    lane = jnp.arange(2 * HEAD_SIZE, dtype=jnp.int32)
    half = HEAD_SIZE // 2
    inverse = jnp.exp(
        (lane % half).astype(jnp.float32) * (-2.0 * math.log(ROPE_BASE) / HEAD_SIZE)
    )
    angles = position.astype(jnp.float32)[:, None] * inverse[None, :]
    sign = jnp.where(lane % HEAD_SIZE < half, -1.0, 1.0)
    return (jnp.cos(angles), jnp.sin(angles) * sign[None, :])
def grid_of(count):
    rows = 1
    while 8 * rows * rows <= count:
        rows *= 2
    return (count // rows, rows)


def ring_cycle(count):
    depth, rows = grid_of(count)
    order = []
    for level in range(depth):
        inner = list(range(1, rows))
        if level % 2:
            inner.reverse()
        order += [level * rows + row for row in inner]
    return order + [level * rows for level in reversed(range(depth))]


class Ring:
    def __init__(self, count):
        self.count = count
        self.order = ring_cycle(count)
        self.depth, self.rows = grid_of(count)
        inner = self.rows - 1
        mine = lax.axis_index("dp")
        level, row = (mine // self.rows, mine % self.rows)
        step = jnp.where(level % 2 == 0, row - 1, inner - row)
        self.spot = jnp.where(
            row > 0, level * inner + step, self.depth * inner + self.depth - 1 - level
        )

    def device_at(self, offset):
        inner = self.rows - 1
        spot = (self.spot + offset + self.count) % self.count
        level, step = (spot // inner, spot % inner)
        row = jnp.where(level % 2 == 0, step + 1, inner - step)
        back = self.count - 1 - spot
        return jnp.where(spot < self.depth * inner, level * self.rows + row, back * self.rows)

    def send(self, block, step):
        count, order = (self.count, self.order)
        return lax.ppermute(
            block, "dp", [(order[k], order[(k + step) % count]) for k in range(count)]
        )


def together(*values):
    return lax.optimization_barrier(values)


def lockstep(*chains):
    results = [None] * len(chains)
    waiting = {k: None for k in range(len(chains))}
    while waiting:
        sent = {}
        for k in list(waiting):
            try:
                sent[k] = chains[k].send(waiting[k])
            except StopIteration as stop:
                results[k] = stop.value
                del waiting[k]
        flat = [value for k in sent for value in sent[k]]
        if len(flat) > 1:
            flat = list(together(*flat))
        for k in sent:
            waiting[k] = flat[: len(sent[k])]
            flat = flat[len(sent[k]) :]
    return results


def after_stages(count, chain):
    for _ in range(count):
        yield []
    return (yield from chain)


def ring_gather(ring, block, extra):
    count = ring.count
    rows = block.shape[0]
    half = rows // 2
    whole = jnp.concatenate([block, extra], axis=0)
    out = jnp.zeros((count * rows,) + block.shape[1:], block.dtype)
    more = jnp.zeros((count,) + extra.shape, block.dtype)

    def put(arrays, piece, offset, start=0):
        out, more = arrays
        device = ring.device_at(offset)
        kept = min(piece.shape[0], rows - start)
        out = lax.dynamic_update_slice_in_dim(out, piece[:kept], device * rows + start, 0)
        if piece.shape[0] > kept:
            more = lax.dynamic_update_index_in_dim(more, piece[kept:], device, 0)
        return (out, more)

    arrays = put((out, more), whole, 0)
    ahead = behind = whole
    for step in range(1, count // 2):
        ahead, behind = yield [ring.send(ahead, 1), ring.send(behind, -1)]
        arrays = put(arrays, ahead, -step)
        arrays = put(arrays, behind, step)
    ahead, behind = yield [ring.send(ahead[:half], 1), ring.send(behind[half:], -1)]
    arrays = put(arrays, ahead, -(count // 2))
    return put(arrays, behind, count // 2, half)


def ring_scatter(ring, *parts):
    count = ring.count
    rows = parts[0].shape[0] // count
    half = rows // 2

    def piece(offset, start=0, size=rows):
        first = ring.device_at(offset) * rows + start
        return jnp.concatenate(
            [lax.dynamic_slice_in_dim(part, first, size, 0).astype(jnp.float32) for part in parts],
            axis=1,
        )

    far = count // 2
    ahead = piece(far, 0, half).astype(jnp.bfloat16)
    behind = piece(far, half, rows - half).astype(jnp.bfloat16)
    for offset in range(far - 1, -1, -1):
        ahead, behind = yield [ring.send(ahead, 1), ring.send(behind, -1)]
        ahead, behind = (ahead.astype(jnp.float32), behind.astype(jnp.float32))
        if offset == far - 1:
            ahead, behind = (
                jnp.concatenate([ahead, jnp.zeros_like(behind)], axis=0),
                jnp.concatenate([jnp.zeros_like(ahead), behind], axis=0),
            )
        if offset:
            ahead = (ahead + piece(offset)).astype(jnp.bfloat16)
            behind = (behind + piece(-offset)).astype(jnp.bfloat16)
    return ahead + behind + piece(0)


def core_swap(block):
    count = lax.axis_size("tensor")
    return lax.ppermute(block, "tensor", [(k, k ^ 1) for k in range(count)])


def chip_shift(block, step):
    count = lax.axis_size("tensor")
    return lax.ppermute(block, "tensor", [(k, (k + 2 * step) % count) for k in range(count)])


def tensor_parts(block):
    chips = lax.axis_size("tensor") // 2
    mate, *others = yield [core_swap(block)] + [chip_shift(block, k) for k in range(1, chips)]
    mates = yield [core_swap(other) for other in others]
    parts = [block, mate]
    for other, beside in zip(others, mates):
        parts += [other, beside]
    return parts


def in_order(parts):
    chips = len(parts) // 2
    mine = lax.axis_index("tensor")
    flipped = mine % 2 == 1
    pairs = []
    for chip in range(chips):
        first, second = (parts[2 * chip], parts[2 * chip + 1])
        pairs.append((jnp.where(flipped, second, first), jnp.where(flipped, first, second)))
    out = []
    for chip in range(chips):
        back = (mine // 2 + chips - chip) % chips
        for core in range(2):
            value = pairs[0][core]
            for step in range(1, chips):
                value = jnp.where(back == step, pairs[step][core], value)
            out.append(value)
    return out


def seq_gather(values):
    parts = yield from tensor_parts(values)
    return jnp.concatenate(parts, axis=0)


def tensor_scatter(pick):
    chips = lax.axis_size("tensor") // 2
    places = [2 * (chips - step) for step in range(1, chips)]
    mate, *others = yield [core_swap(pick(place + 1)) for place in [0] + places]
    merged = [
        (pick(place).astype(jnp.float32) + other.astype(jnp.float32)).astype(jnp.bfloat16)
        for place, other in zip(places, others)
    ]
    received = yield [chip_shift(value, k + 1) for k, value in enumerate(merged)]
    total = pick(0).astype(jnp.float32) + mate.astype(jnp.float32)
    for other in received:
        total = total + other.astype(jnp.float32)
    return total


def seq_reduce(lowered):
    rows = lowered.shape[0] // lax.axis_size("tensor")
    return tensor_scatter(lambda place: lowered[place * rows : (place + 1) * rows])


def width_total(values):
    chips = lax.axis_size("tensor") // 2
    blocks = values.reshape(chips, 2, -1)
    blocks = blocks + core_swap(blocks)[:, ::-1]
    total = blocks
    for step in range(1, chips):
        total = total + jnp.roll(chip_shift(blocks, step), step, axis=0)
    return total.reshape(values.shape)


def exchange(blocks, axes):
    return lax.all_to_all(blocks, axes, 0, 0, tiled=False)


def dp_scatter(values):
    blocks = values.astype(jnp.bfloat16).reshape((lax.axis_size("dp"), -1) + values.shape[1:])
    return jnp.sum(exchange(blocks, "dp").astype(jnp.float32), axis=0)


def run(chain):
    return lockstep(chain)[0]


def local(
    layer_input,
    out_grad,
    segment_ids,
    valid_mask,
    doc_start,
    norm_gains,
    conv_weight,
    conv_bias,
    mixer_gain,
    shared_proj,
    step_bias,
    decay_log,
    skip_gain,
    mamba_gate,
    mamba_input,
    mamba_step,
    query_proj,
    mamba_out,
    attention_out,
    swiglu_gate,
    swiglu_up,
    swiglu_down,
):
    tensor_position = lax.axis_index("tensor")
    dp_count = lax.axis_size("dp")
    tensor_count = lax.axis_size("tensor")
    device = lax.axis_index("dp") * tensor_count + tensor_position
    ring = Ring(dp_count)
    local_width = mamba_gate.shape[1]
    query_width = query_proj.shape[1]
    head_local = mamba_step.shape[1]
    hidden_width = swiglu_gate.shape[1]
    query_slice = query_width // HEAD_SIZE
    slab = 2 * HEAD_SIZE
    wide = -(-local_width // slab) * slab
    early_width = wide + slab
    block_rows = layer_input.shape[0]
    tokens_per_group = block_rows * tensor_count
    seq_count = tokens_per_group // SEQUENCE_TOKENS
    channel_start = tensor_position * local_width
    head_start = tensor_position * head_local
    channels = conv_weight.shape[1] * dp_count * tensor_count

    def padded(values, columns):
        return jnp.pad(values, ((0, 0), (0, columns - values.shape[1])))

    def placed(rows_in, columns, start):
        whole = jnp.zeros((rows_in.shape[0], columns), rows_in.dtype)
        return lax.dynamic_update_slice_in_dim(whole, rows_in, start, 1)

    device_count = dp_count * tensor_count
    rows_in = mamba_gate.shape[0]
    shared_rows = shared_proj.shape[0]
    small = jnp.concatenate(
        [norm_gains.reshape(-1), conv_weight.reshape(-1), conv_bias, mixer_gain]
    )
    small_width = -(-small.shape[0] // 128) * 128
    if small_width > shared_proj.shape[1]:
        raise ValueError("small parameters")
    small = jnp.pad(small, (0, shared_proj.shape[1] - small.shape[0]))
    small = jnp.pad(small[None], ((0, 7), (0, 0)))
    common = lax.all_gather(jnp.concatenate([shared_proj, small], axis=0), "tensor", axis=0)
    shared_own = common[:, :shared_rows].reshape(rows_in, -1)
    small_own = common[:, shared_rows, :small_width].reshape(1, -1)
    valid_f = valid_mask.astype(jnp.float32)
    out_cot = out_grad.astype(jnp.float32) * valid_f[:, None]
    layer_input, shared_own = together(layer_input, shared_own)
    block = pack(
        rows_in,
        (
            (mamba_gate, wide, False),
            (query_proj, slab, False),
            (mamba_out, local_width, True),
            (attention_out, query_width, True),
            (mamba_input, wide, False),
            (mamba_step, slab, False),
            (shared_own, shared_proj.shape[1], False),
        ),
    )
    extra = jnp.pad(small_own, ((0, 7), (0, block.shape[1] - small_own.shape[1])))

    def prepared():
        spots, gate, up, down = yield [doc_start, swiglu_gate, swiglu_up, swiglu_down]
        position = jnp.tile(jnp.arange(SEQUENCE_TOKENS, dtype=jnp.int32), seq_count) - spots
        ffn_block = pack(
            rows_in,
            ((gate, hidden_width, False), (up, hidden_width, False), (down, hidden_width, True)),
        )
        ffn_blocks = jnp.broadcast_to(ffn_block[None], (dp_count,) + ffn_block.shape)
        cosines, sines, ffn_blocks = yield [*rope_rows(position), ffn_blocks]
        return (ffn_blocks, cosines, sines)

    x_full, (w_in, small_all), ffn_grad_in, waited = lockstep(
        seq_gather(layer_input),
        ring_gather(ring, block, extra),
        after_stages(1, seq_gather(out_cot.astype(jnp.bfloat16))),
        prepared(),
    )
    ffn_blocks, cosine_table, sine_table = waited
    w_in, ffn_grad_in, ffn_blocks = together(w_in, ffn_grad_in, ffn_blocks)
    w_ffn = exchange(ffn_blocks, "dp").reshape(D, -1)
    shared_at = w_in.shape[1] - shared_proj.shape[1]
    late_at = early_width + local_width + query_width
    w_out = w_in[:, early_width:late_at]
    gains_f, conv_f, mixer_gain_f = unpack(
        small_all[:, 0],
        tensor_count,
        small_width,
        (
            (2, norm_gains.shape[1]),
            (CONV + 1, conv_weight.shape[1]),
            (1, mixer_gain.shape[0]),
        ),
    )
    tokens_f = layer_input.astype(jnp.float32)
    scale_one = rms_scale(tokens_f)
    first_full, early_act, late_act, common_act = project(
        x_full,
        gains_f,
        (
            (w_in, early_width, 0),
            (w_in, early_width, late_at),
            (w_in, shared_proj.shape[1], shared_at),
        ),
        block_rows,
    )
    taps = jnp.concatenate(
        [lax.dynamic_slice_in_dim(conv_f, channel_start, local_width, 1), conv_f[:, DSSM:]], axis=1
    )
    own_gain = lax.dynamic_slice_in_dim(mixer_gain_f[0], channel_start, local_width, 0)
    own_bias = lax.dynamic_slice_in_dim(step_bias, head_start, head_local, 0)
    own_decay = lax.dynamic_slice_in_dim(decay_log, head_start, head_local, 0)
    own_skip = lax.dynamic_slice_in_dim(skip_gain, head_start, head_local, 0)
    params = jnp.pad(
        jnp.stack([own_bias, -jnp.exp(own_decay)], axis=0), ((0, 6), (0, slab - head_local))
    )
    skip_row = jnp.broadcast_to(jnp.repeat(own_skip, HEAD_SIZE)[None], (8, local_width))
    doc = doc_start[:, None]
    kv = (tensor_position * query_slice // (QUERY_HEADS // KEY_VALUE_HEADS)).astype(jnp.int32)[None]
    device_ids = jnp.arange(tensor_count, dtype=jnp.int32)
    chip_count = tensor_count // 2
    block_order = (tensor_position // 2 + chip_count - device_ids // 2) % chip_count * 2 + (
        tensor_position + device_ids
    ) % 2

    mamba_y, square_rows, kept_states = mamba_forward(
        block_order, block_rows, early_act, late_act, common_act, doc, taps, params, skip_row
    )
    attended, query_rot, key_rot, value_low, log_total = attention_forward(
        kv, block_order, block_rows, early_act, common_act, cosine_table, sine_table, doc
    )
    square_sum = width_total(square_rows[0])
    gate_scale = lax.rsqrt(square_sum / DSSM + EPS)[:, None]
    gate_z = early_act[:, :local_width]
    sigmoid_z = jax.nn.sigmoid(gate_z)
    silu_z = gate_z * sigmoid_z
    gated_y = mamba_y * silu_z
    normed_b = (gated_y * gate_scale * own_gain).astype(jnp.bfloat16)
    mixed_b = jnp.concatenate([normed_b, attended[:, :query_width]], axis=1)
    mixer_sum = run(seq_reduce(product_nt(mixed_b, w_out).astype(jnp.bfloat16)))

    middle = tokens_f + mixer_sum
    scale_two = rms_scale(middle)
    second_b = (middle * scale_two * gains_f[1]).astype(jnp.bfloat16)
    ffn_in = run(seq_gather(second_b))
    gate_up_grad, hidden_b, second_part, ffn_part = feed_forward(
        ffn_in, ffn_grad_in, w_ffn, block_rows
    )
    ffn_in, ffn_grad_in, second_part = together(ffn_in, ffn_grad_in, second_part)
    second_grad = run(seq_reduce(second_part))
    ffn_w_grad = weight_grads(((ffn_in, gate_up_grad), (ffn_grad_in, hidden_b)))
    second_value_grad, gain_two_grad = norm_back(middle, scale_two, gains_f[1], second_grad)
    middle_grad = out_cot + second_value_grad
    middle_grad, ffn_w_grad = together(middle_grad, ffn_w_grad)
    ffn_w_grad = dp_scatter(ffn_w_grad)

    mixer_grad_full = run(seq_gather(middle_grad.astype(jnp.bfloat16)))
    ffn_part, mixer_grad_full = together(ffn_part, mixer_grad_full)
    mixed_grad = product(mixer_grad_full, w_out)
    normed_grad = mixed_grad[:, :local_width]
    scaled_normed = normed_grad * own_gain
    inner_sum = width_total(jnp.sum(scaled_normed * gated_y, axis=1))
    attended_grad, attended_at = (mixed_grad, local_width // slab)
    if local_width % slab or query_width != slab:
        attended_grad, attended_at = (padded(mixed_grad[:, local_width:], slab), 0)
    dq, dkv = attention_backward(
        kv,
        block_order,
        block_rows,
        query_rot,
        key_rot,
        value_low,
        cosine_table,
        sine_table,
        doc,
        log_total,
        attended_grad,
        attended_at,
    )
    own_gain_grad = jnp.sum(normed_grad * gated_y * gate_scale, axis=0)
    gated_grad = (
        gate_scale * scaled_normed
        - gated_y * (gate_scale * gate_scale * gate_scale) * (inner_sum / DSSM)[:, None]
    )
    mamba_y_grad = gated_grad * silu_z
    gate_z_grad = (gated_grad * mamba_y * sigmoid_z * (1.0 + gate_z * (1.0 - sigmoid_z))).astype(
        jnp.bfloat16
    )
    early_grad = jnp.concatenate([padded(gate_z_grad, wide), dq], axis=1)
    early_w_grad, first_early, gain_one_early = weight_grads(
        ((mixer_grad_full, mixed_b), (first_full, early_grad)), (w_in, 0)
    )
    early_ring = ring_scatter(ring, early_w_grad)
    early_sent = next(early_ring)
    ffn_out = run(seq_reduce(ffn_part))
    result_b, stat_terms = finish(valid_f[:, None], layer_input, mixer_sum, middle, ffn_out)
    mamba_y_grad, first_early = together(mamba_y_grad, first_early)
    late_grad, taps_grad, params_grad = mamba_backward(
        block_order,
        block_rows,
        late_act,
        common_act,
        doc,
        taps,
        params,
        skip_row,
        mamba_y,
        mamba_y_grad,
        dkv,
        kept_states,
    )

    late_grad, ffn_w_grad, *early_sent = together(late_grad, ffn_w_grad, *early_sent)
    gate_w_grad = ffn_w_grad[:, :hidden_width]
    up_w_grad = ffn_w_grad[:, hidden_width : 2 * hidden_width]
    down_w_grad = ffn_w_grad[:, 2 * hidden_width :].T
    early_sent = early_ring.send(early_sent)
    back = (w_in, late_at // late_grad.shape[1])
    if late_at % late_grad.shape[1]:
        back = (w_in[:, late_at:], 0)
    late_w_grad, first_part, gain_one_late = weight_grads(
        ((first_full, late_grad),), back, first_early
    )
    def summed(taps_grad, params_grad, gain_one_late):
        taps_grad, params_grad, gain_one_late = yield [taps_grad, params_grad, gain_one_late]
        gain_one_grad = (gain_one_early + gain_one_late)[:, 0] / gains_f[0]
        heads = jnp.concatenate(
            [
                placed(params_grad[:3, :head_local], slab, head_start),
                padded(stat_terms[:6, 0][None], slab),
            ],
            axis=0,
        )
        conv_rows = jnp.concatenate(
            [
                placed(taps_grad[: CONV + 1, :local_width], DSSM, channel_start),
                taps_grad[: CONV + 1, local_width:],
            ],
            axis=1,
        )
        sums = gather_sums(
            device_count,
            (
                jnp.stack([gain_one_grad, gain_two_grad], axis=0),
                conv_rows,
                placed(own_gain_grad[None], DSSM, channel_start),
            ),
            ((2, norm_gains.shape[1]), (CONV + 1, conv_weight.shape[1]), (1, mixer_gain.shape[0])),
            heads,
            (MH, MH, MH, 6),
        )
        got = exchange(sums, ("dp", "tensor"))
        yield []
        (got,) = yield [got]
        outputs = spread_sums(
            got,
            (
                (2, norm_gains.shape[1]),
                (CONV, conv_weight.shape[1]),
                (1, conv_weight.shape[1]),
                (1, mixer_gain.shape[0]),
                (1, MH),
                (1, MH),
                (1, MH),
                (1, 6),
            ),
        )
        stats = outputs[-1][0]
        return (yield list(outputs[:-1]) + [jnp.sqrt(stats[:5] / (stats[5] * D))])

    def finished(part):
        first_grad = yield from seq_reduce(part)
        first_value_grad, _ = norm_back(tokens_f, scale_one, gains_f[0], first_grad)
        return (yield [middle_grad + first_value_grad])

    late_total, early_total, (input_grad,), outputs = lockstep(
        ring_scatter(ring, late_w_grad),
        resumed(early_ring, early_sent),
        after_stages(1, finished(first_part)),
        summed(taps_grad, params_grad, gain_one_late),
    )
    shared_total = late_total[:, early_width:].astype(jnp.bfloat16)
    places = [
        ((tensor_position // 2 + chip_count - place // 2) % chip_count) * 2
        + (tensor_position + place) % 2
        for place in range(tensor_count)
    ]
    shared_proj_grad = run(
        tensor_scatter(
            lambda place: lax.dynamic_slice_in_dim(
                shared_total, places[place] * shared_rows, shared_rows, 0
            )
        )
    )
    mamba_out_grad = early_total[:, :local_width].T
    attend_out_grad = early_total[:, local_width : local_width + query_width].T
    early_at = local_width + query_width
    gate_proj_grad = early_total[:, early_at : early_at + local_width]
    query_proj_grad = early_total[:, early_at + wide : early_at + wide + query_width]
    input_proj_grad = late_total[:, :local_width]
    step_proj_grad = late_total[:, wide : wide + head_local]
    gains_grad, conv_w_grad, conv_b_grad, gain_full_grad, bias_total, decay_total, skip_total, rms = outputs
    return (
        result_b,
        input_grad,
        gains_grad,
        conv_w_grad,
        conv_b_grad[0],
        gain_full_grad[0],
        shared_proj_grad,
        bias_total[0],
        decay_total[0],
        skip_total[0],
        gate_proj_grad,
        input_proj_grad,
        step_proj_grad,
        query_proj_grad,
        mamba_out_grad,
        attend_out_grad,
        gate_w_grad,
        up_w_grad,
        down_w_grad,
        rms,
    )


def solution(mesh):
    in_specs = (
        P(("dp", "tensor"), None),
        P(("dp", "tensor"), None),
        P("dp"),
        P(("dp", "tensor")),
        P("dp"),
        P(None, ("dp", "tensor")),
        P(None, ("dp", "tensor")),
        P(("dp", "tensor")),
        P(("dp", "tensor")),
        P(("dp", "tensor"), None),
        P(),
        P(),
        P(),
        P("dp", "tensor"),
        P("dp", "tensor"),
        P("dp", "tensor"),
        P("dp", "tensor"),
        P("tensor", "dp"),
        P("tensor", "dp"),
        P("dp", "tensor"),
        P("dp", "tensor"),
        P("tensor", "dp"),
    )
    out_specs = (
        P(("dp", "tensor"), None),
        P(("dp", "tensor"), None),
        P(None, ("dp", "tensor")),
        P(None, ("dp", "tensor")),
        P(("dp", "tensor")),
        P(("dp", "tensor")),
        P(("dp", "tensor"), None),
        P(),
        P(),
        P(),
        P("dp", "tensor"),
        P("dp", "tensor"),
        P("dp", "tensor"),
        P("dp", "tensor"),
        P("tensor", "dp"),
        P("tensor", "dp"),
        P("dp", "tensor"),
        P("dp", "tensor"),
        P("tensor", "dp"),
        P(),
    )
    return jax.shard_map(local, mesh=mesh, in_specs=in_specs, out_specs=out_specs, check_vma=False)
```

```python
import functools
import math

import jax
import jax.numpy as jnp
from jax import lax
from jax.experimental import pallas as pl
from jax.experimental.pallas import tpu as pltpu
from jax.sharding import PartitionSpec as P

D = 1024
MH = 24
HEAD_SIZE = 64
MAMBA_STATES = 128
CONV = 4
QUERY_HEADS = 8
KEY_VALUE_HEADS = 2
SEQUENCE_TOKENS = 1024
DSSM = 1536


EPS = 1e-05
ROPE_BASE = 100000000000.0
NEG_FILL = -1e30
HIGH = lax.Precision.HIGHEST


def rms_scale(values):
    return lax.rsqrt(jnp.mean(values * values, axis=-1, keepdims=True) + EPS)


def norm_back(values, row_scale, gain_row, grad_in):
    scaled_grad = grad_in * gain_row
    gain_grad = jnp.sum(grad_in * values * row_scale, axis=0)
    value_grad = row_scale * scaled_grad - values * (row_scale * row_scale * row_scale) * jnp.mean(
        scaled_grad * values, axis=-1, keepdims=True
    )
    return (value_grad, gain_grad)


def product(left, right):
    return jnp.dot(left, right, preferred_element_type=jnp.float32)


def product_tn(left, right):
    return lax.dot_general(
        left, right, (((0,), (0,)), ((), ())), preferred_element_type=jnp.float32
    )


def product_nt(left, right):
    return lax.dot_general(
        left, right, (((1,), (1,)), ((), ())), preferred_element_type=jnp.float32
    )


def split_dot(values, selector, dims):
    high = values.astype(jnp.bfloat16)
    low = (values - high.astype(jnp.float32)).astype(jnp.bfloat16)
    left = lax.dot_general(high, selector, dims, preferred_element_type=jnp.float32)
    return left + lax.dot_general(low, selector, dims, preferred_element_type=jnp.float32)


def estimate(flops, size):
    return pl.CostEstimate(flops=int(flops * 0.05), bytes_accessed=int(size * 0.05), transcendentals=0)


NN = (((1,), (0,)), ((), ()))
NT = (((1,), (1,)), ((), ()))
TN = (((0,), (0,)), ((), ()))


def mxu(left, right, dims):
    return lax.dot_general(
        left.astype(jnp.bfloat16),
        right.astype(jnp.bfloat16),
        dims,
        preferred_element_type=jnp.float32,
    )


def iota(shape, dim):
    return lax.broadcasted_iota(jnp.int32, shape, dim)


def head_groups(width):
    return [(low, min(low + 2 * HEAD_SIZE, width)) for low in range(0, width, 2 * HEAD_SIZE)]


def chunk_common(chunk, start, rows, width, raw_ref, doc_ref, pad_ref, w_ref, par_ref):
    doc = doc_ref[pl.ds(start, chunk), :]
    age = start + iota((chunk, 1), 0) - doc
    span = pad_ref[pl.ds(start, chunk + 8), :]
    conv = w_ref[CONV : CONV + 1, :] + w_ref[CONV - 1 : CONV, :] * span[8:, :]
    lagged = [span[8:, :]]
    for lag in range(1, CONV):
        moved = jnp.where(age >= lag, span[8 - lag : 8 - lag + chunk, :], 0.0)
        lagged.append(moved)
        conv = conv + w_ref[CONV - 1 - lag : CONV - lag, :] * moved
    sig = jax.nn.sigmoid(conv)
    act = conv * sig
    raw = raw_ref[rows, :] + par_ref[0:1, :]
    step = jnp.maximum(raw, 0.0) + jnp.log1p(jnp.exp(-jnp.abs(raw)))
    rate = step * par_ref[1:2, :]
    lower = (iota((chunk, chunk), 0) >= iota((chunk, chunk), 1)).astype(jnp.bfloat16)
    high = rate.astype(jnp.bfloat16)
    low = (rate - high.astype(jnp.float32)).astype(jnp.bfloat16)
    total = mxu(lower, high, NN) + mxu(lower, low, NN)
    lanes = par_ref.shape[1]
    spread = (iota((lanes, width), 0) == iota((lanes, width), 1) // HEAD_SIZE).astype(jnp.bfloat16)
    key_pos = start + iota((chunk, chunk), 1)
    allowed = (key_pos <= start + iota((chunk, chunk), 0)) & (key_pos >= doc)
    doc_last = doc[chunk - 1 : chunk, :]
    ends = total[chunk - 1 : chunk, :]
    live = jnp.where(doc < start, jnp.exp(total), 0.0)
    keep = jnp.where(start + iota((chunk, 1), 0) >= doc_last, jnp.exp(ends - total), 0.0)
    carry = jnp.where(doc_last < start, jnp.exp(ends), 0.0)
    wide = split_dot(jnp.concatenate([step, live, keep, jnp.broadcast_to(carry, (8, lanes))], axis=0), spread, NN)
    return dict(
        conv=conv, sig=sig, act=act, raw=raw, step=step, total=total, turned=total.T, spread=spread, allowed=allowed,
        carry=carry, age=age, lagged=lagged, lower=lower,
        step_w=wide[:chunk], live_w=wide[chunk : 2 * chunk], keep_w=wide[2 * chunk : 3 * chunk],
        carry_w=wide[3 * chunk : 3 * chunk + 1],
    )


def decay_of(part, head):
    gap = part["total"][:, head : head + 1] - part["turned"][head : head + 1, :]
    return jnp.where(part["allowed"], jnp.exp(gap), 0.0)


def only(values, low, high):
    lane = iota(values.shape, 1)
    return jnp.where((lane >= low) & (lane < high), values, jnp.zeros_like(values))


def place_of(order_ref, block_rows, length, start):
    token = pl.program_id(0) * length + start
    return pl.multiple_of(
        order_ref[token // block_rows] * block_rows + token % block_rows, 128
    )


def fill_conv_input(order_ref, block_rows, width, x_ref, bc_ref, pad_ref):
    length = pad_ref.shape[0] - 8
    pad_ref[0:8, :] = jnp.zeros((8, pad_ref.shape[1]), jnp.float32)
    for start in range(0, length, block_rows):
        rows = pl.ds(place_of(order_ref, block_rows, length, start), block_rows)
        pad_ref[8 + start : 8 + start + block_rows, :width] = x_ref[rows, :width]
        pad_ref[8 + start : 8 + start + block_rows, width:] = bc_ref[rows, :]


def mamba_forward_kernel(
    chunk, width, block_rows, order_ref, x_ref, bc_ref, raw_ref, z_ref, doc_ref, w_ref, par_ref, skip_ref, y_ref, square_ref, kept_ref, pad_ref, state_ref
):
    length = pad_ref.shape[0] - 8
    fill_conv_input(order_ref, block_rows, width, x_ref, bc_ref, pad_ref)
    state_ref[...] = jnp.zeros_like(state_ref)

    def one_chunk(index, _):
        start = pl.multiple_of(index * chunk, chunk)
        rows = pl.ds(place_of(order_ref, block_rows, length, start), chunk)
        part = chunk_common(chunk, start, rows, width, raw_ref, doc_ref, pad_ref, w_ref, par_ref)
        inner = part["act"][:, :width]
        bm = part["act"][:, width : width + MAMBA_STATES].astype(jnp.bfloat16)
        cm = part["act"][:, width + MAMBA_STATES :].astype(jnp.bfloat16)
        driven = (inner * part["step_w"]).astype(jnp.bfloat16)
        pair = mxu(cm, bm, NT)
        pieces = []
        for low, high in head_groups(width):
            heads = range(low // HEAD_SIZE, high // HEAD_SIZE)
            mats = [(decay_of(part, head) * pair).astype(jnp.bfloat16) for head in heads]
            piece = driven[:, low:high]
            right = [
                only(piece, HEAD_SIZE * k, HEAD_SIZE * (k + 1)) if len(mats) > 1 else piece
                for k in range(len(mats))
            ]
            pieces.append(
                mxu(jnp.concatenate(mats, axis=1), jnp.concatenate(right, axis=0), NN)
            )
        state = state_ref[...]
        kept_ref[pl.ds(pl.multiple_of(index * MAMBA_STATES, MAMBA_STATES), MAMBA_STATES), :] = state
        y = jnp.concatenate(pieces, axis=1) + part["live_w"] * mxu(cm, state, NN)
        y = y + skip_ref[0:1, :] * inner
        state_ref[...] = state * part["carry_w"] + mxu(
            bm, driven.astype(jnp.float32) * part["keep_w"], TN
        )
        y_ref[rows, :] = y
        z = z_ref[rows, :width]
        gated = y * z * jax.nn.sigmoid(z)
        square_ref[:, rows] = split_dot_left(gated * gated)
        return 0

    lax.fori_loop(0, length // chunk, one_chunk, 0)


def split_dot_left(values):
    ones = jnp.ones((8, values.shape[1]), jnp.bfloat16)
    high = values.astype(jnp.bfloat16)
    low = (values - high.astype(jnp.float32)).astype(jnp.bfloat16)
    return mxu(ones, high, NT) + mxu(ones, low, NT)


def mamba_backward_kernel(
    chunk, width, block_rows, order_ref, x_ref, bc_ref, raw_ref, doc_ref, w_ref, par_ref, skip_ref, y_ref, dy_ref,
    dkv_ref, kept_ref, din_ref, dw_ref, dpar_ref, pad_ref, state_ref, halo_ref, dskip_ref
):
    length = pad_ref.shape[0] - 8
    count = length // chunk
    wide = x_ref.shape[1]
    common_at = wide + 2 * HEAD_SIZE

    @pl.when(pl.program_id(0) == 0)
    def _():
        if wide > width:
            din_ref[...] = jnp.zeros_like(din_ref)
        din_ref[:, common_at + 2 * MAMBA_STATES :] = dkv_ref[...]

    fill_conv_input(order_ref, block_rows, width, x_ref, bc_ref, pad_ref)
    state_ref[...] = jnp.zeros_like(state_ref)
    halo_ref[...] = jnp.zeros_like(halo_ref)

    @pl.when(pl.program_id(0) == 0)
    def _():
        dw_ref[...] = jnp.zeros_like(dw_ref)
        dpar_ref[...] = jnp.zeros_like(dpar_ref)
        dskip_ref[...] = jnp.zeros_like(dskip_ref)

    def one_chunk(step_index, _):
        index = count - 1 - step_index
        start = pl.multiple_of(index * chunk, chunk)
        rows = pl.ds(place_of(order_ref, block_rows, length, start), chunk)
        part = chunk_common(chunk, start, rows, width, raw_ref, doc_ref, pad_ref, w_ref, par_ref)
        inner = part["act"][:, :width]
        bm = part["act"][:, width : width + MAMBA_STATES].astype(jnp.bfloat16)
        cm = part["act"][:, width + MAMBA_STATES :].astype(jnp.bfloat16)
        driven = (inner * part["step_w"]).astype(jnp.bfloat16)
        driven_f = driven.astype(jnp.float32)
        y = y_ref[rows, :]
        dy = dy_ref[rows, :]
        dy_b = dy.astype(jnp.bfloat16)
        pair = mxu(cm, bm, NT)
        pair_grad = jnp.zeros((chunk, chunk), jnp.float32)
        pieces = []
        for low, high in head_groups(width):
            heads = list(range(low // HEAD_SIZE, high // HEAD_SIZE))
            piece = driven[:, low:high]
            grads = [
                only(dy_b[:, low:high], HEAD_SIZE * k, HEAD_SIZE * (k + 1)) if len(heads) > 1 else dy_b[:, low:high]
                for k in range(len(heads))
            ]
            mats = []
            for k, head in enumerate(heads):
                decay = decay_of(part, head)
                mats.append((decay * pair).astype(jnp.bfloat16))
                pair_grad = pair_grad + decay * mxu(grads[k], piece, NT)
            pieces.append(mxu(jnp.concatenate(mats, axis=0), jnp.concatenate(grads, axis=0), TN))
        within = jnp.concatenate(pieces, axis=1)
        state = kept_ref[pl.ds(pl.multiple_of(index * MAMBA_STATES, MAMBA_STATES), MAMBA_STATES), :]
        state_grad = state_ref[...]
        pair_grad = pair_grad.astype(jnp.bfloat16)
        dy_live = (dy * part["live_w"]).astype(jnp.bfloat16)
        driven_keep = (driven_f * part["keep_w"]).astype(jnp.bfloat16)
        later = part["keep_w"] * mxu(bm, state_grad, NN)
        c_grad = mxu(pair_grad, bm, NN) + mxu(dy_live, state, NT)
        b_grad = mxu(pair_grad, cm, TN) + mxu(driven_keep, state_grad, NT)
        state_ref[...] = state_grad * part["carry_w"] + mxu(cm, dy_live, TN)
        driven_grad = within + later
        later_part = driven_f * later
        mixed = y - skip_ref[0:1, :] * inner
        sums = split_dot(
            jnp.concatenate(
                [
                    dy_b.astype(jnp.float32) * mixed - driven_f * within - later_part,
                    driven_grad * inner,
                    jnp.broadcast_to(
                        jnp.sum(later_part, axis=0, keepdims=True)
                        + part["carry_w"] * jnp.sum(state_grad * state, axis=0, keepdims=True),
                        (8, width),
                    ),
                ],
                axis=0,
            ),
            part["spread"],
            NT,
        )
        high = sums[:chunk].astype(jnp.bfloat16)
        low = (sums[:chunk] - high.astype(jnp.float32)).astype(jnp.bfloat16)
        rate_grad = (
            mxu(part["lower"], high, TN) + mxu(part["lower"], low, TN) + sums[2 * chunk : 2 * chunk + 1]
        )
        step_grad = rate_grad * par_ref[1:2, :] + sums[chunk : 2 * chunk]
        raw_grad = step_grad * jax.nn.sigmoid(part["raw"])
        din_ref[rows, wide:common_at] = raw_grad.astype(jnp.bfloat16)
        dpar_ref[0:1, :] += jnp.sum(raw_grad, axis=0, keepdims=True)
        dpar_ref[1:2, :] += par_ref[1:2, :] * jnp.sum(rate_grad * part["step"], axis=0, keepdims=True)
        dskip_ref[0:1, :] += jnp.sum(dy * inner, axis=0, keepdims=True)
        inner_grad = driven_grad * part["step_w"] + skip_ref[0:1, :] * dy
        sig, conv = (part["sig"], part["conv"])
        conv_grad = jnp.concatenate([inner_grad, b_grad, c_grad], axis=1) * (
            sig * (1.0 + conv * (1.0 - sig))
        )
        dw_ref[CONV : CONV + 1, :] += jnp.sum(conv_grad, axis=0, keepdims=True)
        v_grad = w_ref[CONV - 1 : CONV, :] * conv_grad
        long = jnp.concatenate([conv_grad, halo_ref[...]], axis=0)
        next_start = jnp.minimum(start + chunk, length - 8)
        ages = jnp.concatenate([part["age"], start + chunk + iota((8, 1), 0) - doc_ref[pl.ds(pl.multiple_of(next_start, 8), 8), :]], axis=0)
        dw_ref[CONV - 1 : CONV, :] += jnp.sum(conv_grad * part["lagged"][0], axis=0, keepdims=True)
        for lag in range(1, CONV):
            dw_ref[CONV - 1 - lag : CONV - lag, :] += jnp.sum(
                conv_grad * part["lagged"][lag], axis=0, keepdims=True
            )
            masked = jnp.where(ages >= lag, long, 0.0)
            v_grad = v_grad + w_ref[CONV - 1 - lag : CONV - lag, :] * masked[lag : lag + chunk, :]
        halo_ref[...] = conv_grad[:8, :]
        din_ref[rows, :width] = v_grad[:, :width].astype(jnp.bfloat16)
        din_ref[rows, common_at : common_at + 2 * MAMBA_STATES] = v_grad[:, width:].astype(jnp.bfloat16)
        return 0

    lax.fori_loop(0, count, one_chunk, 0)

    @pl.when(pl.program_id(0) == pl.num_programs(0) - 1)
    def _():
        lanes = dpar_ref.shape[1]
        spread = (iota((lanes, width), 0) == iota((lanes, width), 1) // HEAD_SIZE).astype(jnp.bfloat16)
        dpar_ref[2:3, :] = split_dot(dskip_ref[...], spread, NT)[0:1]


CHUNK = 256
VMEM_LIMIT = 60 * 1024 * 1024


def tokens_spec(tokens, width, place=0):
    return pl.BlockSpec((tokens, width), lambda i, *_: (0, place))


def whole_spec(shape):
    return pl.BlockSpec(shape, lambda i, *_: (0,) * len(shape))


def mamba_forward(order, block_rows, early, late, common, doc, taps, params, skip_row, chunk=CHUNK):
    tokens = late.shape[0]
    width = skip_row.shape[1]
    lanes = params.shape[1]
    wide = late.shape[1] - lanes
    seq = SEQUENCE_TOKENS
    count = tokens // seq
    kept = seq // chunk * MAMBA_STATES
    return pl.pallas_call(
        functools.partial(mamba_forward_kernel, chunk, width, block_rows),
        grid_spec=pltpu.PrefetchScalarGridSpec(
        num_scalar_prefetch=1,
        grid=(count,),
        in_specs=[
            tokens_spec(tokens, wide),
            tokens_spec(tokens, 2 * MAMBA_STATES),
            tokens_spec(tokens, lanes, wide // lanes),
            tokens_spec(tokens, wide),
            pl.BlockSpec((seq, 1), lambda i, *_: (i, 0)),
            whole_spec(taps.shape),
            whole_spec(params.shape),
            whole_spec(skip_row.shape),
        ],
        out_specs=[
            tokens_spec(tokens, width),
            whole_spec((8, tokens)),
            pl.BlockSpec((kept, width), lambda i, *_: (i, 0)),
        ],
        scratch_shapes=[
            pltpu.VMEM((seq + 8, width + 2 * MAMBA_STATES), jnp.float32),
            pltpu.VMEM((MAMBA_STATES, width), jnp.float32),
        ],
        ),
        out_shape=[
            jax.ShapeDtypeStruct((tokens, width), jnp.float32),
            jax.ShapeDtypeStruct((8, tokens), jnp.float32),
            jax.ShapeDtypeStruct((count * kept, width), jnp.float32),
        ],
        compiler_params=pltpu.CompilerParams(vmem_limit_bytes=VMEM_LIMIT),
        cost_estimate=estimate(tokens * width * 20000, tokens * width * 20),
    )(order, late, common, late, early, doc, taps, params, skip_row)


def mamba_backward(
    order, block_rows, late, common, doc, taps, params, skip_row, y, dy, dkv, kept_states, chunk=CHUNK
):
    tokens = late.shape[0]
    width = skip_row.shape[1]
    lanes = params.shape[1]
    wide = late.shape[1] - lanes
    seq = SEQUENCE_TOKENS
    count = tokens // seq
    kept = seq // chunk * MAMBA_STATES
    conv_width = width + 2 * MAMBA_STATES
    return pl.pallas_call(
        functools.partial(mamba_backward_kernel, chunk, width, block_rows),
        grid_spec=pltpu.PrefetchScalarGridSpec(
        num_scalar_prefetch=1,
        grid=(count,),
        in_specs=[
            tokens_spec(tokens, wide),
            tokens_spec(tokens, 2 * MAMBA_STATES),
            tokens_spec(tokens, lanes, wide // lanes),
            pl.BlockSpec((seq, 1), lambda i, *_: (i, 0)),
            whole_spec(taps.shape),
            whole_spec(params.shape),
            whole_spec(skip_row.shape),
            tokens_spec(tokens, width),
            tokens_spec(tokens, width),
            tokens_spec(tokens, dkv.shape[1]),
            pl.BlockSpec((kept, width), lambda i, *_: (i, 0)),
        ],
        out_specs=[
            tokens_spec(tokens, late.shape[1] + common.shape[1]),
            whole_spec((8, conv_width)),
            whole_spec((8, lanes)),
        ],
        scratch_shapes=[
            pltpu.VMEM((seq + 8, conv_width), jnp.float32),
            pltpu.VMEM((MAMBA_STATES, width), jnp.float32),
            pltpu.VMEM((8, conv_width), jnp.float32),
            pltpu.VMEM((8, width), jnp.float32),
        ],
        ),
        out_shape=[
            jax.ShapeDtypeStruct((tokens, late.shape[1] + common.shape[1]), jnp.bfloat16),
            jax.ShapeDtypeStruct((8, conv_width), jnp.float32),
            jax.ShapeDtypeStruct((8, lanes), jnp.float32),
        ],
        compiler_params=pltpu.CompilerParams(vmem_limit_bytes=VMEM_LIMIT),
        cost_estimate=estimate(tokens * width * 60000, tokens * width * 20),
    )(
        order, late, common, late, doc, taps, params, skip_row, y, dy, dkv, kept_states
    )


NEGATIVE = -1e30
QUERY_BLOCK = 256


def swap_halves(values):
    half = HEAD_SIZE // 2
    lane = iota(values.shape, 1)
    width = values.shape[1]
    return jnp.where(
        lane % HEAD_SIZE < half,
        pltpu.roll(values, width - half, 1),
        pltpu.roll(values, half, 1),
    )


def attention_mask(start, rows, keys, doc):
    position = start + iota((rows, 1), 0)
    key_pos = iota((rows, keys), 1)
    return (key_pos <= position) & (key_pos >= doc)


def both_heads(values):
    return jnp.concatenate(
        [only(values, 0, HEAD_SIZE), only(values, HEAD_SIZE, 2 * HEAD_SIZE)], axis=0
    )


def chosen(values, kv):
    lane = iota(values.shape, 1)
    turned = pltpu.roll(values, HEAD_SIZE, 1)
    return jnp.where((lane < HEAD_SIZE) == (kv == 0), values, turned)


def attention_forward_kernel(
    block_rows, kv_ref, order_ref, q_ref, key_ref, value_ref, cos_ref, sin_ref, doc_ref, out_ref, qr_ref, kr_ref, vr_ref, log_ref
):
    length = qr_ref.shape[0]
    kv = kv_ref[0]
    rows = block_rows
    for start in range(0, length, rows):
        block = slice(start, start + rows)
        place = pl.ds(place_of(order_ref, block_rows, length, start), rows)
        cos, sin = (cos_ref[block, :], sin_ref[block, :])
        query, key = (q_ref[place, :], key_ref[place, :])
        turned = (query * cos + swap_halves(query) * sin).astype(jnp.bfloat16)
        qr_ref[block, :] = (turned.astype(jnp.float32) * HEAD_SIZE**-0.5).astype(jnp.bfloat16)
        kr_ref[block, :] = chosen(key * cos + swap_halves(key) * sin, kv).astype(jnp.bfloat16)
        vr_ref[block, :] = chosen(value_ref[place, :], kv).astype(jnp.bfloat16)
        keys = start + rows
        mask = attention_mask(start, rows, keys, doc_ref[block, :])
        scores = mxu(both_heads(qr_ref[block, :]), kr_ref[0:keys, :], NT)
        outs = []
        logs = []
        for head in range(2):
            part = jnp.where(mask, scores[head * rows : (head + 1) * rows], NEGATIVE)
            peak = jnp.max(part, axis=1, keepdims=True)
            weight = jnp.exp(part - peak)
            total = jnp.sum(weight, axis=1, keepdims=True)
            outs.append(mxu(weight * (1.0 / total), vr_ref[0:keys, :], NN))
            logs.append(peak + jnp.log(total))
        lane = iota((rows, 2 * HEAD_SIZE), 1)
        out_ref[place, :] = jnp.where(lane < HEAD_SIZE, outs[0], outs[1]).astype(jnp.bfloat16)
        log_ref[block, :] = jnp.where(lane < HEAD_SIZE, logs[0], logs[1])


def attention_backward_kernel(
    block_rows, kv_ref, order_ref, qr_ref, kr_ref, vr_ref, cos_ref, sin_ref, doc_ref, log_ref, grad_ref, dq_ref, dkv_ref, dk_ref, dv_ref
):
    length = qr_ref.shape[0]
    kv = kv_ref[0]
    rows = block_rows
    lane = iota((rows, 2 * HEAD_SIZE), 1)
    mine = (lane < HEAD_SIZE) == (kv == 0)
    dk_ref[...] = jnp.zeros_like(dk_ref)
    dv_ref[...] = jnp.zeros_like(dv_ref)
    for start in reversed(range(0, length, rows)):
        keys = start + rows
        block = slice(start, start + rows)
        place = pl.ds(place_of(order_ref, block_rows, length, start), rows)
        mask = attention_mask(start, rows, keys, doc_ref[block, :])
        query = both_heads(qr_ref[block, :])
        grad = both_heads(grad_ref[place, :].astype(jnp.bfloat16))
        logs = log_ref[block, :]
        scores = mxu(query, kr_ref[0:keys, :], NT)
        prob_grad = mxu(grad, vr_ref[0:keys, :], NT)
        probs = []
        score_grads = []
        for head in range(2):
            part = slice(head * rows, (head + 1) * rows)
            log = logs[:, head * HEAD_SIZE : head * HEAD_SIZE + 1]
            weight = jnp.where(mask, jnp.exp(scores[part] - log), 0.0)
            product_grad = weight * prob_grad[part]
            total = jnp.sum(product_grad, axis=1, keepdims=True)
            probs.append(weight.astype(jnp.bfloat16))
            score_grads.append((product_grad - weight * total).astype(jnp.bfloat16))
        cos, sin = (cos_ref[block, :], sin_ref[block, :])
        dq = mxu(jnp.concatenate(score_grads, axis=0), kr_ref[0:keys, :], NN)
        dq = jnp.where(lane < HEAD_SIZE, dq[:rows], dq[rows:]) * HEAD_SIZE**-0.5
        dq = dq * cos - swap_halves(dq) * sin
        dq_ref[place, :] = dq.astype(jnp.bfloat16)
        dk_ref[0:keys, :] += mxu(jnp.concatenate(score_grads, axis=0), query, TN)
        dv_ref[0:keys, :] += mxu(jnp.concatenate(probs, axis=0), grad, TN)
        dk = dk_ref[block, :]
        dk = dk + pltpu.roll(dk, HEAD_SIZE, 1)
        dk = dk * cos - swap_halves(dk) * sin
        dv = dv_ref[block, :]
        dv = dv + pltpu.roll(dv, HEAD_SIZE, 1)
        dkv_ref[place, : 2 * HEAD_SIZE] = jnp.where(mine, dk, 0.0).astype(jnp.bfloat16)
        dkv_ref[place, 2 * HEAD_SIZE :] = jnp.where(mine, dv, 0.0).astype(jnp.bfloat16)


def attention_call(kernel, kv, order, block_rows, tokens, ins, outs, scratch, flops):
    seq = SEQUENCE_TOKENS

    def spec(columns, place):
        if place is None:
            return pl.BlockSpec((seq, columns), lambda i, *_: (i, 0))
        return tokens_spec(tokens, columns, place)

    return pl.pallas_call(
        functools.partial(kernel, block_rows),
        grid_spec=pltpu.PrefetchScalarGridSpec(
            num_scalar_prefetch=2,
            grid=(tokens // seq,),
            in_specs=[spec(columns, place) for _, columns, place in ins],
            out_specs=[spec(columns, place) for _, columns, place in outs],
            scratch_shapes=scratch,
        ),
        out_shape=[jax.ShapeDtypeStruct((tokens, columns), kind) for kind, columns, _ in outs],
        compiler_params=pltpu.CompilerParams(vmem_limit_bytes=VMEM_LIMIT),
        cost_estimate=estimate(flops * tokens, tokens * 4096),
    )(kv, order, *[value for value, _, _ in ins])


def attention_forward(kv, order, block_rows, early, common, cos, sin, doc):
    two = 2 * HEAD_SIZE
    low, full = (jnp.bfloat16, jnp.float32)
    query_at = early.shape[1] // two - 1
    key_at = 2 * MAMBA_STATES // two
    return attention_call(
        attention_forward_kernel,
        kv,
        order,
        block_rows,
        early.shape[0],
        (
            (early, two, query_at),
            (common, two, key_at),
            (common, two, key_at + 1),
            (cos, two, None),
            (sin, two, None),
            (doc, 1, None),
        ),
        ((low, two, 0), (low, two, None), (low, two, None), (low, two, None), (full, two, None)),
        [],
        4000000,
    )


def attention_backward(kv, order, block_rows, qr, kr, vr, cos, sin, doc, log, grad, grad_at):
    two = 2 * HEAD_SIZE
    seq = SEQUENCE_TOKENS
    return attention_call(
        attention_backward_kernel,
        kv,
        order,
        block_rows,
        qr.shape[0],
        (
            (qr, two, None),
            (kr, two, None),
            (vr, two, None),
            (cos, two, None),
            (sin, two, None),
            (doc, 1, None),
            (log, two, None),
            (grad, two, grad_at),
        ),
        ((jnp.bfloat16, two, 0), (jnp.bfloat16, 2 * two, 0)),
        [pltpu.VMEM((seq, two), jnp.float32), pltpu.VMEM((seq, two), jnp.float32)],
        9000000,
    )


def pack_kernel(widths, turned, *refs):
    spot = 0
    out_ref = refs[-1]
    for ref, width, turn in zip(refs, widths, turned):
        value = ref[...].T if turn else ref[...]
        have = value.shape[1]
        out_ref[:, spot : spot + have] = value
        if width > have:
            out_ref[:, spot + have : spot + width] = jnp.zeros(
                (value.shape[0], width - have), value.dtype
            )
        spot += width


def pack(rows, pieces):
    widths = [width for _, width, _ in pieces]
    turned = [turn for _, _, turn in pieces]
    arrays = [value for value, _, _ in pieces]
    size = rows * sum(widths)
    return pl.pallas_call(
        functools.partial(pack_kernel, widths, turned),
        out_shape=jax.ShapeDtypeStruct((rows, sum(widths)), arrays[0].dtype),
        compiler_params=pltpu.CompilerParams(vmem_limit_bytes=VMEM_LIMIT),
        cost_estimate=estimate(size, 4 * size),
    )(*arrays)


def unpack_kernel(groups, size, pieces, small_ref, *out_refs):
    spot = 0
    for out_ref, (rows, width) in zip(out_refs, pieces):
        total = out_ref.shape[1]
        column = iota((width, total), 1)
        owner = iota((small_ref.shape[0], total), 1) // (width * groups)
        mine = owner == iota((small_ref.shape[0], total), 0)
        for row in range(rows):
            found = jnp.zeros((small_ref.shape[0], total), jnp.float32)
            for group in range(groups):
                pick = (column % width == iota((width, total), 0)) & (
                    column // width % groups == group
                )
                start = group * size + spot
                found = found + mxu(
                    small_ref[:, start : start + width], pick.astype(jnp.bfloat16), NN
                )
            out_ref[row : row + 1, :] = jnp.sum(
                jnp.where(mine, found, 0.0), axis=0, keepdims=True
            )
            spot += width
        if rows < out_ref.shape[0]:
            out_ref[rows:, :] = jnp.zeros((out_ref.shape[0] - rows, total), jnp.float32)


def unpack(small, groups, size, pieces):
    count = small.shape[0] * groups
    return pl.pallas_call(
        functools.partial(unpack_kernel, groups, size, pieces),
        out_shape=[
            jax.ShapeDtypeStruct((8, count * width), jnp.float32) for _, width in pieces
        ],
        compiler_params=pltpu.CompilerParams(vmem_limit_bytes=VMEM_LIMIT),
        cost_estimate=estimate(1 << 26, 1 << 18),
    )(small)


def project_kernel(count, x_ref, gain_ref, *refs):
    x = x_ref[...].astype(jnp.float32)
    scale = lax.rsqrt(jnp.mean(x * x, axis=1, keepdims=True) + EPS)
    first = (x * scale * gain_ref[0:1, :]).astype(jnp.bfloat16)
    refs[count][...] = first
    for w_ref, out_ref in zip(refs[:count], refs[count + 1 :]):
        out_ref[...] = mxu(first, w_ref[...], NN)


def project(x, gains, weights, rows):
    tokens, width = x.shape
    arrays, specs = ([], [])
    for array, columns, start in weights:
        if start % columns:
            array, start = (array[:, start : start + columns], 0)
        arrays.append(array)
        specs.append(
            pl.BlockSpec(
                (width, columns), functools.partial(lambda place, i: (0, place), start // columns)
            )
        )
    by_rows = lambda columns: pl.BlockSpec((rows, columns), lambda i: (i, 0))
    total = sum(columns for _, columns, _ in weights)
    return pl.pallas_call(
        functools.partial(project_kernel, len(weights)),
        grid=(tokens // rows,),
        in_specs=[by_rows(width), pl.BlockSpec(gains.shape, lambda i: (0, 0))] + specs,
        out_specs=[by_rows(width)] + [by_rows(columns) for _, columns, _ in weights],
        out_shape=[jax.ShapeDtypeStruct((tokens, width), jnp.bfloat16)]
        + [jax.ShapeDtypeStruct((tokens, columns), jnp.float32) for _, columns, _ in weights],
        compiler_params=pltpu.CompilerParams(vmem_limit_bytes=VMEM_LIMIT),
        cost_estimate=estimate(2 * tokens * width * total, 2 * width * total + 4 * tokens * (width + total)),
    )(x, gains, *arrays)


def gather_kernel(pieces, extra, *refs):
    out_ref = refs[-1]
    count = out_ref.shape[0]
    out_ref[...] = jnp.zeros_like(out_ref)
    spot = 0
    for ref, (rows, width) in zip(refs, pieces):
        total = ref.shape[1]
        pick = (iota((total, width), 0) % width == iota((total, width), 1)).astype(jnp.bfloat16)
        mine = iota((count, total), 1) // width == iota((count, total), 0)
        for row in range(rows):
            rest = jnp.where(mine, ref[row : row + 1, :], 0.0)
            found = jnp.zeros((count, width), jnp.float32)
            for _ in range(3):
                low = rest.astype(jnp.bfloat16)
                found = found + mxu(low, pick, NN)
                rest = rest - low.astype(jnp.float32)
            out_ref[:, spot : spot + width] = found
            spot += width
    for row in range(refs[-2].shape[0]):
        width = extra[row]
        out_ref[:, spot : spot + width] = jnp.broadcast_to(
            refs[-2][row : row + 1, :width], (count, width)
        )
        spot += width


def gather_sums(count, arrays, pieces, everywhere, extra):
    columns = sum(rows * width for rows, width in pieces) + sum(extra)
    columns = -(-columns // 128) * 128
    return pl.pallas_call(
        functools.partial(gather_kernel, pieces, extra),
        out_shape=jax.ShapeDtypeStruct((count, columns), jnp.float32),
        compiler_params=pltpu.CompilerParams(vmem_limit_bytes=VMEM_LIMIT),
        cost_estimate=estimate(1 << 26, 1 << 18),
    )(*arrays, everywhere)


def spread_kernel(shapes, got_ref, *out_refs):
    sums = jnp.sum(got_ref[...], axis=0, keepdims=True)
    spot = 0
    for out_ref, (rows, width) in zip(out_refs, shapes):
        for row in range(rows):
            out_ref[row : row + 1, :] = sums[:, spot : spot + width]
            spot += width


def spread_sums(got, shapes):
    return pl.pallas_call(
        functools.partial(spread_kernel, shapes),
        out_shape=[jax.ShapeDtypeStruct(shape, jnp.float32) for shape in shapes],
        compiler_params=pltpu.CompilerParams(vmem_limit_bytes=VMEM_LIMIT),
        cost_estimate=estimate(1 << 16, 1 << 17),
    )(got)


def weight_grad_kernel(count, with_back, *refs):
    lefts, rights = (refs[:count], refs[count : 2 * count])
    rest = refs[2 * count :]
    out_ref = rest[-3] if with_back else rest[-1]
    spot = 0
    for left, right in zip(lefts, rights):
        grad = mxu(left[...], right[...], TN)
        columns = right.shape[1]
        out_ref[:, spot : spot + columns] = grad.astype(jnp.bfloat16)
        spot += columns
    if with_back:
        w_ref = rest[0]
        part = mxu(rights[-1][...], w_ref[...], NT)
        if len(rest) > 4:
            part = part + rest[1][...].astype(jnp.float32)
        rest[-2][...] = part.astype(rest[-2].dtype)
        rest[-1][...] = jnp.sum(grad * w_ref[...].astype(jnp.float32), axis=1, keepdims=True)


def weight_grads(pairs, back=None, base=None, kind=jnp.bfloat16):
    tokens, rows = pairs[0][0].shape
    total = sum(right.shape[1] for _, right in pairs)
    block = min(rows, 512)
    ins = [left for left, _ in pairs] + [right for _, right in pairs]
    specs = [pl.BlockSpec((tokens, block), lambda i: (0, i)) for _ in pairs]
    specs += [pl.BlockSpec((tokens, right.shape[1]), lambda i: (0, 0)) for _, right in pairs]
    outs = [jax.ShapeDtypeStruct((rows, total), jnp.bfloat16)]
    out_specs = [pl.BlockSpec((block, total), lambda i: (i, 0))]
    flops = 2 * tokens * rows * total
    if back is not None:
        weight, place = back
        ins.append(weight)
        specs.append(pl.BlockSpec((block, pairs[-1][1].shape[1]), lambda i: (i, place)))
        if base is not None:
            ins.append(base)
            specs.append(pl.BlockSpec((tokens, block), lambda i: (0, i)))
        outs += [
            jax.ShapeDtypeStruct((tokens, rows), kind),
            jax.ShapeDtypeStruct((rows, 1), jnp.float32),
        ]
        out_specs += [
            pl.BlockSpec((tokens, block), lambda i: (0, i)),
            pl.BlockSpec((block, 1), lambda i: (i, 0)),
        ]
        flops += 2 * tokens * rows * pairs[-1][1].shape[1]
    result = pl.pallas_call(
        functools.partial(weight_grad_kernel, len(pairs), back is not None),
        grid=(rows // block,),
        in_specs=specs,
        out_specs=out_specs,
        out_shape=outs,
        compiler_params=pltpu.CompilerParams(vmem_limit_bytes=VMEM_LIMIT),
        cost_estimate=estimate(flops, 4 * tokens * rows + 2 * rows * total),
    )(*ins)
    return result if back is not None else result[0]


def feed_forward_kernel(hidden_width, x_ref, cot_ref, w_ref, grad_ref, hidden_ref, back_ref, out_ref):
    wide = 2 * hidden_width
    acts = mxu(x_ref[...], w_ref[:, :wide], NN)
    hidden_grad = mxu(cot_ref[...], w_ref[:, wide:], NN)
    gate, up = (acts[:, :hidden_width], acts[:, hidden_width:])
    sig = jax.nn.sigmoid(gate)
    silu = gate * sig
    grads = jnp.concatenate(
        [hidden_grad * up * (sig * (1.0 + gate * (1.0 - sig))), hidden_grad * silu], axis=1
    ).astype(jnp.bfloat16)
    grad_ref[...] = grads
    back_ref[...] = mxu(grads, w_ref[:, :wide], NT).astype(jnp.bfloat16)
    hidden = (silu * up).astype(jnp.bfloat16)
    hidden_ref[...] = hidden
    out_ref[...] = mxu(hidden, w_ref[:, wide:], NT).astype(jnp.bfloat16)


def feed_forward(x, cot, weights, rows):
    tokens, width = x.shape
    hidden_width = weights.shape[1] // 3
    by_rows = lambda columns: pl.BlockSpec((rows, columns), lambda i: (i, 0))
    sizes = (2 * hidden_width, hidden_width, width, width)
    return pl.pallas_call(
        functools.partial(feed_forward_kernel, hidden_width),
        grid=(tokens // rows,),
        in_specs=[by_rows(width), by_rows(width), pl.BlockSpec(weights.shape, lambda i: (0, 0))],
        out_specs=[by_rows(columns) for columns in sizes],
        out_shape=[jax.ShapeDtypeStruct((tokens, columns), jnp.bfloat16) for columns in sizes],
        compiler_params=pltpu.CompilerParams(vmem_limit_bytes=VMEM_LIMIT),
        cost_estimate=estimate(12 * tokens * width * hidden_width, 14 * tokens * width),
    )(x, cot, weights)


def finish_kernel(valid_ref, x_ref, mixer_ref, middle_ref, ffn_ref, out_ref, stat_ref):
    valid = valid_ref[...]
    middle, ffn = (middle_ref[...], ffn_ref[...])
    result = middle + ffn
    out_ref[...] = result.astype(jnp.bfloat16)
    tracked = (x_ref[...].astype(jnp.float32), mixer_ref[...], middle, ffn, result)
    stat_ref[...] = jnp.zeros_like(stat_ref)
    for k, values in enumerate(tracked):
        stat_ref[k : k + 1, 0:1] = jnp.sum(
            valid * jnp.sum(values * values, axis=1, keepdims=True), axis=0, keepdims=True
        )
    stat_ref[len(tracked) : len(tracked) + 1, 0:1] = jnp.sum(valid, axis=0, keepdims=True)


def finish(valid, x, mixer_sum, middle, ffn_out):
    return pl.pallas_call(
        finish_kernel,
        out_shape=[
            jax.ShapeDtypeStruct(x.shape, jnp.bfloat16),
            jax.ShapeDtypeStruct((8, 128), jnp.float32),
        ],
        compiler_params=pltpu.CompilerParams(vmem_limit_bytes=VMEM_LIMIT),
        cost_estimate=estimate(16 * x.size, 16 * x.size),
    )(valid, x, mixer_sum, middle, ffn_out)


def resumed(chain, sent):
    while True:
        got = yield sent
        try:
            sent = chain.send(got)
        except StopIteration as stop:
            return stop.value


def passengers(stages, *values):
    for _ in range(stages):
        yield []
    return (yield list(values))


def rope_rows(position):
    lane = jnp.arange(2 * HEAD_SIZE, dtype=jnp.int32)
    half = HEAD_SIZE // 2
    inverse = jnp.exp(
        (lane % half).astype(jnp.float32) * (-2.0 * math.log(ROPE_BASE) / HEAD_SIZE)
    )
    angles = position.astype(jnp.float32)[:, None] * inverse[None, :]
    sign = jnp.where(lane % HEAD_SIZE < half, -1.0, 1.0)
    return (jnp.cos(angles), jnp.sin(angles) * sign[None, :])
def grid_of(count):
    rows = 1
    while 8 * rows * rows <= count:
        rows *= 2
    return (count // rows, rows)


def ring_cycle(count):
    depth, rows = grid_of(count)
    order = []
    for level in range(depth):
        inner = list(range(1, rows))
        if level % 2:
            inner.reverse()
        order += [level * rows + row for row in inner]
    return order + [level * rows for level in reversed(range(depth))]


class Ring:
    def __init__(self, count):
        self.count = count
        self.order = ring_cycle(count)
        self.depth, self.rows = grid_of(count)
        inner = self.rows - 1
        mine = lax.axis_index("dp")
        level, row = (mine // self.rows, mine % self.rows)
        step = jnp.where(level % 2 == 0, row - 1, inner - row)
        self.spot = jnp.where(
            row > 0, level * inner + step, self.depth * inner + self.depth - 1 - level
        )

    def device_at(self, offset):
        inner = self.rows - 1
        spot = (self.spot + offset + self.count) % self.count
        level, step = (spot // inner, spot % inner)
        row = jnp.where(level % 2 == 0, step + 1, inner - step)
        back = self.count - 1 - spot
        return jnp.where(spot < self.depth * inner, level * self.rows + row, back * self.rows)

    def send(self, block, step):
        count, order = (self.count, self.order)
        return lax.ppermute(
            block, "dp", [(order[k], order[(k + step) % count]) for k in range(count)]
        )


def together(*values):
    return lax.optimization_barrier(values)


def lockstep(*chains):
    results = [None] * len(chains)
    waiting = {k: None for k in range(len(chains))}
    while waiting:
        sent = {}
        for k in list(waiting):
            try:
                sent[k] = chains[k].send(waiting[k])
            except StopIteration as stop:
                results[k] = stop.value
                del waiting[k]
        flat = [value for k in sent for value in sent[k]]
        if len(flat) > 1:
            flat = list(together(*flat))
        for k in sent:
            waiting[k] = flat[: len(sent[k])]
            flat = flat[len(sent[k]) :]
    return results


def after_stages(count, chain):
    for _ in range(count):
        yield []
    return (yield from chain)


def ring_gather(ring, block, extra):
    count = ring.count
    rows = block.shape[0]
    half = rows // 2
    whole = jnp.concatenate([block, extra], axis=0)
    out = jnp.zeros((count * rows,) + block.shape[1:], block.dtype)
    more = jnp.zeros((count,) + extra.shape, block.dtype)

    def put(arrays, piece, offset, start=0):
        out, more = arrays
        device = ring.device_at(offset)
        kept = min(piece.shape[0], rows - start)
        out = lax.dynamic_update_slice_in_dim(out, piece[:kept], device * rows + start, 0)
        if piece.shape[0] > kept:
            more = lax.dynamic_update_index_in_dim(more, piece[kept:], device, 0)
        return (out, more)

    arrays = put((out, more), whole, 0)
    ahead = behind = whole
    for step in range(1, count // 2):
        ahead, behind = yield [ring.send(ahead, 1), ring.send(behind, -1)]
        arrays = put(arrays, ahead, -step)
        arrays = put(arrays, behind, step)
    ahead, behind = yield [ring.send(ahead[:half], 1), ring.send(behind[half:], -1)]
    arrays = put(arrays, ahead, -(count // 2))
    return put(arrays, behind, count // 2, half)


def ring_scatter(ring, *parts):
    count = ring.count
    rows = parts[0].shape[0] // count
    half = rows // 2

    def piece(offset, start=0, size=rows):
        first = ring.device_at(offset) * rows + start
        return jnp.concatenate(
            [lax.dynamic_slice_in_dim(part, first, size, 0).astype(jnp.float32) for part in parts],
            axis=1,
        )

    far = count // 2
    ahead = piece(far, 0, half).astype(jnp.bfloat16)
    behind = piece(far, half, rows - half).astype(jnp.bfloat16)
    for offset in range(far - 1, -1, -1):
        ahead, behind = yield [ring.send(ahead, 1), ring.send(behind, -1)]
        ahead, behind = (ahead.astype(jnp.float32), behind.astype(jnp.float32))
        if offset == far - 1:
            ahead, behind = (
                jnp.concatenate([ahead, jnp.zeros_like(behind)], axis=0),
                jnp.concatenate([jnp.zeros_like(ahead), behind], axis=0),
            )
        if offset:
            ahead = (ahead + piece(offset)).astype(jnp.bfloat16)
            behind = (behind + piece(-offset)).astype(jnp.bfloat16)
    return ahead + behind + piece(0)


def core_swap(block):
    count = lax.axis_size("tensor")
    return lax.ppermute(block, "tensor", [(k, k ^ 1) for k in range(count)])


def chip_shift(block, step):
    count = lax.axis_size("tensor")
    return lax.ppermute(block, "tensor", [(k, (k + 2 * step) % count) for k in range(count)])


def tensor_parts(block):
    chips = lax.axis_size("tensor") // 2
    mate, *others = yield [core_swap(block)] + [chip_shift(block, k) for k in range(1, chips)]
    mates = yield [core_swap(other) for other in others]
    parts = [block, mate]
    for other, beside in zip(others, mates):
        parts += [other, beside]
    return parts


def in_order(parts):
    chips = len(parts) // 2
    mine = lax.axis_index("tensor")
    flipped = mine % 2 == 1
    pairs = []
    for chip in range(chips):
        first, second = (parts[2 * chip], parts[2 * chip + 1])
        pairs.append((jnp.where(flipped, second, first), jnp.where(flipped, first, second)))
    out = []
    for chip in range(chips):
        back = (mine // 2 + chips - chip) % chips
        for core in range(2):
            value = pairs[0][core]
            for step in range(1, chips):
                value = jnp.where(back == step, pairs[step][core], value)
            out.append(value)
    return out


def seq_gather(values):
    parts = yield from tensor_parts(values)
    return jnp.concatenate(parts, axis=0)


def tensor_scatter(pick):
    chips = lax.axis_size("tensor") // 2
    places = [2 * (chips - step) for step in range(1, chips)]
    mate, *others = yield [core_swap(pick(place + 1)) for place in [0] + places]
    merged = [
        (pick(place).astype(jnp.float32) + other.astype(jnp.float32)).astype(jnp.bfloat16)
        for place, other in zip(places, others)
    ]
    received = yield [chip_shift(value, k + 1) for k, value in enumerate(merged)]
    total = pick(0).astype(jnp.float32) + mate.astype(jnp.float32)
    for other in received:
        total = total + other.astype(jnp.float32)
    return total


def seq_reduce(lowered):
    rows = lowered.shape[0] // lax.axis_size("tensor")
    return tensor_scatter(lambda place: lowered[place * rows : (place + 1) * rows])


def width_total(values):
    chips = lax.axis_size("tensor") // 2
    blocks = values.reshape(chips, 2, -1)
    blocks = blocks + core_swap(blocks)[:, ::-1]
    total = blocks
    for step in range(1, chips):
        total = total + jnp.roll(chip_shift(blocks, step), step, axis=0)
    return total.reshape(values.shape)


def exchange(blocks, axes):
    return lax.all_to_all(blocks, axes, 0, 0, tiled=False)


def dp_scatter(values):
    blocks = values.astype(jnp.bfloat16).reshape((lax.axis_size("dp"), -1) + values.shape[1:])
    return jnp.sum(exchange(blocks, "dp").astype(jnp.float32), axis=0)


def run(chain):
    return lockstep(chain)[0]


def local(
    layer_input,
    out_grad,
    segment_ids,
    valid_mask,
    doc_start,
    norm_gains,
    conv_weight,
    conv_bias,
    mixer_gain,
    shared_proj,
    step_bias,
    decay_log,
    skip_gain,
    mamba_gate,
    mamba_input,
    mamba_step,
    query_proj,
    mamba_out,
    attention_out,
    swiglu_gate,
    swiglu_up,
    swiglu_down,
):
    tensor_position = lax.axis_index("tensor")
    dp_count = lax.axis_size("dp")
    tensor_count = lax.axis_size("tensor")
    device = lax.axis_index("dp") * tensor_count + tensor_position
    ring = Ring(dp_count)
    local_width = mamba_gate.shape[1]
    query_width = query_proj.shape[1]
    head_local = mamba_step.shape[1]
    hidden_width = swiglu_gate.shape[1]
    query_slice = query_width // HEAD_SIZE
    slab = 2 * HEAD_SIZE
    wide = -(-local_width // slab) * slab
    early_width = wide + slab
    block_rows = layer_input.shape[0]
    tokens_per_group = block_rows * tensor_count
    seq_count = tokens_per_group // SEQUENCE_TOKENS
    channel_start = tensor_position * local_width
    head_start = tensor_position * head_local
    channels = conv_weight.shape[1] * dp_count * tensor_count

    def padded(values, columns):
        return jnp.pad(values, ((0, 0), (0, columns - values.shape[1])))

    def placed(rows_in, columns, start):
        whole = jnp.zeros((rows_in.shape[0], columns), rows_in.dtype)
        return lax.dynamic_update_slice_in_dim(whole, rows_in, start, 1)

    device_count = dp_count * tensor_count
    rows_in = mamba_gate.shape[0]
    shared_rows = shared_proj.shape[0]
    small = jnp.concatenate(
        [norm_gains.reshape(-1), conv_weight.reshape(-1), conv_bias, mixer_gain]
    )
    small_width = -(-small.shape[0] // 128) * 128
    if small_width > shared_proj.shape[1]:
        raise ValueError("small parameters")
    small = jnp.pad(small, (0, shared_proj.shape[1] - small.shape[0]))
    small = jnp.pad(small[None], ((0, 7), (0, 0)))
    common = lax.all_gather(jnp.concatenate([shared_proj, small], axis=0), "tensor", axis=0)
    shared_own = common[:, :shared_rows].reshape(rows_in, -1)
    small_own = common[:, shared_rows, :small_width].reshape(1, -1)
    valid_f = valid_mask.astype(jnp.float32)
    out_cot = out_grad.astype(jnp.float32) * valid_f[:, None]
    layer_input, shared_own = together(layer_input, shared_own)
    block = pack(
        rows_in,
        (
            (mamba_gate, wide, False),
            (query_proj, slab, False),
            (mamba_out, local_width, True),
            (attention_out, query_width, True),
            (mamba_input, wide, False),
            (mamba_step, slab, False),
            (shared_own, shared_proj.shape[1], False),
        ),
    )
    extra = jnp.pad(small_own, ((0, 7), (0, block.shape[1] - small_own.shape[1])))

    def prepared():
        spots, gate, up, down = yield [doc_start, swiglu_gate, swiglu_up, swiglu_down]
        position = jnp.tile(jnp.arange(SEQUENCE_TOKENS, dtype=jnp.int32), seq_count) - spots
        ffn_block = pack(
            rows_in,
            ((gate, hidden_width, False), (up, hidden_width, False), (down, hidden_width, True)),
        )
        ffn_blocks = jnp.broadcast_to(ffn_block[None], (dp_count,) + ffn_block.shape)
        cosines, sines, ffn_blocks = yield [*rope_rows(position), ffn_blocks]
        return (ffn_blocks, cosines, sines)

    x_full, (w_in, small_all), ffn_grad_in, waited = lockstep(
        seq_gather(layer_input),
        ring_gather(ring, block, extra),
        after_stages(1, seq_gather(out_cot.astype(jnp.bfloat16))),
        prepared(),
    )
    ffn_blocks, cosine_table, sine_table = waited
    w_in, ffn_grad_in, ffn_blocks = together(w_in, ffn_grad_in, ffn_blocks)
    w_ffn = exchange(ffn_blocks, "dp").reshape(D, -1)
    shared_at = w_in.shape[1] - shared_proj.shape[1]
    late_at = early_width + local_width + query_width
    w_out = w_in[:, early_width:late_at]
    gains_f, conv_f, mixer_gain_f = unpack(
        small_all[:, 0],
        tensor_count,
        small_width,
        (
            (2, norm_gains.shape[1]),
            (CONV + 1, conv_weight.shape[1]),
            (1, mixer_gain.shape[0]),
        ),
    )
    tokens_f = layer_input.astype(jnp.float32)
    scale_one = rms_scale(tokens_f)
    first_full, early_act, late_act, common_act = project(
        x_full,
        gains_f,
        (
            (w_in, early_width, 0),
            (w_in, early_width, late_at),
            (w_in, shared_proj.shape[1], shared_at),
        ),
        block_rows,
    )
    taps = jnp.concatenate(
        [lax.dynamic_slice_in_dim(conv_f, channel_start, local_width, 1), conv_f[:, DSSM:]], axis=1
    )
    own_gain = lax.dynamic_slice_in_dim(mixer_gain_f[0], channel_start, local_width, 0)
    own_bias = lax.dynamic_slice_in_dim(step_bias, head_start, head_local, 0)
    own_decay = lax.dynamic_slice_in_dim(decay_log, head_start, head_local, 0)
    own_skip = lax.dynamic_slice_in_dim(skip_gain, head_start, head_local, 0)
    params = jnp.pad(
        jnp.stack([own_bias, -jnp.exp(own_decay)], axis=0), ((0, 6), (0, slab - head_local))
    )
    skip_row = jnp.broadcast_to(jnp.repeat(own_skip, HEAD_SIZE)[None], (8, local_width))
    doc = doc_start[:, None]
    kv = (tensor_position * query_slice // (QUERY_HEADS // KEY_VALUE_HEADS)).astype(jnp.int32)[None]
    device_ids = jnp.arange(tensor_count, dtype=jnp.int32)
    chip_count = tensor_count // 2
    block_order = (tensor_position // 2 + chip_count - device_ids // 2) % chip_count * 2 + (
        tensor_position + device_ids
    ) % 2

    mamba_y, square_rows, kept_states = mamba_forward(
        block_order, block_rows, early_act, late_act, common_act, doc, taps, params, skip_row
    )
    attended, query_rot, key_rot, value_low, log_total = attention_forward(
        kv, block_order, block_rows, early_act, common_act, cosine_table, sine_table, doc
    )
    square_sum = width_total(square_rows[0])
    gate_scale = lax.rsqrt(square_sum / DSSM + EPS)[:, None]
    gate_z = early_act[:, :local_width]
    sigmoid_z = jax.nn.sigmoid(gate_z)
    silu_z = gate_z * sigmoid_z
    gated_y = mamba_y * silu_z
    normed_b = (gated_y * gate_scale * own_gain).astype(jnp.bfloat16)
    mixed_b = jnp.concatenate([normed_b, attended[:, :query_width]], axis=1)
    mixer_sum = run(seq_reduce(product_nt(mixed_b, w_out).astype(jnp.bfloat16)))

    middle = tokens_f + mixer_sum
    scale_two = rms_scale(middle)
    second_b = (middle * scale_two * gains_f[1]).astype(jnp.bfloat16)
    ffn_in = run(seq_gather(second_b))
    gate_up_grad, hidden_b, second_part, ffn_part = feed_forward(
        ffn_in, ffn_grad_in, w_ffn, block_rows
    )
    ffn_in, ffn_grad_in, second_part = together(ffn_in, ffn_grad_in, second_part)
    second_grad = run(seq_reduce(second_part))
    ffn_w_grad = weight_grads(((ffn_in, gate_up_grad), (ffn_grad_in, hidden_b)))
    second_value_grad, gain_two_grad = norm_back(middle, scale_two, gains_f[1], second_grad)
    middle_grad = out_cot + second_value_grad
    middle_grad, ffn_w_grad = together(middle_grad, ffn_w_grad)

    gathered = seq_gather(middle_grad.astype(jnp.bfloat16))
    mate, *others = next(gathered)
    mate, ffn_w_grad = together(mate, ffn_w_grad)
    ffn_w_grad = dp_scatter(ffn_w_grad)
    mixer_grad_full = run(resumed(gathered, [mate, *others]))
    ffn_part, mixer_grad_full = together(ffn_part, mixer_grad_full)
    mixed_grad = product(mixer_grad_full, w_out)
    normed_grad = mixed_grad[:, :local_width]
    scaled_normed = normed_grad * own_gain
    inner_sum = width_total(jnp.sum(scaled_normed * gated_y, axis=1))
    attended_grad, attended_at = (mixed_grad, local_width // slab)
    if local_width % slab or query_width != slab:
        attended_grad, attended_at = (padded(mixed_grad[:, local_width:], slab), 0)
    dq, dkv = attention_backward(
        kv,
        block_order,
        block_rows,
        query_rot,
        key_rot,
        value_low,
        cosine_table,
        sine_table,
        doc,
        log_total,
        attended_grad,
        attended_at,
    )
    own_gain_grad = jnp.sum(normed_grad * gated_y * gate_scale, axis=0)
    gated_grad = (
        gate_scale * scaled_normed
        - gated_y * (gate_scale * gate_scale * gate_scale) * (inner_sum / DSSM)[:, None]
    )
    mamba_y_grad = gated_grad * silu_z
    gate_z_grad = (gated_grad * mamba_y * sigmoid_z * (1.0 + gate_z * (1.0 - sigmoid_z))).astype(
        jnp.bfloat16
    )
    early_grad = jnp.concatenate([padded(gate_z_grad, wide), dq], axis=1)
    early_w_grad, first_early, gain_one_early = weight_grads(
        ((mixer_grad_full, mixed_b), (first_full, early_grad)), (w_in, 0)
    )
    early_ring = ring_scatter(ring, early_w_grad)
    early_sent = next(early_ring)
    ffn_out = run(seq_reduce(ffn_part))
    mamba_y_grad, first_early = together(mamba_y_grad, first_early)
    late_grad, taps_grad, params_grad = mamba_backward(
        block_order,
        block_rows,
        late_act,
        common_act,
        doc,
        taps,
        params,
        skip_row,
        mamba_y,
        mamba_y_grad,
        dkv,
        kept_states,
    )

    late_grad, ffn_w_grad, *early_sent = together(late_grad, ffn_w_grad, *early_sent)
    gate_w_grad = ffn_w_grad[:, :hidden_width]
    up_w_grad = ffn_w_grad[:, hidden_width : 2 * hidden_width]
    down_w_grad = ffn_w_grad[:, 2 * hidden_width :].T
    early_sent = early_ring.send(early_sent)
    back = (w_in, late_at // late_grad.shape[1])
    if late_at % late_grad.shape[1]:
        back = (w_in[:, late_at:], 0)
    late_w_grad, first_part, gain_one_late = weight_grads(
        ((first_full, late_grad),), back, first_early
    )
    def summed(taps_grad, params_grad, gain_one_late, ffn_out):
        taps_grad, params_grad, gain_one_late, ffn_out = yield [
            taps_grad,
            params_grad,
            gain_one_late,
            ffn_out,
        ]
        result_b, stat_terms = finish(valid_f[:, None], layer_input, mixer_sum, middle, ffn_out)
        gain_one_grad = (gain_one_early + gain_one_late)[:, 0] / gains_f[0]
        heads = jnp.concatenate(
            [
                placed(params_grad[:3, :head_local], slab, head_start),
                padded(stat_terms[:6, 0][None], slab),
            ],
            axis=0,
        )
        conv_rows = jnp.concatenate(
            [
                placed(taps_grad[: CONV + 1, :local_width], DSSM, channel_start),
                taps_grad[: CONV + 1, local_width:],
            ],
            axis=1,
        )
        sums = gather_sums(
            device_count,
            (
                jnp.stack([gain_one_grad, gain_two_grad], axis=0),
                conv_rows,
                placed(own_gain_grad[None], DSSM, channel_start),
            ),
            ((2, norm_gains.shape[1]), (CONV + 1, conv_weight.shape[1]), (1, mixer_gain.shape[0])),
            heads,
            (MH, MH, MH, 6),
        )
        (sums,) = yield [sums]
        (got,) = yield [exchange(sums, ("dp", "tensor"))]
        outputs = spread_sums(
            got,
            (
                (2, norm_gains.shape[1]),
                (CONV, conv_weight.shape[1]),
                (1, conv_weight.shape[1]),
                (1, mixer_gain.shape[0]),
                (1, MH),
                (1, MH),
                (1, MH),
                (1, 6),
            ),
        )
        stats = outputs[-1][0]
        return (yield list(outputs[:-1]) + [jnp.sqrt(stats[:5] / (stats[5] * D)), result_b])

    def finished(part):
        first_grad = yield from seq_reduce(part)
        first_value_grad, _ = norm_back(tokens_f, scale_one, gains_f[0], first_grad)
        return (yield [middle_grad + first_value_grad])

    late_total, early_total, (input_grad,), outputs = lockstep(
        ring_scatter(ring, late_w_grad),
        resumed(early_ring, early_sent),
        after_stages(1, finished(first_part)),
        summed(taps_grad, params_grad, gain_one_late, ffn_out),
    )
    shared_total = late_total[:, early_width:].astype(jnp.bfloat16)
    places = [
        ((tensor_position // 2 + chip_count - place // 2) % chip_count) * 2
        + (tensor_position + place) % 2
        for place in range(tensor_count)
    ]
    shared_proj_grad = run(
        tensor_scatter(
            lambda place: lax.dynamic_slice_in_dim(
                shared_total, places[place] * shared_rows, shared_rows, 0
            )
        )
    )
    mamba_out_grad = early_total[:, :local_width].T
    attend_out_grad = early_total[:, local_width : local_width + query_width].T
    early_at = local_width + query_width
    gate_proj_grad = early_total[:, early_at : early_at + local_width]
    query_proj_grad = early_total[:, early_at + wide : early_at + wide + query_width]
    input_proj_grad = late_total[:, :local_width]
    step_proj_grad = late_total[:, wide : wide + head_local]
    gains_grad, conv_w_grad, conv_b_grad, gain_full_grad, bias_total, decay_total, skip_total, rms, result_b = outputs
    return (
        result_b,
        input_grad,
        gains_grad,
        conv_w_grad,
        conv_b_grad[0],
        gain_full_grad[0],
        shared_proj_grad,
        bias_total[0],
        decay_total[0],
        skip_total[0],
        gate_proj_grad,
        input_proj_grad,
        step_proj_grad,
        query_proj_grad,
        mamba_out_grad,
        attend_out_grad,
        gate_w_grad,
        up_w_grad,
        down_w_grad,
        rms,
    )


def solution(mesh):
    in_specs = (
        P(("dp", "tensor"), None),
        P(("dp", "tensor"), None),
        P("dp"),
        P(("dp", "tensor")),
        P("dp"),
        P(None, ("dp", "tensor")),
        P(None, ("dp", "tensor")),
        P(("dp", "tensor")),
        P(("dp", "tensor")),
        P(("dp", "tensor"), None),
        P(),
        P(),
        P(),
        P("dp", "tensor"),
        P("dp", "tensor"),
        P("dp", "tensor"),
        P("dp", "tensor"),
        P("tensor", "dp"),
        P("tensor", "dp"),
        P("dp", "tensor"),
        P("dp", "tensor"),
        P("tensor", "dp"),
    )
    out_specs = (
        P(("dp", "tensor"), None),
        P(("dp", "tensor"), None),
        P(None, ("dp", "tensor")),
        P(None, ("dp", "tensor")),
        P(("dp", "tensor")),
        P(("dp", "tensor")),
        P(("dp", "tensor"), None),
        P(),
        P(),
        P(),
        P("dp", "tensor"),
        P("dp", "tensor"),
        P("dp", "tensor"),
        P("dp", "tensor"),
        P("tensor", "dp"),
        P("tensor", "dp"),
        P("dp", "tensor"),
        P("dp", "tensor"),
        P("tensor", "dp"),
        P(),
    )
    return jax.shard_map(local, mesh=mesh, in_specs=in_specs, out_specs=out_specs, check_vma=False)
```

```python
import functools
import math

import jax
import jax.numpy as jnp
from jax import lax
from jax.experimental import pallas as pl
from jax.experimental.pallas import tpu as pltpu
from jax.sharding import PartitionSpec as P

D = 1024
MH = 24
HEAD_SIZE = 64
MAMBA_STATES = 128
CONV = 4
QUERY_HEADS = 8
KEY_VALUE_HEADS = 2
SEQUENCE_TOKENS = 1024
DSSM = 1536


EPS = 1e-05
ROPE_BASE = 100000000000.0
NEG_FILL = -1e30
HIGH = lax.Precision.HIGHEST


def rms_scale(values):
    return lax.rsqrt(jnp.mean(values * values, axis=-1, keepdims=True) + EPS)


def norm_back(values, row_scale, gain_row, grad_in):
    scaled_grad = grad_in * gain_row
    gain_grad = jnp.sum(grad_in * values * row_scale, axis=0)
    value_grad = row_scale * scaled_grad - values * (row_scale * row_scale * row_scale) * jnp.mean(
        scaled_grad * values, axis=-1, keepdims=True
    )
    return (value_grad, gain_grad)


def product(left, right):
    return jnp.dot(left, right, preferred_element_type=jnp.float32)


def product_tn(left, right):
    return lax.dot_general(
        left, right, (((0,), (0,)), ((), ())), preferred_element_type=jnp.float32
    )


def product_nt(left, right):
    return lax.dot_general(
        left, right, (((1,), (1,)), ((), ())), preferred_element_type=jnp.float32
    )


def split_dot(values, selector, dims):
    high = values.astype(jnp.bfloat16)
    low = (values - high.astype(jnp.float32)).astype(jnp.bfloat16)
    left = lax.dot_general(high, selector, dims, preferred_element_type=jnp.float32)
    return left + lax.dot_general(low, selector, dims, preferred_element_type=jnp.float32)


def estimate(flops, size):
    return pl.CostEstimate(flops=int(flops * 0.05), bytes_accessed=int(size * 0.05), transcendentals=0)


NN = (((1,), (0,)), ((), ()))
NT = (((1,), (1,)), ((), ()))
TN = (((0,), (0,)), ((), ()))


def mxu(left, right, dims):
    return lax.dot_general(
        left.astype(jnp.bfloat16),
        right.astype(jnp.bfloat16),
        dims,
        preferred_element_type=jnp.float32,
    )


def iota(shape, dim):
    return lax.broadcasted_iota(jnp.int32, shape, dim)


def head_groups(width):
    return [(low, min(low + 2 * HEAD_SIZE, width)) for low in range(0, width, 2 * HEAD_SIZE)]


def chunk_common(chunk, start, rows, width, raw_ref, doc_ref, pad_ref, w_ref, par_ref):
    doc = doc_ref[pl.ds(start, chunk), :]
    age = start + iota((chunk, 1), 0) - doc
    span = pad_ref[pl.ds(start, chunk + 8), :]
    conv = w_ref[CONV : CONV + 1, :] + w_ref[CONV - 1 : CONV, :] * span[8:, :]
    lagged = [span[8:, :]]
    for lag in range(1, CONV):
        moved = jnp.where(age >= lag, span[8 - lag : 8 - lag + chunk, :], 0.0)
        lagged.append(moved)
        conv = conv + w_ref[CONV - 1 - lag : CONV - lag, :] * moved
    sig = jax.nn.sigmoid(conv)
    act = conv * sig
    raw = raw_ref[rows, :] + par_ref[0:1, :]
    step = jnp.maximum(raw, 0.0) + jnp.log1p(jnp.exp(-jnp.abs(raw)))
    rate = step * par_ref[1:2, :]
    lower = (iota((chunk, chunk), 0) >= iota((chunk, chunk), 1)).astype(jnp.bfloat16)
    high = rate.astype(jnp.bfloat16)
    low = (rate - high.astype(jnp.float32)).astype(jnp.bfloat16)
    total = mxu(lower, high, NN) + mxu(lower, low, NN)
    lanes = par_ref.shape[1]
    spread = (iota((lanes, width), 0) == iota((lanes, width), 1) // HEAD_SIZE).astype(jnp.bfloat16)
    key_pos = start + iota((chunk, chunk), 1)
    allowed = (key_pos <= start + iota((chunk, chunk), 0)) & (key_pos >= doc)
    doc_last = doc[chunk - 1 : chunk, :]
    ends = total[chunk - 1 : chunk, :]
    live = jnp.where(doc < start, jnp.exp(total), 0.0)
    keep = jnp.where(start + iota((chunk, 1), 0) >= doc_last, jnp.exp(ends - total), 0.0)
    carry = jnp.where(doc_last < start, jnp.exp(ends), 0.0)
    wide = split_dot(jnp.concatenate([step, live, keep, jnp.broadcast_to(carry, (8, lanes))], axis=0), spread, NN)
    return dict(
        conv=conv, sig=sig, act=act, raw=raw, step=step, total=total, turned=total.T, spread=spread, allowed=allowed,
        carry=carry, age=age, lagged=lagged, lower=lower,
        step_w=wide[:chunk], live_w=wide[chunk : 2 * chunk], keep_w=wide[2 * chunk : 3 * chunk],
        carry_w=wide[3 * chunk : 3 * chunk + 1],
    )


def decay_of(part, head):
    gap = part["total"][:, head : head + 1] - part["turned"][head : head + 1, :]
    return jnp.where(part["allowed"], jnp.exp(gap), 0.0)


def only(values, low, high):
    lane = iota(values.shape, 1)
    return jnp.where((lane >= low) & (lane < high), values, jnp.zeros_like(values))


def place_of(order_ref, block_rows, length, start):
    token = pl.program_id(0) * length + start
    return pl.multiple_of(
        order_ref[token // block_rows] * block_rows + token % block_rows, 128
    )


def fill_conv_input(order_ref, block_rows, width, x_ref, bc_ref, pad_ref):
    length = pad_ref.shape[0] - 8
    pad_ref[0:8, :] = jnp.zeros((8, pad_ref.shape[1]), jnp.float32)
    for start in range(0, length, block_rows):
        rows = pl.ds(place_of(order_ref, block_rows, length, start), block_rows)
        pad_ref[8 + start : 8 + start + block_rows, :width] = x_ref[rows, :width]
        pad_ref[8 + start : 8 + start + block_rows, width:] = bc_ref[rows, :]


def mamba_forward_kernel(
    chunk, width, block_rows, order_ref, x_ref, bc_ref, raw_ref, z_ref, doc_ref, w_ref, par_ref, skip_ref, y_ref, square_ref, kept_ref, pad_ref, state_ref
):
    length = pad_ref.shape[0] - 8
    fill_conv_input(order_ref, block_rows, width, x_ref, bc_ref, pad_ref)
    state_ref[...] = jnp.zeros_like(state_ref)

    def one_chunk(index, _):
        start = pl.multiple_of(index * chunk, chunk)
        rows = pl.ds(place_of(order_ref, block_rows, length, start), chunk)
        part = chunk_common(chunk, start, rows, width, raw_ref, doc_ref, pad_ref, w_ref, par_ref)
        inner = part["act"][:, :width]
        bm = part["act"][:, width : width + MAMBA_STATES].astype(jnp.bfloat16)
        cm = part["act"][:, width + MAMBA_STATES :].astype(jnp.bfloat16)
        driven = (inner * part["step_w"]).astype(jnp.bfloat16)
        pair = mxu(cm, bm, NT)
        pieces = []
        for low, high in head_groups(width):
            heads = range(low // HEAD_SIZE, high // HEAD_SIZE)
            mats = [(decay_of(part, head) * pair).astype(jnp.bfloat16) for head in heads]
            piece = driven[:, low:high]
            right = [
                only(piece, HEAD_SIZE * k, HEAD_SIZE * (k + 1)) if len(mats) > 1 else piece
                for k in range(len(mats))
            ]
            pieces.append(
                mxu(jnp.concatenate(mats, axis=1), jnp.concatenate(right, axis=0), NN)
            )
        state = state_ref[...]
        kept_ref[pl.ds(pl.multiple_of(index * MAMBA_STATES, MAMBA_STATES), MAMBA_STATES), :] = state
        y = jnp.concatenate(pieces, axis=1) + part["live_w"] * mxu(cm, state, NN)
        y = y + skip_ref[0:1, :] * inner
        state_ref[...] = state * part["carry_w"] + mxu(
            bm, driven.astype(jnp.float32) * part["keep_w"], TN
        )
        y_ref[rows, :] = y
        z = z_ref[rows, :width]
        gated = y * z * jax.nn.sigmoid(z)
        square_ref[:, rows] = split_dot_left(gated * gated)
        return 0

    lax.fori_loop(0, length // chunk, one_chunk, 0)


def split_dot_left(values):
    ones = jnp.ones((8, values.shape[1]), jnp.bfloat16)
    high = values.astype(jnp.bfloat16)
    low = (values - high.astype(jnp.float32)).astype(jnp.bfloat16)
    return mxu(ones, high, NT) + mxu(ones, low, NT)


def mamba_backward_kernel(
    chunk, width, block_rows, order_ref, x_ref, bc_ref, raw_ref, doc_ref, w_ref, par_ref, skip_ref, y_ref, dy_ref,
    dkv_ref, kept_ref, din_ref, dw_ref, dpar_ref, pad_ref, state_ref, halo_ref, dskip_ref
):
    length = pad_ref.shape[0] - 8
    count = length // chunk
    wide = x_ref.shape[1]
    common_at = wide + 2 * HEAD_SIZE

    @pl.when(pl.program_id(0) == 0)
    def _():
        if wide > width:
            din_ref[...] = jnp.zeros_like(din_ref)
        din_ref[:, common_at + 2 * MAMBA_STATES :] = dkv_ref[...]

    fill_conv_input(order_ref, block_rows, width, x_ref, bc_ref, pad_ref)
    state_ref[...] = jnp.zeros_like(state_ref)
    halo_ref[...] = jnp.zeros_like(halo_ref)

    @pl.when(pl.program_id(0) == 0)
    def _():
        dw_ref[...] = jnp.zeros_like(dw_ref)
        dpar_ref[...] = jnp.zeros_like(dpar_ref)
        dskip_ref[...] = jnp.zeros_like(dskip_ref)

    def one_chunk(step_index, _):
        index = count - 1 - step_index
        start = pl.multiple_of(index * chunk, chunk)
        rows = pl.ds(place_of(order_ref, block_rows, length, start), chunk)
        part = chunk_common(chunk, start, rows, width, raw_ref, doc_ref, pad_ref, w_ref, par_ref)
        inner = part["act"][:, :width]
        bm = part["act"][:, width : width + MAMBA_STATES].astype(jnp.bfloat16)
        cm = part["act"][:, width + MAMBA_STATES :].astype(jnp.bfloat16)
        driven = (inner * part["step_w"]).astype(jnp.bfloat16)
        driven_f = driven.astype(jnp.float32)
        y = y_ref[rows, :]
        dy = dy_ref[rows, :]
        dy_b = dy.astype(jnp.bfloat16)
        pair = mxu(cm, bm, NT)
        pair_grad = jnp.zeros((chunk, chunk), jnp.float32)
        pieces = []
        for low, high in head_groups(width):
            heads = list(range(low // HEAD_SIZE, high // HEAD_SIZE))
            piece = driven[:, low:high]
            grads = [
                only(dy_b[:, low:high], HEAD_SIZE * k, HEAD_SIZE * (k + 1)) if len(heads) > 1 else dy_b[:, low:high]
                for k in range(len(heads))
            ]
            mats = []
            for k, head in enumerate(heads):
                decay = decay_of(part, head)
                mats.append((decay * pair).astype(jnp.bfloat16))
                pair_grad = pair_grad + decay * mxu(grads[k], piece, NT)
            pieces.append(mxu(jnp.concatenate(mats, axis=0), jnp.concatenate(grads, axis=0), TN))
        within = jnp.concatenate(pieces, axis=1)
        state = kept_ref[pl.ds(pl.multiple_of(index * MAMBA_STATES, MAMBA_STATES), MAMBA_STATES), :]
        state_grad = state_ref[...]
        pair_grad = pair_grad.astype(jnp.bfloat16)
        dy_live = (dy * part["live_w"]).astype(jnp.bfloat16)
        driven_keep = (driven_f * part["keep_w"]).astype(jnp.bfloat16)
        later = part["keep_w"] * mxu(bm, state_grad, NN)
        c_grad = mxu(pair_grad, bm, NN) + mxu(dy_live, state, NT)
        b_grad = mxu(pair_grad, cm, TN) + mxu(driven_keep, state_grad, NT)
        state_ref[...] = state_grad * part["carry_w"] + mxu(cm, dy_live, TN)
        driven_grad = within + later
        later_part = driven_f * later
        mixed = y - skip_ref[0:1, :] * inner
        sums = split_dot(
            jnp.concatenate(
                [
                    dy_b.astype(jnp.float32) * mixed - driven_f * within - later_part,
                    driven_grad * inner,
                    jnp.broadcast_to(
                        jnp.sum(later_part, axis=0, keepdims=True)
                        + part["carry_w"] * jnp.sum(state_grad * state, axis=0, keepdims=True),
                        (8, width),
                    ),
                ],
                axis=0,
            ),
            part["spread"],
            NT,
        )
        high = sums[:chunk].astype(jnp.bfloat16)
        low = (sums[:chunk] - high.astype(jnp.float32)).astype(jnp.bfloat16)
        rate_grad = (
            mxu(part["lower"], high, TN) + mxu(part["lower"], low, TN) + sums[2 * chunk : 2 * chunk + 1]
        )
        step_grad = rate_grad * par_ref[1:2, :] + sums[chunk : 2 * chunk]
        raw_grad = step_grad * jax.nn.sigmoid(part["raw"])
        din_ref[rows, wide:common_at] = raw_grad.astype(jnp.bfloat16)
        dpar_ref[0:1, :] += jnp.sum(raw_grad, axis=0, keepdims=True)
        dpar_ref[1:2, :] += par_ref[1:2, :] * jnp.sum(rate_grad * part["step"], axis=0, keepdims=True)
        dskip_ref[0:1, :] += jnp.sum(dy * inner, axis=0, keepdims=True)
        inner_grad = driven_grad * part["step_w"] + skip_ref[0:1, :] * dy
        sig, conv = (part["sig"], part["conv"])
        conv_grad = jnp.concatenate([inner_grad, b_grad, c_grad], axis=1) * (
            sig * (1.0 + conv * (1.0 - sig))
        )
        dw_ref[CONV : CONV + 1, :] += jnp.sum(conv_grad, axis=0, keepdims=True)
        v_grad = w_ref[CONV - 1 : CONV, :] * conv_grad
        long = jnp.concatenate([conv_grad, halo_ref[...]], axis=0)
        next_start = jnp.minimum(start + chunk, length - 8)
        ages = jnp.concatenate([part["age"], start + chunk + iota((8, 1), 0) - doc_ref[pl.ds(pl.multiple_of(next_start, 8), 8), :]], axis=0)
        dw_ref[CONV - 1 : CONV, :] += jnp.sum(conv_grad * part["lagged"][0], axis=0, keepdims=True)
        for lag in range(1, CONV):
            dw_ref[CONV - 1 - lag : CONV - lag, :] += jnp.sum(
                conv_grad * part["lagged"][lag], axis=0, keepdims=True
            )
            masked = jnp.where(ages >= lag, long, 0.0)
            v_grad = v_grad + w_ref[CONV - 1 - lag : CONV - lag, :] * masked[lag : lag + chunk, :]
        halo_ref[...] = conv_grad[:8, :]
        din_ref[rows, :width] = v_grad[:, :width].astype(jnp.bfloat16)
        din_ref[rows, common_at : common_at + 2 * MAMBA_STATES] = v_grad[:, width:].astype(jnp.bfloat16)
        return 0

    lax.fori_loop(0, count, one_chunk, 0)

    @pl.when(pl.program_id(0) == pl.num_programs(0) - 1)
    def _():
        lanes = dpar_ref.shape[1]
        spread = (iota((lanes, width), 0) == iota((lanes, width), 1) // HEAD_SIZE).astype(jnp.bfloat16)
        dpar_ref[2:3, :] = split_dot(dskip_ref[...], spread, NT)[0:1]


CHUNK = 256
VMEM_LIMIT = 60 * 1024 * 1024


def tokens_spec(tokens, width, place=0):
    return pl.BlockSpec((tokens, width), lambda i, *_: (0, place))


def whole_spec(shape):
    return pl.BlockSpec(shape, lambda i, *_: (0,) * len(shape))


def mamba_forward(order, block_rows, early, late, common, doc, taps, params, skip_row, chunk=CHUNK):
    tokens = late.shape[0]
    width = skip_row.shape[1]
    lanes = params.shape[1]
    wide = late.shape[1] - lanes
    seq = SEQUENCE_TOKENS
    count = tokens // seq
    kept = seq // chunk * MAMBA_STATES
    return pl.pallas_call(
        functools.partial(mamba_forward_kernel, chunk, width, block_rows),
        grid_spec=pltpu.PrefetchScalarGridSpec(
        num_scalar_prefetch=1,
        grid=(count,),
        in_specs=[
            tokens_spec(tokens, wide),
            tokens_spec(tokens, 2 * MAMBA_STATES),
            tokens_spec(tokens, lanes, wide // lanes),
            tokens_spec(tokens, wide),
            pl.BlockSpec((seq, 1), lambda i, *_: (i, 0)),
            whole_spec(taps.shape),
            whole_spec(params.shape),
            whole_spec(skip_row.shape),
        ],
        out_specs=[
            tokens_spec(tokens, width),
            whole_spec((8, tokens)),
            pl.BlockSpec((kept, width), lambda i, *_: (i, 0)),
        ],
        scratch_shapes=[
            pltpu.VMEM((seq + 8, width + 2 * MAMBA_STATES), jnp.float32),
            pltpu.VMEM((MAMBA_STATES, width), jnp.float32),
        ],
        ),
        out_shape=[
            jax.ShapeDtypeStruct((tokens, width), jnp.float32),
            jax.ShapeDtypeStruct((8, tokens), jnp.float32),
            jax.ShapeDtypeStruct((count * kept, width), jnp.float32),
        ],
        compiler_params=pltpu.CompilerParams(vmem_limit_bytes=VMEM_LIMIT),
        cost_estimate=estimate(tokens * width * 20000, tokens * width * 20),
    )(order, late, common, late, early, doc, taps, params, skip_row)


def mamba_backward(
    order, block_rows, late, common, doc, taps, params, skip_row, y, dy, dkv, kept_states, chunk=CHUNK
):
    tokens = late.shape[0]
    width = skip_row.shape[1]
    lanes = params.shape[1]
    wide = late.shape[1] - lanes
    seq = SEQUENCE_TOKENS
    count = tokens // seq
    kept = seq // chunk * MAMBA_STATES
    conv_width = width + 2 * MAMBA_STATES
    return pl.pallas_call(
        functools.partial(mamba_backward_kernel, chunk, width, block_rows),
        grid_spec=pltpu.PrefetchScalarGridSpec(
        num_scalar_prefetch=1,
        grid=(count,),
        in_specs=[
            tokens_spec(tokens, wide),
            tokens_spec(tokens, 2 * MAMBA_STATES),
            tokens_spec(tokens, lanes, wide // lanes),
            pl.BlockSpec((seq, 1), lambda i, *_: (i, 0)),
            whole_spec(taps.shape),
            whole_spec(params.shape),
            whole_spec(skip_row.shape),
            tokens_spec(tokens, width),
            tokens_spec(tokens, width),
            tokens_spec(tokens, dkv.shape[1]),
            pl.BlockSpec((kept, width), lambda i, *_: (i, 0)),
        ],
        out_specs=[
            tokens_spec(tokens, late.shape[1] + common.shape[1]),
            whole_spec((8, conv_width)),
            whole_spec((8, lanes)),
        ],
        scratch_shapes=[
            pltpu.VMEM((seq + 8, conv_width), jnp.float32),
            pltpu.VMEM((MAMBA_STATES, width), jnp.float32),
            pltpu.VMEM((8, conv_width), jnp.float32),
            pltpu.VMEM((8, width), jnp.float32),
        ],
        ),
        out_shape=[
            jax.ShapeDtypeStruct((tokens, late.shape[1] + common.shape[1]), jnp.bfloat16),
            jax.ShapeDtypeStruct((8, conv_width), jnp.float32),
            jax.ShapeDtypeStruct((8, lanes), jnp.float32),
        ],
        compiler_params=pltpu.CompilerParams(vmem_limit_bytes=VMEM_LIMIT),
        cost_estimate=estimate(tokens * width * 60000, tokens * width * 20),
    )(
        order, late, common, late, doc, taps, params, skip_row, y, dy, dkv, kept_states
    )


NEGATIVE = -1e30
QUERY_BLOCK = 256


def swap_halves(values):
    half = HEAD_SIZE // 2
    lane = iota(values.shape, 1)
    width = values.shape[1]
    return jnp.where(
        lane % HEAD_SIZE < half,
        pltpu.roll(values, width - half, 1),
        pltpu.roll(values, half, 1),
    )


def attention_mask(start, rows, keys, doc):
    position = start + iota((rows, 1), 0)
    key_pos = iota((rows, keys), 1)
    return (key_pos <= position) & (key_pos >= doc)


def both_heads(values):
    return jnp.concatenate(
        [only(values, 0, HEAD_SIZE), only(values, HEAD_SIZE, 2 * HEAD_SIZE)], axis=0
    )


def chosen(values, kv):
    lane = iota(values.shape, 1)
    turned = pltpu.roll(values, HEAD_SIZE, 1)
    return jnp.where((lane < HEAD_SIZE) == (kv == 0), values, turned)


def attention_forward_kernel(
    block_rows, kv_ref, order_ref, q_ref, key_ref, value_ref, cos_ref, sin_ref, doc_ref, out_ref, qr_ref, kr_ref, vr_ref, log_ref
):
    length = qr_ref.shape[0]
    kv = kv_ref[0]
    rows = block_rows
    for start in range(0, length, rows):
        block = slice(start, start + rows)
        place = pl.ds(place_of(order_ref, block_rows, length, start), rows)
        cos, sin = (cos_ref[block, :], sin_ref[block, :])
        query, key = (q_ref[place, :], key_ref[place, :])
        turned = (query * cos + swap_halves(query) * sin).astype(jnp.bfloat16)
        qr_ref[block, :] = (turned.astype(jnp.float32) * HEAD_SIZE**-0.5).astype(jnp.bfloat16)
        kr_ref[block, :] = chosen(key * cos + swap_halves(key) * sin, kv).astype(jnp.bfloat16)
        vr_ref[block, :] = chosen(value_ref[place, :], kv).astype(jnp.bfloat16)
        keys = start + rows
        mask = attention_mask(start, rows, keys, doc_ref[block, :])
        scores = mxu(both_heads(qr_ref[block, :]), kr_ref[0:keys, :], NT)
        outs = []
        logs = []
        for head in range(2):
            part = jnp.where(mask, scores[head * rows : (head + 1) * rows], NEGATIVE)
            peak = jnp.max(part, axis=1, keepdims=True)
            weight = jnp.exp(part - peak)
            total = jnp.sum(weight, axis=1, keepdims=True)
            outs.append(mxu(weight * (1.0 / total), vr_ref[0:keys, :], NN))
            logs.append(peak + jnp.log(total))
        lane = iota((rows, 2 * HEAD_SIZE), 1)
        out_ref[place, :] = jnp.where(lane < HEAD_SIZE, outs[0], outs[1]).astype(jnp.bfloat16)
        log_ref[block, :] = jnp.where(lane < HEAD_SIZE, logs[0], logs[1])


def attention_backward_kernel(
    block_rows, kv_ref, order_ref, qr_ref, kr_ref, vr_ref, cos_ref, sin_ref, doc_ref, log_ref, grad_ref, dq_ref, dkv_ref, dk_ref, dv_ref
):
    length = qr_ref.shape[0]
    kv = kv_ref[0]
    rows = block_rows
    lane = iota((rows, 2 * HEAD_SIZE), 1)
    mine = (lane < HEAD_SIZE) == (kv == 0)
    dk_ref[...] = jnp.zeros_like(dk_ref)
    dv_ref[...] = jnp.zeros_like(dv_ref)
    for start in reversed(range(0, length, rows)):
        keys = start + rows
        block = slice(start, start + rows)
        place = pl.ds(place_of(order_ref, block_rows, length, start), rows)
        mask = attention_mask(start, rows, keys, doc_ref[block, :])
        query = both_heads(qr_ref[block, :])
        grad = both_heads(grad_ref[place, :].astype(jnp.bfloat16))
        logs = log_ref[block, :]
        scores = mxu(query, kr_ref[0:keys, :], NT)
        prob_grad = mxu(grad, vr_ref[0:keys, :], NT)
        probs = []
        score_grads = []
        for head in range(2):
            part = slice(head * rows, (head + 1) * rows)
            log = logs[:, head * HEAD_SIZE : head * HEAD_SIZE + 1]
            weight = jnp.where(mask, jnp.exp(scores[part] - log), 0.0)
            product_grad = weight * prob_grad[part]
            total = jnp.sum(product_grad, axis=1, keepdims=True)
            probs.append(weight.astype(jnp.bfloat16))
            score_grads.append((product_grad - weight * total).astype(jnp.bfloat16))
        cos, sin = (cos_ref[block, :], sin_ref[block, :])
        dq = mxu(jnp.concatenate(score_grads, axis=0), kr_ref[0:keys, :], NN)
        dq = jnp.where(lane < HEAD_SIZE, dq[:rows], dq[rows:]) * HEAD_SIZE**-0.5
        dq = dq * cos - swap_halves(dq) * sin
        dq_ref[place, :] = dq.astype(jnp.bfloat16)
        dk_ref[0:keys, :] += mxu(jnp.concatenate(score_grads, axis=0), query, TN)
        dv_ref[0:keys, :] += mxu(jnp.concatenate(probs, axis=0), grad, TN)
        dk = dk_ref[block, :]
        dk = dk + pltpu.roll(dk, HEAD_SIZE, 1)
        dk = dk * cos - swap_halves(dk) * sin
        dv = dv_ref[block, :]
        dv = dv + pltpu.roll(dv, HEAD_SIZE, 1)
        dkv_ref[place, : 2 * HEAD_SIZE] = jnp.where(mine, dk, 0.0).astype(jnp.bfloat16)
        dkv_ref[place, 2 * HEAD_SIZE :] = jnp.where(mine, dv, 0.0).astype(jnp.bfloat16)


def attention_call(kernel, kv, order, block_rows, tokens, ins, outs, scratch, flops):
    seq = SEQUENCE_TOKENS

    def spec(columns, place):
        if place is None:
            return pl.BlockSpec((seq, columns), lambda i, *_: (i, 0))
        return tokens_spec(tokens, columns, place)

    return pl.pallas_call(
        functools.partial(kernel, block_rows),
        grid_spec=pltpu.PrefetchScalarGridSpec(
            num_scalar_prefetch=2,
            grid=(tokens // seq,),
            in_specs=[spec(columns, place) for _, columns, place in ins],
            out_specs=[spec(columns, place) for _, columns, place in outs],
            scratch_shapes=scratch,
        ),
        out_shape=[jax.ShapeDtypeStruct((tokens, columns), kind) for kind, columns, _ in outs],
        compiler_params=pltpu.CompilerParams(vmem_limit_bytes=VMEM_LIMIT),
        cost_estimate=estimate(flops * tokens, tokens * 4096),
    )(kv, order, *[value for value, _, _ in ins])


def attention_forward(kv, order, block_rows, early, common, cos, sin, doc):
    two = 2 * HEAD_SIZE
    low, full = (jnp.bfloat16, jnp.float32)
    query_at = early.shape[1] // two - 1
    key_at = 2 * MAMBA_STATES // two
    return attention_call(
        attention_forward_kernel,
        kv,
        order,
        block_rows,
        early.shape[0],
        (
            (early, two, query_at),
            (common, two, key_at),
            (common, two, key_at + 1),
            (cos, two, None),
            (sin, two, None),
            (doc, 1, None),
        ),
        ((low, two, 0), (low, two, None), (low, two, None), (low, two, None), (full, two, None)),
        [],
        4000000,
    )


def attention_backward(kv, order, block_rows, qr, kr, vr, cos, sin, doc, log, grad, grad_at):
    two = 2 * HEAD_SIZE
    seq = SEQUENCE_TOKENS
    return attention_call(
        attention_backward_kernel,
        kv,
        order,
        block_rows,
        qr.shape[0],
        (
            (qr, two, None),
            (kr, two, None),
            (vr, two, None),
            (cos, two, None),
            (sin, two, None),
            (doc, 1, None),
            (log, two, None),
            (grad, two, grad_at),
        ),
        ((jnp.bfloat16, two, 0), (jnp.bfloat16, 2 * two, 0)),
        [pltpu.VMEM((seq, two), jnp.float32), pltpu.VMEM((seq, two), jnp.float32)],
        9000000,
    )


def pack_kernel(rows, widths, turned, *refs):
    spot = 0
    out_ref = refs[-1]
    if out_ref.shape[0] > rows:
        extra_ref = refs[-2]
        out_ref[rows:, :] = jnp.zeros((out_ref.shape[0] - rows, out_ref.shape[1]), out_ref.dtype)
        out_ref[rows:, : extra_ref.shape[1]] = extra_ref[...]
    for ref, width, turn in zip(refs, widths, turned):
        value = ref[...].T if turn else ref[...]
        have = value.shape[1]
        out_ref[:rows, spot : spot + have] = value
        if width > have:
            out_ref[:rows, spot + have : spot + width] = jnp.zeros(
                (value.shape[0], width - have), value.dtype
            )
        spot += width


def pack(rows, pieces, extra=None):
    widths = [width for _, width, _ in pieces]
    turned = [turn for _, _, turn in pieces]
    arrays = [value for value, _, _ in pieces]
    size = rows * sum(widths)
    below = 0
    if extra is not None:
        arrays.append(extra)
        below = extra.shape[0]
    return pl.pallas_call(
        functools.partial(pack_kernel, rows, widths, turned),
        out_shape=jax.ShapeDtypeStruct((rows + below, sum(widths)), arrays[0].dtype),
        compiler_params=pltpu.CompilerParams(vmem_limit_bytes=VMEM_LIMIT),
        cost_estimate=estimate(size, 4 * size),
    )(*arrays)


def unpack_kernel(groups, size, pieces, small_ref, *out_refs):
    spot = 0
    for out_ref, (rows, width) in zip(out_refs, pieces):
        total = out_ref.shape[1]
        column = iota((width, total), 1)
        owner = iota((small_ref.shape[0], total), 1) // (width * groups)
        mine = owner == iota((small_ref.shape[0], total), 0)
        for row in range(rows):
            found = jnp.zeros((small_ref.shape[0], total), jnp.float32)
            for group in range(groups):
                pick = (column % width == iota((width, total), 0)) & (
                    column // width % groups == group
                )
                start = group * size + spot
                found = found + mxu(
                    small_ref[:, start : start + width], pick.astype(jnp.bfloat16), NN
                )
            out_ref[row : row + 1, :] = jnp.sum(
                jnp.where(mine, found, 0.0), axis=0, keepdims=True
            )
            spot += width
        if rows < out_ref.shape[0]:
            out_ref[rows:, :] = jnp.zeros((out_ref.shape[0] - rows, total), jnp.float32)


def unpack(small, groups, size, pieces):
    count = small.shape[0] * groups
    return pl.pallas_call(
        functools.partial(unpack_kernel, groups, size, pieces),
        out_shape=[
            jax.ShapeDtypeStruct((8, count * width), jnp.float32) for _, width in pieces
        ],
        compiler_params=pltpu.CompilerParams(vmem_limit_bytes=VMEM_LIMIT),
        cost_estimate=estimate(1 << 26, 1 << 18),
    )(small)


def project_kernel(count, x_ref, gain_ref, *refs):
    x = x_ref[...].astype(jnp.float32)
    scale = lax.rsqrt(jnp.mean(x * x, axis=1, keepdims=True) + EPS)
    first = (x * scale * gain_ref[0:1, :]).astype(jnp.bfloat16)
    refs[count][...] = first
    for w_ref, out_ref in zip(refs[:count], refs[count + 1 :]):
        out_ref[...] = mxu(first, w_ref[...], NN)


def project(x, gains, weights, rows):
    tokens, width = x.shape
    arrays, specs = ([], [])
    for array, columns, start in weights:
        if start % columns:
            array, start = (array[:, start : start + columns], 0)
        arrays.append(array)
        specs.append(
            pl.BlockSpec(
                (width, columns), functools.partial(lambda place, i: (0, place), start // columns)
            )
        )
    by_rows = lambda columns: pl.BlockSpec((rows, columns), lambda i: (i, 0))
    total = sum(columns for _, columns, _ in weights)
    return pl.pallas_call(
        functools.partial(project_kernel, len(weights)),
        grid=(tokens // rows,),
        in_specs=[by_rows(width), pl.BlockSpec(gains.shape, lambda i: (0, 0))] + specs,
        out_specs=[by_rows(width)] + [by_rows(columns) for _, columns, _ in weights],
        out_shape=[jax.ShapeDtypeStruct((tokens, width), jnp.bfloat16)]
        + [jax.ShapeDtypeStruct((tokens, columns), jnp.float32) for _, columns, _ in weights],
        compiler_params=pltpu.CompilerParams(vmem_limit_bytes=VMEM_LIMIT),
        cost_estimate=estimate(2 * tokens * width * total, 2 * width * total + 4 * tokens * (width + total)),
    )(x, gains, *arrays)


def gather_kernel(pieces, extra, *refs):
    out_ref = refs[-1]
    count = out_ref.shape[0]
    out_ref[...] = jnp.zeros_like(out_ref)
    spot = 0
    for ref, (rows, width) in zip(refs, pieces):
        total = ref.shape[1]
        pick = (iota((total, width), 0) % width == iota((total, width), 1)).astype(jnp.bfloat16)
        mine = iota((count, total), 1) // width == iota((count, total), 0)
        for row in range(rows):
            rest = jnp.where(mine, ref[row : row + 1, :], 0.0)
            found = jnp.zeros((count, width), jnp.float32)
            for _ in range(3):
                low = rest.astype(jnp.bfloat16)
                found = found + mxu(low, pick, NN)
                rest = rest - low.astype(jnp.float32)
            out_ref[:, spot : spot + width] = found
            spot += width
    for row in range(refs[-2].shape[0]):
        width = extra[row]
        out_ref[:, spot : spot + width] = jnp.broadcast_to(
            refs[-2][row : row + 1, :width], (count, width)
        )
        spot += width


def gather_sums(count, arrays, pieces, everywhere, extra):
    columns = sum(rows * width for rows, width in pieces) + sum(extra)
    columns = -(-columns // 128) * 128
    return pl.pallas_call(
        functools.partial(gather_kernel, pieces, extra),
        out_shape=jax.ShapeDtypeStruct((count, columns), jnp.float32),
        compiler_params=pltpu.CompilerParams(vmem_limit_bytes=VMEM_LIMIT),
        cost_estimate=estimate(1 << 26, 1 << 18),
    )(*arrays, everywhere)


def spread_kernel(shapes, got_ref, *out_refs):
    sums = jnp.sum(got_ref[...], axis=0, keepdims=True)
    spot = 0
    for out_ref, (rows, width) in zip(out_refs, shapes):
        for row in range(rows):
            out_ref[row : row + 1, :] = sums[:, spot : spot + width]
            spot += width


def spread_sums(got, shapes):
    return pl.pallas_call(
        functools.partial(spread_kernel, shapes),
        out_shape=[jax.ShapeDtypeStruct(shape, jnp.float32) for shape in shapes],
        compiler_params=pltpu.CompilerParams(vmem_limit_bytes=VMEM_LIMIT),
        cost_estimate=estimate(1 << 16, 1 << 17),
    )(got)


def weight_grad_kernel(count, with_back, *refs):
    lefts, rights = (refs[:count], refs[count : 2 * count])
    rest = refs[2 * count :]
    out_ref = rest[-3] if with_back else rest[-1]
    spot = 0
    for left, right in zip(lefts, rights):
        grad = mxu(left[...], right[...], TN)
        columns = right.shape[1]
        out_ref[:, spot : spot + columns] = grad.astype(jnp.bfloat16)
        spot += columns
    if with_back:
        w_ref = rest[0]
        part = mxu(rights[-1][...], w_ref[...], NT)
        if len(rest) > 4:
            part = part + rest[1][...].astype(jnp.float32)
        rest[-2][...] = part.astype(rest[-2].dtype)
        rest[-1][...] = jnp.sum(grad * w_ref[...].astype(jnp.float32), axis=1, keepdims=True)


def weight_grads(pairs, back=None, base=None, kind=jnp.bfloat16):
    tokens, rows = pairs[0][0].shape
    total = sum(right.shape[1] for _, right in pairs)
    block = min(rows, 512)
    ins = [left for left, _ in pairs] + [right for _, right in pairs]
    specs = [pl.BlockSpec((tokens, block), lambda i: (0, i)) for _ in pairs]
    specs += [pl.BlockSpec((tokens, right.shape[1]), lambda i: (0, 0)) for _, right in pairs]
    outs = [jax.ShapeDtypeStruct((rows, total), jnp.bfloat16)]
    out_specs = [pl.BlockSpec((block, total), lambda i: (i, 0))]
    flops = 2 * tokens * rows * total
    if back is not None:
        weight, place = back
        ins.append(weight)
        specs.append(pl.BlockSpec((block, pairs[-1][1].shape[1]), lambda i: (i, place)))
        if base is not None:
            ins.append(base)
            specs.append(pl.BlockSpec((tokens, block), lambda i: (0, i)))
        outs += [
            jax.ShapeDtypeStruct((tokens, rows), kind),
            jax.ShapeDtypeStruct((rows, 1), jnp.float32),
        ]
        out_specs += [
            pl.BlockSpec((tokens, block), lambda i: (0, i)),
            pl.BlockSpec((block, 1), lambda i: (i, 0)),
        ]
        flops += 2 * tokens * rows * pairs[-1][1].shape[1]
    result = pl.pallas_call(
        functools.partial(weight_grad_kernel, len(pairs), back is not None),
        grid=(rows // block,),
        in_specs=specs,
        out_specs=out_specs,
        out_shape=outs,
        compiler_params=pltpu.CompilerParams(vmem_limit_bytes=VMEM_LIMIT),
        cost_estimate=estimate(flops, 4 * tokens * rows + 2 * rows * total),
    )(*ins)
    return result if back is not None else result[0]


def feed_forward_kernel(hidden_width, x_ref, cot_ref, w_ref, grad_ref, hidden_ref, back_ref, out_ref):
    wide = 2 * hidden_width
    acts = mxu(x_ref[...], w_ref[:, :wide], NN)
    hidden_grad = mxu(cot_ref[...], w_ref[:, wide:], NN)
    gate, up = (acts[:, :hidden_width], acts[:, hidden_width:])
    sig = jax.nn.sigmoid(gate)
    silu = gate * sig
    grads = jnp.concatenate(
        [hidden_grad * up * (sig * (1.0 + gate * (1.0 - sig))), hidden_grad * silu], axis=1
    ).astype(jnp.bfloat16)
    grad_ref[...] = grads
    back_ref[...] = mxu(grads, w_ref[:, :wide], NT).astype(jnp.bfloat16)
    hidden = (silu * up).astype(jnp.bfloat16)
    hidden_ref[...] = hidden
    out_ref[...] = mxu(hidden, w_ref[:, wide:], NT).astype(jnp.bfloat16)


def feed_forward(x, cot, weights, rows):
    tokens, width = x.shape
    hidden_width = weights.shape[1] // 3
    by_rows = lambda columns: pl.BlockSpec((rows, columns), lambda i: (i, 0))
    sizes = (2 * hidden_width, hidden_width, width, width)
    return pl.pallas_call(
        functools.partial(feed_forward_kernel, hidden_width),
        grid=(tokens // rows,),
        in_specs=[by_rows(width), by_rows(width), pl.BlockSpec(weights.shape, lambda i: (0, 0))],
        out_specs=[by_rows(columns) for columns in sizes],
        out_shape=[jax.ShapeDtypeStruct((tokens, columns), jnp.bfloat16) for columns in sizes],
        compiler_params=pltpu.CompilerParams(vmem_limit_bytes=VMEM_LIMIT),
        cost_estimate=estimate(12 * tokens * width * hidden_width, 14 * tokens * width),
    )(x, cot, weights)


def finish_kernel(valid_ref, x_ref, mixer_ref, middle_ref, ffn_ref, out_ref, stat_ref):
    valid = valid_ref[...]
    middle, ffn = (middle_ref[...], ffn_ref[...])
    result = middle + ffn
    out_ref[...] = result.astype(jnp.bfloat16)
    tracked = (x_ref[...].astype(jnp.float32), mixer_ref[...], middle, ffn, result)
    stat_ref[...] = jnp.zeros_like(stat_ref)
    for k, values in enumerate(tracked):
        stat_ref[k : k + 1, 0:1] = jnp.sum(
            valid * jnp.sum(values * values, axis=1, keepdims=True), axis=0, keepdims=True
        )
    stat_ref[len(tracked) : len(tracked) + 1, 0:1] = jnp.sum(valid, axis=0, keepdims=True)


def finish(valid, x, mixer_sum, middle, ffn_out):
    return pl.pallas_call(
        finish_kernel,
        out_shape=[
            jax.ShapeDtypeStruct(x.shape, jnp.bfloat16),
            jax.ShapeDtypeStruct((8, 128), jnp.float32),
        ],
        compiler_params=pltpu.CompilerParams(vmem_limit_bytes=VMEM_LIMIT),
        cost_estimate=estimate(16 * x.size, 16 * x.size),
    )(valid, x, mixer_sum, middle, ffn_out)


def resumed(chain, sent):
    while True:
        got = yield sent
        try:
            sent = chain.send(got)
        except StopIteration as stop:
            return stop.value


def passengers(stages, *values):
    for _ in range(stages):
        yield []
    return (yield list(values))


def rope_rows(position):
    lane = jnp.arange(2 * HEAD_SIZE, dtype=jnp.int32)
    half = HEAD_SIZE // 2
    inverse = jnp.exp(
        (lane % half).astype(jnp.float32) * (-2.0 * math.log(ROPE_BASE) / HEAD_SIZE)
    )
    angles = position.astype(jnp.float32)[:, None] * inverse[None, :]
    sign = jnp.where(lane % HEAD_SIZE < half, -1.0, 1.0)
    return (jnp.cos(angles), jnp.sin(angles) * sign[None, :])
def grid_of(count):
    rows = 1
    while 8 * rows * rows <= count:
        rows *= 2
    return (count // rows, rows)


def ring_cycle(count):
    depth, rows = grid_of(count)
    order = []
    for level in range(depth):
        inner = list(range(1, rows))
        if level % 2:
            inner.reverse()
        order += [level * rows + row for row in inner]
    return order + [level * rows for level in reversed(range(depth))]


class Ring:
    def __init__(self, count):
        self.count = count
        self.order = ring_cycle(count)
        self.depth, self.rows = grid_of(count)
        inner = self.rows - 1
        mine = lax.axis_index("dp")
        level, row = (mine // self.rows, mine % self.rows)
        step = jnp.where(level % 2 == 0, row - 1, inner - row)
        self.spot = jnp.where(
            row > 0, level * inner + step, self.depth * inner + self.depth - 1 - level
        )

    def device_at(self, offset):
        inner = self.rows - 1
        spot = (self.spot + offset + self.count) % self.count
        level, step = (spot // inner, spot % inner)
        row = jnp.where(level % 2 == 0, step + 1, inner - step)
        back = self.count - 1 - spot
        return jnp.where(spot < self.depth * inner, level * self.rows + row, back * self.rows)

    def send(self, block, step):
        count, order = (self.count, self.order)
        return lax.ppermute(
            block, "dp", [(order[k], order[(k + step) % count]) for k in range(count)]
        )


def together(*values):
    return lax.optimization_barrier(values)


def lockstep(*chains):
    results = [None] * len(chains)
    waiting = {k: None for k in range(len(chains))}
    while waiting:
        sent = {}
        for k in list(waiting):
            try:
                sent[k] = chains[k].send(waiting[k])
            except StopIteration as stop:
                results[k] = stop.value
                del waiting[k]
        flat = [value for k in sent for value in sent[k]]
        if len(flat) > 1:
            flat = list(together(*flat))
        for k in sent:
            waiting[k] = flat[: len(sent[k])]
            flat = flat[len(sent[k]) :]
    return results


def after_stages(count, chain):
    for _ in range(count):
        yield []
    return (yield from chain)


def ring_gather(ring, whole, rows):
    count = ring.count
    half = rows // 2
    out = jnp.zeros((count * rows, whole.shape[1]), whole.dtype)
    more = jnp.zeros((count, whole.shape[0] - rows, whole.shape[1]), whole.dtype)

    def put(arrays, piece, offset, start=0):
        out, more = arrays
        device = ring.device_at(offset)
        kept = min(piece.shape[0], rows - start)
        out = lax.dynamic_update_slice_in_dim(out, piece[:kept], device * rows + start, 0)
        if piece.shape[0] > kept:
            more = lax.dynamic_update_index_in_dim(more, piece[kept:], device, 0)
        return (out, more)

    arrays = put((out, more), whole, 0)
    ahead = behind = whole
    for step in range(1, count // 2):
        ahead, behind = yield [ring.send(ahead, 1), ring.send(behind, -1)]
        arrays = put(arrays, ahead, -step)
        arrays = put(arrays, behind, step)
    ahead, behind = yield [ring.send(ahead[:half], 1), ring.send(behind[half:], -1)]
    arrays = put(arrays, ahead, -(count // 2))
    return put(arrays, behind, count // 2, half)


def ring_scatter(ring, *parts):
    count = ring.count
    rows = parts[0].shape[0] // count
    half = rows // 2

    def piece(offset, start=0, size=rows):
        first = ring.device_at(offset) * rows + start
        return jnp.concatenate(
            [lax.dynamic_slice_in_dim(part, first, size, 0).astype(jnp.float32) for part in parts],
            axis=1,
        )

    far = count // 2
    ahead = piece(far, 0, half).astype(jnp.bfloat16)
    behind = piece(far, half, rows - half).astype(jnp.bfloat16)
    for offset in range(far - 1, -1, -1):
        ahead, behind = yield [ring.send(ahead, 1), ring.send(behind, -1)]
        ahead, behind = (ahead.astype(jnp.float32), behind.astype(jnp.float32))
        if offset == far - 1:
            ahead, behind = (
                jnp.concatenate([ahead, jnp.zeros_like(behind)], axis=0),
                jnp.concatenate([jnp.zeros_like(ahead), behind], axis=0),
            )
        if offset:
            ahead = (ahead + piece(offset)).astype(jnp.bfloat16)
            behind = (behind + piece(-offset)).astype(jnp.bfloat16)
    return ahead + behind + piece(0)


def core_swap(block):
    count = lax.axis_size("tensor")
    return lax.ppermute(block, "tensor", [(k, k ^ 1) for k in range(count)])


def chip_shift(block, step):
    count = lax.axis_size("tensor")
    return lax.ppermute(block, "tensor", [(k, (k + 2 * step) % count) for k in range(count)])


def tensor_parts(block):
    chips = lax.axis_size("tensor") // 2
    mate, *others = yield [core_swap(block)] + [chip_shift(block, k) for k in range(1, chips)]
    mates = yield [core_swap(other) for other in others]
    parts = [block, mate]
    for other, beside in zip(others, mates):
        parts += [other, beside]
    return parts


def in_order(parts):
    chips = len(parts) // 2
    mine = lax.axis_index("tensor")
    flipped = mine % 2 == 1
    pairs = []
    for chip in range(chips):
        first, second = (parts[2 * chip], parts[2 * chip + 1])
        pairs.append((jnp.where(flipped, second, first), jnp.where(flipped, first, second)))
    out = []
    for chip in range(chips):
        back = (mine // 2 + chips - chip) % chips
        for core in range(2):
            value = pairs[0][core]
            for step in range(1, chips):
                value = jnp.where(back == step, pairs[step][core], value)
            out.append(value)
    return out


def seq_gather(values):
    parts = yield from tensor_parts(values)
    return jnp.concatenate(parts, axis=0)


def tensor_scatter(pick):
    chips = lax.axis_size("tensor") // 2
    places = [2 * (chips - step) for step in range(1, chips)]
    mate, *others = yield [core_swap(pick(place + 1)) for place in [0] + places]
    merged = [
        (pick(place).astype(jnp.float32) + other.astype(jnp.float32)).astype(jnp.bfloat16)
        for place, other in zip(places, others)
    ]
    received = yield [chip_shift(value, k + 1) for k, value in enumerate(merged)]
    total = pick(0).astype(jnp.float32) + mate.astype(jnp.float32)
    for other in received:
        total = total + other.astype(jnp.float32)
    return total


def seq_reduce(lowered):
    rows = lowered.shape[0] // lax.axis_size("tensor")
    return tensor_scatter(lambda place: lowered[place * rows : (place + 1) * rows])


def width_total(values):
    chips = lax.axis_size("tensor") // 2
    blocks = values.reshape(chips, 2, -1)
    blocks = blocks + core_swap(blocks)[:, ::-1]
    total = blocks
    for step in range(1, chips):
        total = total + jnp.roll(chip_shift(blocks, step), step, axis=0)
    return total.reshape(values.shape)


def exchange(blocks, axes):
    return lax.all_to_all(blocks, axes, 0, 0, tiled=False)


def dp_scatter(values):
    blocks = values.astype(jnp.bfloat16).reshape((lax.axis_size("dp"), -1) + values.shape[1:])
    return jnp.sum(exchange(blocks, "dp").astype(jnp.float32), axis=0)


def run(chain):
    return lockstep(chain)[0]


def local(
    layer_input,
    out_grad,
    segment_ids,
    valid_mask,
    doc_start,
    norm_gains,
    conv_weight,
    conv_bias,
    mixer_gain,
    shared_proj,
    step_bias,
    decay_log,
    skip_gain,
    mamba_gate,
    mamba_input,
    mamba_step,
    query_proj,
    mamba_out,
    attention_out,
    swiglu_gate,
    swiglu_up,
    swiglu_down,
):
    tensor_position = lax.axis_index("tensor")
    dp_count = lax.axis_size("dp")
    tensor_count = lax.axis_size("tensor")
    device = lax.axis_index("dp") * tensor_count + tensor_position
    ring = Ring(dp_count)
    local_width = mamba_gate.shape[1]
    query_width = query_proj.shape[1]
    head_local = mamba_step.shape[1]
    hidden_width = swiglu_gate.shape[1]
    query_slice = query_width // HEAD_SIZE
    slab = 2 * HEAD_SIZE
    wide = -(-local_width // slab) * slab
    early_width = wide + slab
    block_rows = layer_input.shape[0]
    tokens_per_group = block_rows * tensor_count
    seq_count = tokens_per_group // SEQUENCE_TOKENS
    channel_start = tensor_position * local_width
    head_start = tensor_position * head_local
    channels = conv_weight.shape[1] * dp_count * tensor_count

    def padded(values, columns):
        return jnp.pad(values, ((0, 0), (0, columns - values.shape[1])))

    def placed(rows_in, columns, start):
        whole = jnp.zeros((rows_in.shape[0], columns), rows_in.dtype)
        return lax.dynamic_update_slice_in_dim(whole, rows_in, start, 1)

    device_count = dp_count * tensor_count
    rows_in = mamba_gate.shape[0]
    shared_rows = shared_proj.shape[0]
    small = jnp.concatenate(
        [norm_gains.reshape(-1), conv_weight.reshape(-1), conv_bias, mixer_gain]
    )
    small_width = -(-small.shape[0] // 128) * 128
    if small_width > shared_proj.shape[1]:
        raise ValueError("small parameters")
    small = jnp.pad(small, (0, shared_proj.shape[1] - small.shape[0]))
    small = jnp.pad(small[None], ((0, 7), (0, 0)))
    common = lax.all_gather(jnp.concatenate([shared_proj, small], axis=0), "tensor", axis=0)
    shared_own = common[:, :shared_rows].reshape(rows_in, -1)
    small_own = common[:, shared_rows, :small_width].reshape(1, -1)
    valid_f = valid_mask.astype(jnp.float32)
    out_cot = out_grad.astype(jnp.float32) * valid_f[:, None]
    layer_input, shared_own = together(layer_input, shared_own)
    block = pack(
        rows_in,
        (
            (mamba_gate, wide, False),
            (query_proj, slab, False),
            (mamba_out, local_width, True),
            (attention_out, query_width, True),
            (mamba_input, wide, False),
            (mamba_step, slab, False),
            (shared_own, shared_proj.shape[1], False),
        ),
        jnp.broadcast_to(small_own, (8, small_own.shape[1])),
    )

    def prepared():
        spots, gate, up, down = yield [doc_start, swiglu_gate, swiglu_up, swiglu_down]
        position = jnp.tile(jnp.arange(SEQUENCE_TOKENS, dtype=jnp.int32), seq_count) - spots
        ffn_block = pack(
            rows_in,
            ((gate, hidden_width, False), (up, hidden_width, False), (down, hidden_width, True)),
        )
        ffn_blocks = jnp.broadcast_to(ffn_block[None], (dp_count,) + ffn_block.shape)
        cosines, sines, ffn_blocks = yield [*rope_rows(position), ffn_blocks]
        return (ffn_blocks, cosines, sines)

    x_full, (w_in, small_all), ffn_grad_in, waited = lockstep(
        seq_gather(layer_input),
        ring_gather(ring, block, rows_in),
        after_stages(1, seq_gather(out_cot.astype(jnp.bfloat16))),
        prepared(),
    )
    ffn_blocks, cosine_table, sine_table = waited
    w_in, ffn_grad_in, ffn_blocks = together(w_in, ffn_grad_in, ffn_blocks)
    w_ffn = exchange(ffn_blocks, "dp").reshape(D, -1)
    shared_at = w_in.shape[1] - shared_proj.shape[1]
    late_at = early_width + local_width + query_width
    w_out = w_in[:, early_width:late_at]
    gains_f, conv_f, mixer_gain_f = unpack(
        small_all[:, 0],
        tensor_count,
        small_width,
        (
            (2, norm_gains.shape[1]),
            (CONV + 1, conv_weight.shape[1]),
            (1, mixer_gain.shape[0]),
        ),
    )
    tokens_f = layer_input.astype(jnp.float32)
    scale_one = rms_scale(tokens_f)
    first_full, early_act, late_act, common_act = project(
        x_full,
        gains_f,
        (
            (w_in, early_width, 0),
            (w_in, early_width, late_at),
            (w_in, shared_proj.shape[1], shared_at),
        ),
        block_rows,
    )
    taps = jnp.concatenate(
        [lax.dynamic_slice_in_dim(conv_f, channel_start, local_width, 1), conv_f[:, DSSM:]], axis=1
    )
    own_gain = lax.dynamic_slice_in_dim(mixer_gain_f[0], channel_start, local_width, 0)
    own_bias = lax.dynamic_slice_in_dim(step_bias, head_start, head_local, 0)
    own_decay = lax.dynamic_slice_in_dim(decay_log, head_start, head_local, 0)
    own_skip = lax.dynamic_slice_in_dim(skip_gain, head_start, head_local, 0)
    params = jnp.pad(
        jnp.stack([own_bias, -jnp.exp(own_decay)], axis=0), ((0, 6), (0, slab - head_local))
    )
    skip_row = jnp.broadcast_to(jnp.repeat(own_skip, HEAD_SIZE)[None], (8, local_width))
    doc = doc_start[:, None]
    kv = (tensor_position * query_slice // (QUERY_HEADS // KEY_VALUE_HEADS)).astype(jnp.int32)[None]
    device_ids = jnp.arange(tensor_count, dtype=jnp.int32)
    chip_count = tensor_count // 2
    block_order = (tensor_position // 2 + chip_count - device_ids // 2) % chip_count * 2 + (
        tensor_position + device_ids
    ) % 2

    mamba_y, square_rows, kept_states = mamba_forward(
        block_order, block_rows, early_act, late_act, common_act, doc, taps, params, skip_row
    )
    attended, query_rot, key_rot, value_low, log_total = attention_forward(
        kv, block_order, block_rows, early_act, common_act, cosine_table, sine_table, doc
    )
    square_sum = width_total(square_rows[0])
    gate_scale = lax.rsqrt(square_sum / DSSM + EPS)[:, None]
    gate_z = early_act[:, :local_width]
    sigmoid_z = jax.nn.sigmoid(gate_z)
    silu_z = gate_z * sigmoid_z
    gated_y = mamba_y * silu_z
    normed_b = (gated_y * gate_scale * own_gain).astype(jnp.bfloat16)
    mixed_b = jnp.concatenate([normed_b, attended[:, :query_width]], axis=1)
    mixer_part = product_nt(mixed_b, w_out).astype(jnp.bfloat16)
    mixer_sum = run(seq_reduce(mixer_part))

    middle = tokens_f + mixer_sum
    scale_two = rms_scale(middle)
    second_b = (middle * scale_two * gains_f[1]).astype(jnp.bfloat16)
    ffn_in = run(seq_gather(second_b))
    gate_up_grad, hidden_b, second_part, ffn_part = feed_forward(
        ffn_in, ffn_grad_in, w_ffn, block_rows
    )
    ffn_in, ffn_grad_in, second_part, mixed_b = together(ffn_in, ffn_grad_in, second_part, mixed_b)
    second_grad = run(seq_reduce(second_part))
    ffn_w_grad = weight_grads(((ffn_in, gate_up_grad), (ffn_grad_in, hidden_b)))
    second_value_grad, gain_two_grad = norm_back(middle, scale_two, gains_f[1], second_grad)
    middle_grad = out_cot + second_value_grad
    middle_grad, ffn_w_grad = together(middle_grad, ffn_w_grad)

    gathered = seq_gather(middle_grad.astype(jnp.bfloat16))
    mate, *others = next(gathered)
    mate, ffn_w_grad = together(mate, ffn_w_grad)
    ffn_w_grad = dp_scatter(ffn_w_grad)
    mixer_grad_full = run(resumed(gathered, [mate, *others]))
    ffn_part, mixer_grad_full = together(ffn_part, mixer_grad_full)
    mixed_grad = product(mixer_grad_full, w_out)
    normed_grad = mixed_grad[:, :local_width]
    scaled_normed = normed_grad * own_gain
    inner_sum = width_total(jnp.sum(scaled_normed * gated_y, axis=1))
    attended_grad, attended_at = (mixed_grad, local_width // slab)
    if local_width % slab or query_width != slab:
        attended_grad, attended_at = (padded(mixed_grad[:, local_width:], slab), 0)
    dq, dkv = attention_backward(
        kv,
        block_order,
        block_rows,
        query_rot,
        key_rot,
        value_low,
        cosine_table,
        sine_table,
        doc,
        log_total,
        attended_grad,
        attended_at,
    )
    own_gain_grad = jnp.sum(normed_grad * gated_y * gate_scale, axis=0)
    gated_grad = (
        gate_scale * scaled_normed
        - gated_y * (gate_scale * gate_scale * gate_scale) * (inner_sum / DSSM)[:, None]
    )
    mamba_y_grad = gated_grad * silu_z
    gate_z_grad = (gated_grad * mamba_y * sigmoid_z * (1.0 + gate_z * (1.0 - sigmoid_z))).astype(
        jnp.bfloat16
    )
    early_grad = jnp.concatenate([padded(gate_z_grad, wide), dq], axis=1)
    early_w_grad, first_early, gain_one_early = weight_grads(
        ((mixer_grad_full, mixed_b), (first_full, early_grad)), (w_in, 0)
    )
    early_ring = ring_scatter(ring, early_w_grad)
    early_sent = next(early_ring)
    ffn_out = run(seq_reduce(ffn_part))
    mamba_y_grad, first_early = together(mamba_y_grad, first_early)
    late_grad, taps_grad, params_grad = mamba_backward(
        block_order,
        block_rows,
        late_act,
        common_act,
        doc,
        taps,
        params,
        skip_row,
        mamba_y,
        mamba_y_grad,
        dkv,
        kept_states,
    )

    late_grad, ffn_w_grad, *early_sent = together(late_grad, ffn_w_grad, *early_sent)
    gate_w_grad = ffn_w_grad[:, :hidden_width]
    up_w_grad = ffn_w_grad[:, hidden_width : 2 * hidden_width]
    down_w_grad = ffn_w_grad[:, 2 * hidden_width :].T
    early_sent = early_ring.send(early_sent)
    back = (w_in, late_at // late_grad.shape[1])
    if late_at % late_grad.shape[1]:
        back = (w_in[:, late_at:], 0)
    late_w_grad, first_part, gain_one_late = weight_grads(
        ((first_full, late_grad),), back, first_early
    )
    def summed(taps_grad, params_grad, gain_one_late, ffn_out):
        taps_grad, params_grad, gain_one_late, ffn_out = yield [
            taps_grad,
            params_grad,
            gain_one_late,
            ffn_out,
        ]
        result_b, stat_terms = finish(valid_f[:, None], layer_input, mixer_sum, middle, ffn_out)
        gain_one_grad = (gain_one_early + gain_one_late)[:, 0] / gains_f[0]
        heads = jnp.concatenate(
            [
                placed(params_grad[:3, :head_local], slab, head_start),
                padded(stat_terms[:6, 0][None], slab),
            ],
            axis=0,
        )
        conv_rows = jnp.concatenate(
            [
                placed(taps_grad[: CONV + 1, :local_width], DSSM, channel_start),
                taps_grad[: CONV + 1, local_width:],
            ],
            axis=1,
        )
        sums = gather_sums(
            device_count,
            (
                jnp.stack([gain_one_grad, gain_two_grad], axis=0),
                conv_rows,
                placed(own_gain_grad[None], DSSM, channel_start),
            ),
            ((2, norm_gains.shape[1]), (CONV + 1, conv_weight.shape[1]), (1, mixer_gain.shape[0])),
            heads,
            (MH, MH, MH, 6),
        )
        (sums,) = yield [sums]
        (got,) = yield [exchange(sums, ("dp", "tensor"))]
        outputs = spread_sums(
            got,
            (
                (2, norm_gains.shape[1]),
                (CONV, conv_weight.shape[1]),
                (1, conv_weight.shape[1]),
                (1, mixer_gain.shape[0]),
                (1, MH),
                (1, MH),
                (1, MH),
                (1, 6),
            ),
        )
        stats = outputs[-1][0]
        return (yield list(outputs[:-1]) + [jnp.sqrt(stats[:5] / (stats[5] * D)), result_b])

    def finished(part):
        first_grad = yield from seq_reduce(part)
        first_value_grad, _ = norm_back(tokens_f, scale_one, gains_f[0], first_grad)
        return (yield [middle_grad + first_value_grad])

    late_total, early_total, (input_grad,), outputs = lockstep(
        ring_scatter(ring, late_w_grad),
        resumed(early_ring, early_sent),
        after_stages(1, finished(first_part)),
        summed(taps_grad, params_grad, gain_one_late, ffn_out),
    )
    shared_total = late_total[:, early_width:].astype(jnp.bfloat16)
    places = [
        ((tensor_position // 2 + chip_count - place // 2) % chip_count) * 2
        + (tensor_position + place) % 2
        for place in range(tensor_count)
    ]
    shared_proj_grad = run(
        tensor_scatter(
            lambda place: lax.dynamic_slice_in_dim(
                shared_total, places[place] * shared_rows, shared_rows, 0
            )
        )
    )
    mamba_out_grad = early_total[:, :local_width].T
    attend_out_grad = early_total[:, local_width : local_width + query_width].T
    early_at = local_width + query_width
    gate_proj_grad = early_total[:, early_at : early_at + local_width]
    query_proj_grad = early_total[:, early_at + wide : early_at + wide + query_width]
    input_proj_grad = late_total[:, :local_width]
    step_proj_grad = late_total[:, wide : wide + head_local]
    gains_grad, conv_w_grad, conv_b_grad, gain_full_grad, bias_total, decay_total, skip_total, rms, result_b = outputs
    return (
        result_b,
        input_grad,
        gains_grad,
        conv_w_grad,
        conv_b_grad[0],
        gain_full_grad[0],
        shared_proj_grad,
        bias_total[0],
        decay_total[0],
        skip_total[0],
        gate_proj_grad,
        input_proj_grad,
        step_proj_grad,
        query_proj_grad,
        mamba_out_grad,
        attend_out_grad,
        gate_w_grad,
        up_w_grad,
        down_w_grad,
        rms,
    )


def solution(mesh):
    in_specs = (
        P(("dp", "tensor"), None),
        P(("dp", "tensor"), None),
        P("dp"),
        P(("dp", "tensor")),
        P("dp"),
        P(None, ("dp", "tensor")),
        P(None, ("dp", "tensor")),
        P(("dp", "tensor")),
        P(("dp", "tensor")),
        P(("dp", "tensor"), None),
        P(),
        P(),
        P(),
        P("dp", "tensor"),
        P("dp", "tensor"),
        P("dp", "tensor"),
        P("dp", "tensor"),
        P("tensor", "dp"),
        P("tensor", "dp"),
        P("dp", "tensor"),
        P("dp", "tensor"),
        P("tensor", "dp"),
    )
    out_specs = (
        P(("dp", "tensor"), None),
        P(("dp", "tensor"), None),
        P(None, ("dp", "tensor")),
        P(None, ("dp", "tensor")),
        P(("dp", "tensor")),
        P(("dp", "tensor")),
        P(("dp", "tensor"), None),
        P(),
        P(),
        P(),
        P("dp", "tensor"),
        P("dp", "tensor"),
        P("dp", "tensor"),
        P("dp", "tensor"),
        P("tensor", "dp"),
        P("tensor", "dp"),
        P("dp", "tensor"),
        P("dp", "tensor"),
        P("tensor", "dp"),
        P(),
    )
    return jax.shard_map(local, mesh=mesh, in_specs=in_specs, out_specs=out_specs, check_vma=False)
```

```python
import functools
import math

import jax
import jax.numpy as jnp
from jax import lax
from jax.experimental import pallas as pl
from jax.experimental.pallas import tpu as pltpu
from jax.sharding import PartitionSpec as P

D = 1024
MH = 24
HEAD_SIZE = 64
MAMBA_STATES = 128
CONV = 4
QUERY_HEADS = 8
KEY_VALUE_HEADS = 2
SEQUENCE_TOKENS = 1024
DSSM = 1536


EPS = 1e-05
ROPE_BASE = 100000000000.0
NEG_FILL = -1e30
HIGH = lax.Precision.HIGHEST


def rms_scale(values):
    return lax.rsqrt(jnp.mean(values * values, axis=-1, keepdims=True) + EPS)


def norm_back(values, row_scale, gain_row, grad_in):
    scaled_grad = grad_in * gain_row
    gain_grad = jnp.sum(grad_in * values * row_scale, axis=0)
    value_grad = row_scale * scaled_grad - values * (row_scale * row_scale * row_scale) * jnp.mean(
        scaled_grad * values, axis=-1, keepdims=True
    )
    return (value_grad, gain_grad)


def product(left, right):
    return jnp.dot(left, right, preferred_element_type=jnp.float32)


def product_tn(left, right):
    return lax.dot_general(
        left, right, (((0,), (0,)), ((), ())), preferred_element_type=jnp.float32
    )


def product_nt(left, right):
    return lax.dot_general(
        left, right, (((1,), (1,)), ((), ())), preferred_element_type=jnp.float32
    )


def split_dot(values, selector, dims):
    high = values.astype(jnp.bfloat16)
    low = (values - high.astype(jnp.float32)).astype(jnp.bfloat16)
    left = lax.dot_general(high, selector, dims, preferred_element_type=jnp.float32)
    return left + lax.dot_general(low, selector, dims, preferred_element_type=jnp.float32)


def estimate(flops, size):
    return pl.CostEstimate(flops=int(flops * 0.05), bytes_accessed=int(size * 0.05), transcendentals=0)


NN = (((1,), (0,)), ((), ()))
NT = (((1,), (1,)), ((), ()))
TN = (((0,), (0,)), ((), ()))


def mxu(left, right, dims):
    return lax.dot_general(
        left.astype(jnp.bfloat16),
        right.astype(jnp.bfloat16),
        dims,
        preferred_element_type=jnp.float32,
    )


def iota(shape, dim):
    return lax.broadcasted_iota(jnp.int32, shape, dim)


def head_groups(width):
    return [(low, min(low + 2 * HEAD_SIZE, width)) for low in range(0, width, 2 * HEAD_SIZE)]


def chunk_common(chunk, start, rows, width, raw_ref, doc_ref, pad_ref, w_ref, par_ref):
    doc = doc_ref[pl.ds(start, chunk), :]
    age = start + iota((chunk, 1), 0) - doc
    span = pad_ref[pl.ds(start, chunk + 8), :]
    conv = w_ref[CONV : CONV + 1, :] + w_ref[CONV - 1 : CONV, :] * span[8:, :]
    lagged = [span[8:, :]]
    for lag in range(1, CONV):
        moved = jnp.where(age >= lag, span[8 - lag : 8 - lag + chunk, :], 0.0)
        lagged.append(moved)
        conv = conv + w_ref[CONV - 1 - lag : CONV - lag, :] * moved
    sig = jax.nn.sigmoid(conv)
    act = conv * sig
    raw = raw_ref[rows, :] + par_ref[0:1, :]
    step = jnp.maximum(raw, 0.0) + jnp.log1p(jnp.exp(-jnp.abs(raw)))
    rate = step * par_ref[1:2, :]
    lower = (iota((chunk, chunk), 0) >= iota((chunk, chunk), 1)).astype(jnp.bfloat16)
    high = rate.astype(jnp.bfloat16)
    low = (rate - high.astype(jnp.float32)).astype(jnp.bfloat16)
    total = mxu(lower, high, NN) + mxu(lower, low, NN)
    lanes = par_ref.shape[1]
    spread = (iota((lanes, width), 0) == iota((lanes, width), 1) // HEAD_SIZE).astype(jnp.bfloat16)
    key_pos = start + iota((chunk, chunk), 1)
    allowed = (key_pos <= start + iota((chunk, chunk), 0)) & (key_pos >= doc)
    doc_last = doc[chunk - 1 : chunk, :]
    ends = total[chunk - 1 : chunk, :]
    live = jnp.where(doc < start, jnp.exp(total), 0.0)
    keep = jnp.where(start + iota((chunk, 1), 0) >= doc_last, jnp.exp(ends - total), 0.0)
    carry = jnp.where(doc_last < start, jnp.exp(ends), 0.0)
    wide = split_dot(jnp.concatenate([step, live, keep, jnp.broadcast_to(carry, (8, lanes))], axis=0), spread, NN)
    return dict(
        conv=conv, sig=sig, act=act, raw=raw, step=step, total=total, turned=total.T, spread=spread, allowed=allowed,
        carry=carry, age=age, lagged=lagged, lower=lower,
        step_w=wide[:chunk], live_w=wide[chunk : 2 * chunk], keep_w=wide[2 * chunk : 3 * chunk],
        carry_w=wide[3 * chunk : 3 * chunk + 1],
    )


def decay_of(part, head):
    gap = part["total"][:, head : head + 1] - part["turned"][head : head + 1, :]
    return jnp.where(part["allowed"], jnp.exp(gap), 0.0)


def only(values, low, high):
    lane = iota(values.shape, 1)
    return jnp.where((lane >= low) & (lane < high), values, jnp.zeros_like(values))


def place_of(order_ref, block_rows, length, start):
    token = pl.program_id(0) * length + start
    return pl.multiple_of(
        order_ref[token // block_rows] * block_rows + token % block_rows, 128
    )


def fill_conv_input(order_ref, block_rows, width, x_ref, bc_ref, pad_ref):
    length = pad_ref.shape[0] - 8
    pad_ref[0:8, :] = jnp.zeros((8, pad_ref.shape[1]), jnp.float32)
    for start in range(0, length, block_rows):
        rows = pl.ds(place_of(order_ref, block_rows, length, start), block_rows)
        pad_ref[8 + start : 8 + start + block_rows, :width] = x_ref[rows, :width]
        pad_ref[8 + start : 8 + start + block_rows, width:] = bc_ref[rows, :]


def mamba_forward_kernel(
    chunk, width, block_rows, order_ref, x_ref, bc_ref, raw_ref, z_ref, doc_ref, w_ref, par_ref, skip_ref, y_ref, square_ref, kept_ref, pad_ref, state_ref
):
    length = pad_ref.shape[0] - 8
    fill_conv_input(order_ref, block_rows, width, x_ref, bc_ref, pad_ref)
    state_ref[...] = jnp.zeros_like(state_ref)

    def one_chunk(index, _):
        start = pl.multiple_of(index * chunk, chunk)
        rows = pl.ds(place_of(order_ref, block_rows, length, start), chunk)
        part = chunk_common(chunk, start, rows, width, raw_ref, doc_ref, pad_ref, w_ref, par_ref)
        inner = part["act"][:, :width]
        bm = part["act"][:, width : width + MAMBA_STATES].astype(jnp.bfloat16)
        cm = part["act"][:, width + MAMBA_STATES :].astype(jnp.bfloat16)
        driven = (inner * part["step_w"]).astype(jnp.bfloat16)
        pair = mxu(cm, bm, NT)
        pieces = []
        for low, high in head_groups(width):
            heads = range(low // HEAD_SIZE, high // HEAD_SIZE)
            mats = [(decay_of(part, head) * pair).astype(jnp.bfloat16) for head in heads]
            piece = driven[:, low:high]
            right = [
                only(piece, HEAD_SIZE * k, HEAD_SIZE * (k + 1)) if len(mats) > 1 else piece
                for k in range(len(mats))
            ]
            pieces.append(
                mxu(jnp.concatenate(mats, axis=1), jnp.concatenate(right, axis=0), NN)
            )
        state = state_ref[...]
        kept_ref[pl.ds(pl.multiple_of(index * MAMBA_STATES, MAMBA_STATES), MAMBA_STATES), :] = state
        y = jnp.concatenate(pieces, axis=1) + part["live_w"] * mxu(cm, state, NN)
        y = y + skip_ref[0:1, :] * inner
        state_ref[...] = state * part["carry_w"] + mxu(
            bm, driven.astype(jnp.float32) * part["keep_w"], TN
        )
        y_ref[rows, :] = y
        z = z_ref[rows, :width]
        gated = y * z * jax.nn.sigmoid(z)
        square_ref[:, rows] = split_dot_left(gated * gated)
        return 0

    lax.fori_loop(0, length // chunk, one_chunk, 0, unroll=2)


def split_dot_left(values):
    ones = jnp.ones((8, values.shape[1]), jnp.bfloat16)
    high = values.astype(jnp.bfloat16)
    low = (values - high.astype(jnp.float32)).astype(jnp.bfloat16)
    return mxu(ones, high, NT) + mxu(ones, low, NT)


def mamba_backward_kernel(
    chunk, width, block_rows, order_ref, x_ref, bc_ref, raw_ref, doc_ref, w_ref, par_ref, skip_ref, y_ref, dy_ref,
    dkv_ref, kept_ref, din_ref, dw_ref, dpar_ref, pad_ref, state_ref, halo_ref, dskip_ref
):
    length = pad_ref.shape[0] - 8
    count = length // chunk
    wide = x_ref.shape[1]
    common_at = wide + 2 * HEAD_SIZE

    @pl.when(pl.program_id(0) == 0)
    def _():
        if wide > width:
            din_ref[...] = jnp.zeros_like(din_ref)
        din_ref[:, common_at + 2 * MAMBA_STATES :] = dkv_ref[...]

    fill_conv_input(order_ref, block_rows, width, x_ref, bc_ref, pad_ref)
    state_ref[...] = jnp.zeros_like(state_ref)
    halo_ref[...] = jnp.zeros_like(halo_ref)

    @pl.when(pl.program_id(0) == 0)
    def _():
        dw_ref[...] = jnp.zeros_like(dw_ref)
        dpar_ref[...] = jnp.zeros_like(dpar_ref)
        dskip_ref[...] = jnp.zeros_like(dskip_ref)

    def one_chunk(step_index, _):
        index = count - 1 - step_index
        start = pl.multiple_of(index * chunk, chunk)
        rows = pl.ds(place_of(order_ref, block_rows, length, start), chunk)
        part = chunk_common(chunk, start, rows, width, raw_ref, doc_ref, pad_ref, w_ref, par_ref)
        inner = part["act"][:, :width]
        bm = part["act"][:, width : width + MAMBA_STATES].astype(jnp.bfloat16)
        cm = part["act"][:, width + MAMBA_STATES :].astype(jnp.bfloat16)
        driven = (inner * part["step_w"]).astype(jnp.bfloat16)
        driven_f = driven.astype(jnp.float32)
        y = y_ref[rows, :]
        dy = dy_ref[rows, :]
        dy_b = dy.astype(jnp.bfloat16)
        pair = mxu(cm, bm, NT)
        pair_grad = jnp.zeros((chunk, chunk), jnp.float32)
        pieces = []
        for low, high in head_groups(width):
            heads = list(range(low // HEAD_SIZE, high // HEAD_SIZE))
            piece = driven[:, low:high]
            grads = [
                only(dy_b[:, low:high], HEAD_SIZE * k, HEAD_SIZE * (k + 1)) if len(heads) > 1 else dy_b[:, low:high]
                for k in range(len(heads))
            ]
            mats = []
            for k, head in enumerate(heads):
                decay = decay_of(part, head)
                mats.append((decay * pair).astype(jnp.bfloat16))
                pair_grad = pair_grad + decay * mxu(grads[k], piece, NT)
            pieces.append(mxu(jnp.concatenate(mats, axis=0), jnp.concatenate(grads, axis=0), TN))
        within = jnp.concatenate(pieces, axis=1)
        state = kept_ref[pl.ds(pl.multiple_of(index * MAMBA_STATES, MAMBA_STATES), MAMBA_STATES), :]
        state_grad = state_ref[...]
        pair_grad = pair_grad.astype(jnp.bfloat16)
        dy_live = (dy * part["live_w"]).astype(jnp.bfloat16)
        driven_keep = (driven_f * part["keep_w"]).astype(jnp.bfloat16)
        later = part["keep_w"] * mxu(bm, state_grad, NN)
        c_grad = mxu(pair_grad, bm, NN) + mxu(dy_live, state, NT)
        b_grad = mxu(pair_grad, cm, TN) + mxu(driven_keep, state_grad, NT)
        state_ref[...] = state_grad * part["carry_w"] + mxu(cm, dy_live, TN)
        driven_grad = within + later
        later_part = driven_f * later
        mixed = y - skip_ref[0:1, :] * inner
        sums = split_dot(
            jnp.concatenate(
                [
                    dy_b.astype(jnp.float32) * mixed - driven_f * within - later_part,
                    driven_grad * inner,
                    jnp.broadcast_to(
                        jnp.sum(later_part, axis=0, keepdims=True)
                        + part["carry_w"] * jnp.sum(state_grad * state, axis=0, keepdims=True),
                        (8, width),
                    ),
                ],
                axis=0,
            ),
            part["spread"],
            NT,
        )
        high = sums[:chunk].astype(jnp.bfloat16)
        low = (sums[:chunk] - high.astype(jnp.float32)).astype(jnp.bfloat16)
        rate_grad = (
            mxu(part["lower"], high, TN) + mxu(part["lower"], low, TN) + sums[2 * chunk : 2 * chunk + 1]
        )
        step_grad = rate_grad * par_ref[1:2, :] + sums[chunk : 2 * chunk]
        raw_grad = step_grad * jax.nn.sigmoid(part["raw"])
        din_ref[rows, wide:common_at] = raw_grad.astype(jnp.bfloat16)
        dpar_ref[0:1, :] += jnp.sum(raw_grad, axis=0, keepdims=True)
        dpar_ref[1:2, :] += par_ref[1:2, :] * jnp.sum(rate_grad * part["step"], axis=0, keepdims=True)
        dskip_ref[0:1, :] += jnp.sum(dy * inner, axis=0, keepdims=True)
        inner_grad = driven_grad * part["step_w"] + skip_ref[0:1, :] * dy
        sig, conv = (part["sig"], part["conv"])
        conv_grad = jnp.concatenate([inner_grad, b_grad, c_grad], axis=1) * (
            sig * (1.0 + conv * (1.0 - sig))
        )
        dw_ref[CONV : CONV + 1, :] += jnp.sum(conv_grad, axis=0, keepdims=True)
        v_grad = w_ref[CONV - 1 : CONV, :] * conv_grad
        long = jnp.concatenate([conv_grad, halo_ref[...]], axis=0)
        next_start = jnp.minimum(start + chunk, length - 8)
        ages = jnp.concatenate([part["age"], start + chunk + iota((8, 1), 0) - doc_ref[pl.ds(pl.multiple_of(next_start, 8), 8), :]], axis=0)
        dw_ref[CONV - 1 : CONV, :] += jnp.sum(conv_grad * part["lagged"][0], axis=0, keepdims=True)
        for lag in range(1, CONV):
            dw_ref[CONV - 1 - lag : CONV - lag, :] += jnp.sum(
                conv_grad * part["lagged"][lag], axis=0, keepdims=True
            )
            masked = jnp.where(ages >= lag, long, 0.0)
            v_grad = v_grad + w_ref[CONV - 1 - lag : CONV - lag, :] * masked[lag : lag + chunk, :]
        halo_ref[...] = conv_grad[:8, :]
        din_ref[rows, :width] = v_grad[:, :width].astype(jnp.bfloat16)
        din_ref[rows, common_at : common_at + 2 * MAMBA_STATES] = v_grad[:, width:].astype(jnp.bfloat16)
        return 0

    lax.fori_loop(0, count, one_chunk, 0, unroll=2)

    @pl.when(pl.program_id(0) == pl.num_programs(0) - 1)
    def _():
        lanes = dpar_ref.shape[1]
        spread = (iota((lanes, width), 0) == iota((lanes, width), 1) // HEAD_SIZE).astype(jnp.bfloat16)
        dpar_ref[2:3, :] = split_dot(dskip_ref[...], spread, NT)[0:1]


CHUNK = 256
VMEM_LIMIT = 60 * 1024 * 1024


def tokens_spec(tokens, width, place=0):
    return pl.BlockSpec((tokens, width), lambda i, *_: (0, place))


def whole_spec(shape):
    return pl.BlockSpec(shape, lambda i, *_: (0,) * len(shape))


def mamba_forward(order, block_rows, early, late, common, doc, taps, params, skip_row, chunk=CHUNK):
    tokens = late.shape[0]
    width = skip_row.shape[1]
    lanes = params.shape[1]
    wide = late.shape[1] - lanes
    seq = SEQUENCE_TOKENS
    count = tokens // seq
    kept = seq // chunk * MAMBA_STATES
    return pl.pallas_call(
        functools.partial(mamba_forward_kernel, chunk, width, block_rows),
        grid_spec=pltpu.PrefetchScalarGridSpec(
        num_scalar_prefetch=1,
        grid=(count,),
        in_specs=[
            tokens_spec(tokens, wide),
            tokens_spec(tokens, 2 * MAMBA_STATES),
            tokens_spec(tokens, lanes, wide // lanes),
            tokens_spec(tokens, wide),
            pl.BlockSpec((seq, 1), lambda i, *_: (i, 0)),
            whole_spec(taps.shape),
            whole_spec(params.shape),
            whole_spec(skip_row.shape),
        ],
        out_specs=[
            tokens_spec(tokens, width),
            whole_spec((8, tokens)),
            pl.BlockSpec((kept, width), lambda i, *_: (i, 0)),
        ],
        scratch_shapes=[
            pltpu.VMEM((seq + 8, width + 2 * MAMBA_STATES), jnp.float32),
            pltpu.VMEM((MAMBA_STATES, width), jnp.float32),
        ],
        ),
        out_shape=[
            jax.ShapeDtypeStruct((tokens, width), jnp.float32),
            jax.ShapeDtypeStruct((8, tokens), jnp.float32),
            jax.ShapeDtypeStruct((count * kept, width), jnp.float32),
        ],
        compiler_params=pltpu.CompilerParams(vmem_limit_bytes=VMEM_LIMIT),
        cost_estimate=estimate(tokens * width * 20000, tokens * width * 20),
    )(order, late, common, late, early, doc, taps, params, skip_row)


def mamba_backward(
    order, block_rows, late, common, doc, taps, params, skip_row, y, dy, dkv, kept_states, chunk=CHUNK
):
    tokens = late.shape[0]
    width = skip_row.shape[1]
    lanes = params.shape[1]
    wide = late.shape[1] - lanes
    seq = SEQUENCE_TOKENS
    count = tokens // seq
    kept = seq // chunk * MAMBA_STATES
    conv_width = width + 2 * MAMBA_STATES
    return pl.pallas_call(
        functools.partial(mamba_backward_kernel, chunk, width, block_rows),
        grid_spec=pltpu.PrefetchScalarGridSpec(
        num_scalar_prefetch=1,
        grid=(count,),
        in_specs=[
            tokens_spec(tokens, wide),
            tokens_spec(tokens, 2 * MAMBA_STATES),
            tokens_spec(tokens, lanes, wide // lanes),
            pl.BlockSpec((seq, 1), lambda i, *_: (i, 0)),
            whole_spec(taps.shape),
            whole_spec(params.shape),
            whole_spec(skip_row.shape),
            tokens_spec(tokens, width),
            tokens_spec(tokens, width),
            tokens_spec(tokens, dkv.shape[1]),
            pl.BlockSpec((kept, width), lambda i, *_: (i, 0)),
        ],
        out_specs=[
            tokens_spec(tokens, late.shape[1] + common.shape[1]),
            whole_spec((8, conv_width)),
            whole_spec((8, lanes)),
        ],
        scratch_shapes=[
            pltpu.VMEM((seq + 8, conv_width), jnp.float32),
            pltpu.VMEM((MAMBA_STATES, width), jnp.float32),
            pltpu.VMEM((8, conv_width), jnp.float32),
            pltpu.VMEM((8, width), jnp.float32),
        ],
        ),
        out_shape=[
            jax.ShapeDtypeStruct((tokens, late.shape[1] + common.shape[1]), jnp.bfloat16),
            jax.ShapeDtypeStruct((8, conv_width), jnp.float32),
            jax.ShapeDtypeStruct((8, lanes), jnp.float32),
        ],
        compiler_params=pltpu.CompilerParams(vmem_limit_bytes=VMEM_LIMIT),
        cost_estimate=estimate(tokens * width * 60000, tokens * width * 20),
    )(
        order, late, common, late, doc, taps, params, skip_row, y, dy, dkv, kept_states
    )


NEGATIVE = -1e30
QUERY_BLOCK = 256


def swap_halves(values):
    half = HEAD_SIZE // 2
    lane = iota(values.shape, 1)
    width = values.shape[1]
    return jnp.where(
        lane % HEAD_SIZE < half,
        pltpu.roll(values, width - half, 1),
        pltpu.roll(values, half, 1),
    )


def attention_mask(start, rows, keys, doc):
    position = start + iota((rows, 1), 0)
    key_pos = iota((rows, keys), 1)
    return (key_pos <= position) & (key_pos >= doc)


def both_heads(values):
    return jnp.concatenate(
        [only(values, 0, HEAD_SIZE), only(values, HEAD_SIZE, 2 * HEAD_SIZE)], axis=0
    )


def chosen(values, kv):
    lane = iota(values.shape, 1)
    turned = pltpu.roll(values, HEAD_SIZE, 1)
    return jnp.where((lane < HEAD_SIZE) == (kv == 0), values, turned)


def attention_forward_kernel(
    block_rows, kv_ref, order_ref, q_ref, key_ref, value_ref, cos_ref, sin_ref, doc_ref, out_ref, qr_ref, kr_ref, vr_ref, log_ref
):
    length = qr_ref.shape[0]
    kv = kv_ref[0]
    rows = block_rows
    for start in range(0, length, rows):
        block = slice(start, start + rows)
        place = pl.ds(place_of(order_ref, block_rows, length, start), rows)
        cos, sin = (cos_ref[block, :], sin_ref[block, :])
        query, key = (q_ref[place, :], key_ref[place, :])
        turned = (query * cos + swap_halves(query) * sin).astype(jnp.bfloat16)
        qr_ref[block, :] = (turned.astype(jnp.float32) * HEAD_SIZE**-0.5).astype(jnp.bfloat16)
        kr_ref[block, :] = chosen(key * cos + swap_halves(key) * sin, kv).astype(jnp.bfloat16)
        vr_ref[block, :] = chosen(value_ref[place, :], kv).astype(jnp.bfloat16)
        keys = start + rows
        mask = attention_mask(start, rows, keys, doc_ref[block, :])
        scores = mxu(both_heads(qr_ref[block, :]), kr_ref[0:keys, :], NT)
        outs = []
        logs = []
        for head in range(2):
            part = jnp.where(mask, scores[head * rows : (head + 1) * rows], NEGATIVE)
            peak = jnp.max(part, axis=1, keepdims=True)
            weight = jnp.exp(part - peak)
            total = jnp.sum(weight, axis=1, keepdims=True)
            outs.append(mxu(weight * (1.0 / total), vr_ref[0:keys, :], NN))
            logs.append(peak + jnp.log(total))
        lane = iota((rows, 2 * HEAD_SIZE), 1)
        out_ref[place, :] = jnp.where(lane < HEAD_SIZE, outs[0], outs[1]).astype(jnp.bfloat16)
        log_ref[block, :] = jnp.where(lane < HEAD_SIZE, logs[0], logs[1])


def attention_backward_kernel(
    block_rows, kv_ref, order_ref, qr_ref, kr_ref, vr_ref, cos_ref, sin_ref, doc_ref, log_ref, grad_ref, dq_ref, dkv_ref, dk_ref, dv_ref
):
    length = qr_ref.shape[0]
    kv = kv_ref[0]
    rows = block_rows
    lane = iota((rows, 2 * HEAD_SIZE), 1)
    mine = (lane < HEAD_SIZE) == (kv == 0)
    dk_ref[...] = jnp.zeros_like(dk_ref)
    dv_ref[...] = jnp.zeros_like(dv_ref)
    for start in reversed(range(0, length, rows)):
        keys = start + rows
        block = slice(start, start + rows)
        place = pl.ds(place_of(order_ref, block_rows, length, start), rows)
        mask = attention_mask(start, rows, keys, doc_ref[block, :])
        query = both_heads(qr_ref[block, :])
        grad = both_heads(grad_ref[place, :].astype(jnp.bfloat16))
        logs = log_ref[block, :]
        scores = mxu(query, kr_ref[0:keys, :], NT)
        prob_grad = mxu(grad, vr_ref[0:keys, :], NT)
        probs = []
        score_grads = []
        for head in range(2):
            part = slice(head * rows, (head + 1) * rows)
            log = logs[:, head * HEAD_SIZE : head * HEAD_SIZE + 1]
            weight = jnp.where(mask, jnp.exp(scores[part] - log), 0.0)
            product_grad = weight * prob_grad[part]
            total = jnp.sum(product_grad, axis=1, keepdims=True)
            probs.append(weight.astype(jnp.bfloat16))
            score_grads.append((product_grad - weight * total).astype(jnp.bfloat16))
        cos, sin = (cos_ref[block, :], sin_ref[block, :])
        dq = mxu(jnp.concatenate(score_grads, axis=0), kr_ref[0:keys, :], NN)
        dq = jnp.where(lane < HEAD_SIZE, dq[:rows], dq[rows:]) * HEAD_SIZE**-0.5
        dq = dq * cos - swap_halves(dq) * sin
        dq_ref[place, :] = dq.astype(jnp.bfloat16)
        dk_ref[0:keys, :] += mxu(jnp.concatenate(score_grads, axis=0), query, TN)
        dv_ref[0:keys, :] += mxu(jnp.concatenate(probs, axis=0), grad, TN)
        dk = dk_ref[block, :]
        dk = dk + pltpu.roll(dk, HEAD_SIZE, 1)
        dk = dk * cos - swap_halves(dk) * sin
        dv = dv_ref[block, :]
        dv = dv + pltpu.roll(dv, HEAD_SIZE, 1)
        dkv_ref[place, : 2 * HEAD_SIZE] = jnp.where(mine, dk, 0.0).astype(jnp.bfloat16)
        dkv_ref[place, 2 * HEAD_SIZE :] = jnp.where(mine, dv, 0.0).astype(jnp.bfloat16)


def attention_call(kernel, kv, order, block_rows, tokens, ins, outs, scratch, flops):
    seq = SEQUENCE_TOKENS

    def spec(columns, place):
        if place is None:
            return pl.BlockSpec((seq, columns), lambda i, *_: (i, 0))
        return tokens_spec(tokens, columns, place)

    return pl.pallas_call(
        functools.partial(kernel, block_rows),
        grid_spec=pltpu.PrefetchScalarGridSpec(
            num_scalar_prefetch=2,
            grid=(tokens // seq,),
            in_specs=[spec(columns, place) for _, columns, place in ins],
            out_specs=[spec(columns, place) for _, columns, place in outs],
            scratch_shapes=scratch,
        ),
        out_shape=[jax.ShapeDtypeStruct((tokens, columns), kind) for kind, columns, _ in outs],
        compiler_params=pltpu.CompilerParams(vmem_limit_bytes=VMEM_LIMIT),
        cost_estimate=estimate(flops * tokens, tokens * 4096),
    )(kv, order, *[value for value, _, _ in ins])


def attention_forward(kv, order, block_rows, early, common, cos, sin, doc):
    two = 2 * HEAD_SIZE
    low, full = (jnp.bfloat16, jnp.float32)
    query_at = early.shape[1] // two - 1
    key_at = 2 * MAMBA_STATES // two
    return attention_call(
        attention_forward_kernel,
        kv,
        order,
        block_rows,
        early.shape[0],
        (
            (early, two, query_at),
            (common, two, key_at),
            (common, two, key_at + 1),
            (cos, two, None),
            (sin, two, None),
            (doc, 1, None),
        ),
        ((low, two, 0), (low, two, None), (low, two, None), (low, two, None), (full, two, None)),
        [],
        4000000,
    )


def attention_backward(kv, order, block_rows, qr, kr, vr, cos, sin, doc, log, grad, grad_at):
    two = 2 * HEAD_SIZE
    seq = SEQUENCE_TOKENS
    return attention_call(
        attention_backward_kernel,
        kv,
        order,
        block_rows,
        qr.shape[0],
        (
            (qr, two, None),
            (kr, two, None),
            (vr, two, None),
            (cos, two, None),
            (sin, two, None),
            (doc, 1, None),
            (log, two, None),
            (grad, two, grad_at),
        ),
        ((jnp.bfloat16, two, 0), (jnp.bfloat16, 2 * two, 0)),
        [pltpu.VMEM((seq, two), jnp.float32), pltpu.VMEM((seq, two), jnp.float32)],
        9000000,
    )


def pack_kernel(rows, widths, turned, *refs):
    spot = 0
    out_ref = refs[-1]
    if out_ref.shape[0] > rows:
        extra_ref = refs[-2]
        out_ref[rows:, :] = jnp.zeros((out_ref.shape[0] - rows, out_ref.shape[1]), out_ref.dtype)
        out_ref[rows:, : extra_ref.shape[1]] = extra_ref[...]
    for ref, width, turn in zip(refs, widths, turned):
        value = ref[...].T if turn else ref[...]
        have = value.shape[1]
        out_ref[:rows, spot : spot + have] = value
        if width > have:
            out_ref[:rows, spot + have : spot + width] = jnp.zeros(
                (value.shape[0], width - have), value.dtype
            )
        spot += width


def pack(rows, pieces, extra=None):
    widths = [width for _, width, _ in pieces]
    turned = [turn for _, _, turn in pieces]
    arrays = [value for value, _, _ in pieces]
    size = rows * sum(widths)
    below = 0
    if extra is not None:
        arrays.append(extra)
        below = extra.shape[0]
    return pl.pallas_call(
        functools.partial(pack_kernel, rows, widths, turned),
        out_shape=jax.ShapeDtypeStruct((rows + below, sum(widths)), arrays[0].dtype),
        compiler_params=pltpu.CompilerParams(vmem_limit_bytes=VMEM_LIMIT),
        cost_estimate=estimate(size, 4 * size),
    )(*arrays)


def unpack_kernel(groups, size, pieces, small_ref, *out_refs):
    spot = 0
    for out_ref, (rows, width) in zip(out_refs, pieces):
        total = out_ref.shape[1]
        column = iota((width, total), 1)
        owner = iota((small_ref.shape[0], total), 1) // (width * groups)
        mine = owner == iota((small_ref.shape[0], total), 0)
        for row in range(rows):
            found = jnp.zeros((small_ref.shape[0], total), jnp.float32)
            for group in range(groups):
                pick = (column % width == iota((width, total), 0)) & (
                    column // width % groups == group
                )
                start = group * size + spot
                found = found + mxu(
                    small_ref[:, start : start + width], pick.astype(jnp.bfloat16), NN
                )
            out_ref[row : row + 1, :] = jnp.sum(
                jnp.where(mine, found, 0.0), axis=0, keepdims=True
            )
            spot += width
        if rows < out_ref.shape[0]:
            out_ref[rows:, :] = jnp.zeros((out_ref.shape[0] - rows, total), jnp.float32)


def unpack(small, groups, size, pieces):
    count = small.shape[0] * groups
    return pl.pallas_call(
        functools.partial(unpack_kernel, groups, size, pieces),
        out_shape=[
            jax.ShapeDtypeStruct((8, count * width), jnp.float32) for _, width in pieces
        ],
        compiler_params=pltpu.CompilerParams(vmem_limit_bytes=VMEM_LIMIT),
        cost_estimate=estimate(1 << 26, 1 << 18),
    )(small)


def project_kernel(count, x_ref, gain_ref, *refs):
    x = x_ref[...].astype(jnp.float32)
    scale = lax.rsqrt(jnp.mean(x * x, axis=1, keepdims=True) + EPS)
    first = (x * scale * gain_ref[0:1, :]).astype(jnp.bfloat16)
    refs[count][...] = first
    for w_ref, out_ref in zip(refs[:count], refs[count + 1 :]):
        out_ref[...] = mxu(first, w_ref[...], NN)


def project(x, gains, weights, rows):
    tokens, width = x.shape
    arrays, specs = ([], [])
    for array, columns, start in weights:
        if start % columns:
            array, start = (array[:, start : start + columns], 0)
        arrays.append(array)
        specs.append(
            pl.BlockSpec(
                (width, columns), functools.partial(lambda place, i: (0, place), start // columns)
            )
        )
    by_rows = lambda columns: pl.BlockSpec((rows, columns), lambda i: (i, 0))
    total = sum(columns for _, columns, _ in weights)
    return pl.pallas_call(
        functools.partial(project_kernel, len(weights)),
        grid=(tokens // rows,),
        in_specs=[by_rows(width), pl.BlockSpec(gains.shape, lambda i: (0, 0))] + specs,
        out_specs=[by_rows(width)] + [by_rows(columns) for _, columns, _ in weights],
        out_shape=[jax.ShapeDtypeStruct((tokens, width), jnp.bfloat16)]
        + [jax.ShapeDtypeStruct((tokens, columns), jnp.float32) for _, columns, _ in weights],
        compiler_params=pltpu.CompilerParams(vmem_limit_bytes=VMEM_LIMIT),
        cost_estimate=estimate(2 * tokens * width * total, 2 * width * total + 4 * tokens * (width + total)),
    )(x, gains, *arrays)


def gather_kernel(pieces, extra, *refs):
    out_ref = refs[-1]
    count = out_ref.shape[0]
    out_ref[...] = jnp.zeros_like(out_ref)
    spot = 0
    for ref, (rows, width) in zip(refs, pieces):
        total = ref.shape[1]
        pick = (iota((total, width), 0) % width == iota((total, width), 1)).astype(jnp.bfloat16)
        mine = iota((count, total), 1) // width == iota((count, total), 0)
        for row in range(rows):
            rest = jnp.where(mine, ref[row : row + 1, :], 0.0)
            found = jnp.zeros((count, width), jnp.float32)
            for _ in range(3):
                low = rest.astype(jnp.bfloat16)
                found = found + mxu(low, pick, NN)
                rest = rest - low.astype(jnp.float32)
            out_ref[:, spot : spot + width] = found
            spot += width
    for row in range(refs[-2].shape[0]):
        width = extra[row]
        out_ref[:, spot : spot + width] = jnp.broadcast_to(
            refs[-2][row : row + 1, :width], (count, width)
        )
        spot += width


def gather_sums(count, arrays, pieces, everywhere, extra):
    columns = sum(rows * width for rows, width in pieces) + sum(extra)
    columns = -(-columns // 128) * 128
    return pl.pallas_call(
        functools.partial(gather_kernel, pieces, extra),
        out_shape=jax.ShapeDtypeStruct((count, columns), jnp.float32),
        compiler_params=pltpu.CompilerParams(vmem_limit_bytes=VMEM_LIMIT),
        cost_estimate=estimate(1 << 26, 1 << 18),
    )(*arrays, everywhere)


def spread_kernel(shapes, got_ref, *out_refs):
    sums = jnp.sum(got_ref[...], axis=0, keepdims=True)
    spot = 0
    for out_ref, (rows, width) in zip(out_refs, shapes):
        for row in range(rows):
            out_ref[row : row + 1, :] = sums[:, spot : spot + width]
            spot += width


def spread_sums(got, shapes):
    return pl.pallas_call(
        functools.partial(spread_kernel, shapes),
        out_shape=[jax.ShapeDtypeStruct(shape, jnp.float32) for shape in shapes],
        compiler_params=pltpu.CompilerParams(vmem_limit_bytes=VMEM_LIMIT),
        cost_estimate=estimate(1 << 16, 1 << 17),
    )(got)


def weight_grad_kernel(count, with_back, *refs):
    lefts, rights = (refs[:count], refs[count : 2 * count])
    rest = refs[2 * count :]
    out_ref = rest[-3] if with_back else rest[-1]
    spot = 0
    for left, right in zip(lefts, rights):
        grad = mxu(left[...], right[...], TN)
        columns = right.shape[1]
        out_ref[:, spot : spot + columns] = grad.astype(jnp.bfloat16)
        spot += columns
    if with_back:
        w_ref = rest[0]
        part = mxu(rights[-1][...], w_ref[...], NT)
        if len(rest) > 4:
            part = part + rest[1][...].astype(jnp.float32)
        rest[-2][...] = part.astype(rest[-2].dtype)
        rest[-1][...] = jnp.sum(grad * w_ref[...].astype(jnp.float32), axis=1, keepdims=True)


def weight_grads(pairs, back=None, base=None, kind=jnp.bfloat16):
    tokens, rows = pairs[0][0].shape
    total = sum(right.shape[1] for _, right in pairs)
    block = min(rows, 512)
    ins = [left for left, _ in pairs] + [right for _, right in pairs]
    specs = [pl.BlockSpec((tokens, block), lambda i: (0, i)) for _ in pairs]
    specs += [pl.BlockSpec((tokens, right.shape[1]), lambda i: (0, 0)) for _, right in pairs]
    outs = [jax.ShapeDtypeStruct((rows, total), jnp.bfloat16)]
    out_specs = [pl.BlockSpec((block, total), lambda i: (i, 0))]
    flops = 2 * tokens * rows * total
    if back is not None:
        weight, place = back
        ins.append(weight)
        specs.append(pl.BlockSpec((block, pairs[-1][1].shape[1]), lambda i: (i, place)))
        if base is not None:
            ins.append(base)
            specs.append(pl.BlockSpec((tokens, block), lambda i: (0, i)))
        outs += [
            jax.ShapeDtypeStruct((tokens, rows), kind),
            jax.ShapeDtypeStruct((rows, 1), jnp.float32),
        ]
        out_specs += [
            pl.BlockSpec((tokens, block), lambda i: (0, i)),
            pl.BlockSpec((block, 1), lambda i: (i, 0)),
        ]
        flops += 2 * tokens * rows * pairs[-1][1].shape[1]
    result = pl.pallas_call(
        functools.partial(weight_grad_kernel, len(pairs), back is not None),
        grid=(rows // block,),
        in_specs=specs,
        out_specs=out_specs,
        out_shape=outs,
        compiler_params=pltpu.CompilerParams(vmem_limit_bytes=VMEM_LIMIT),
        cost_estimate=estimate(flops, 4 * tokens * rows + 2 * rows * total),
    )(*ins)
    return result if back is not None else result[0]


def feed_forward_kernel(hidden_width, x_ref, cot_ref, w_ref, grad_ref, hidden_ref, back_ref, out_ref):
    wide = 2 * hidden_width
    acts = mxu(x_ref[...], w_ref[:, :wide], NN)
    hidden_grad = mxu(cot_ref[...], w_ref[:, wide:], NN)
    gate, up = (acts[:, :hidden_width], acts[:, hidden_width:])
    sig = jax.nn.sigmoid(gate)
    silu = gate * sig
    grads = jnp.concatenate(
        [hidden_grad * up * (sig * (1.0 + gate * (1.0 - sig))), hidden_grad * silu], axis=1
    ).astype(jnp.bfloat16)
    grad_ref[...] = grads
    back_ref[...] = mxu(grads, w_ref[:, :wide], NT).astype(jnp.bfloat16)
    hidden = (silu * up).astype(jnp.bfloat16)
    hidden_ref[...] = hidden
    out_ref[...] = mxu(hidden, w_ref[:, wide:], NT).astype(jnp.bfloat16)


def feed_forward(x, cot, weights, rows):
    tokens, width = x.shape
    hidden_width = weights.shape[1] // 3
    by_rows = lambda columns: pl.BlockSpec((rows, columns), lambda i: (i, 0))
    sizes = (2 * hidden_width, hidden_width, width, width)
    return pl.pallas_call(
        functools.partial(feed_forward_kernel, hidden_width),
        grid=(tokens // rows,),
        in_specs=[by_rows(width), by_rows(width), pl.BlockSpec(weights.shape, lambda i: (0, 0))],
        out_specs=[by_rows(columns) for columns in sizes],
        out_shape=[jax.ShapeDtypeStruct((tokens, columns), jnp.bfloat16) for columns in sizes],
        compiler_params=pltpu.CompilerParams(vmem_limit_bytes=VMEM_LIMIT),
        cost_estimate=estimate(12 * tokens * width * hidden_width, 14 * tokens * width),
    )(x, cot, weights)


def finish_kernel(valid_ref, x_ref, mixer_ref, middle_ref, ffn_ref, out_ref, stat_ref):
    valid = valid_ref[...]
    middle, ffn = (middle_ref[...], ffn_ref[...])
    result = middle + ffn
    out_ref[...] = result.astype(jnp.bfloat16)
    tracked = (x_ref[...].astype(jnp.float32), mixer_ref[...], middle, ffn, result)
    stat_ref[...] = jnp.zeros_like(stat_ref)
    for k, values in enumerate(tracked):
        stat_ref[k : k + 1, 0:1] = jnp.sum(
            valid * jnp.sum(values * values, axis=1, keepdims=True), axis=0, keepdims=True
        )
    stat_ref[len(tracked) : len(tracked) + 1, 0:1] = jnp.sum(valid, axis=0, keepdims=True)


def finish(valid, x, mixer_sum, middle, ffn_out):
    return pl.pallas_call(
        finish_kernel,
        out_shape=[
            jax.ShapeDtypeStruct(x.shape, jnp.bfloat16),
            jax.ShapeDtypeStruct((8, 128), jnp.float32),
        ],
        compiler_params=pltpu.CompilerParams(vmem_limit_bytes=VMEM_LIMIT),
        cost_estimate=estimate(16 * x.size, 16 * x.size),
    )(valid, x, mixer_sum, middle, ffn_out)


def resumed(chain, sent):
    while True:
        got = yield sent
        try:
            sent = chain.send(got)
        except StopIteration as stop:
            return stop.value


def passengers(stages, *values):
    for _ in range(stages):
        yield []
    return (yield list(values))


def rope_rows(position):
    lane = jnp.arange(2 * HEAD_SIZE, dtype=jnp.int32)
    half = HEAD_SIZE // 2
    inverse = jnp.exp(
        (lane % half).astype(jnp.float32) * (-2.0 * math.log(ROPE_BASE) / HEAD_SIZE)
    )
    angles = position.astype(jnp.float32)[:, None] * inverse[None, :]
    sign = jnp.where(lane % HEAD_SIZE < half, -1.0, 1.0)
    return (jnp.cos(angles), jnp.sin(angles) * sign[None, :])
def grid_of(count):
    rows = 1
    while 8 * rows * rows <= count:
        rows *= 2
    return (count // rows, rows)


def ring_cycle(count):
    depth, rows = grid_of(count)
    order = []
    for level in range(depth):
        inner = list(range(1, rows))
        if level % 2:
            inner.reverse()
        order += [level * rows + row for row in inner]
    return order + [level * rows for level in reversed(range(depth))]


class Ring:
    def __init__(self, count):
        self.count = count
        self.order = ring_cycle(count)
        self.depth, self.rows = grid_of(count)
        inner = self.rows - 1
        mine = lax.axis_index("dp")
        level, row = (mine // self.rows, mine % self.rows)
        step = jnp.where(level % 2 == 0, row - 1, inner - row)
        self.spot = jnp.where(
            row > 0, level * inner + step, self.depth * inner + self.depth - 1 - level
        )

    def device_at(self, offset):
        inner = self.rows - 1
        spot = (self.spot + offset + self.count) % self.count
        level, step = (spot // inner, spot % inner)
        row = jnp.where(level % 2 == 0, step + 1, inner - step)
        back = self.count - 1 - spot
        return jnp.where(spot < self.depth * inner, level * self.rows + row, back * self.rows)

    def send(self, block, step):
        count, order = (self.count, self.order)
        return lax.ppermute(
            block, "dp", [(order[k], order[(k + step) % count]) for k in range(count)]
        )


def together(*values):
    return lax.optimization_barrier(values)


def lockstep(*chains):
    results = [None] * len(chains)
    waiting = {k: None for k in range(len(chains))}
    while waiting:
        sent = {}
        for k in list(waiting):
            try:
                sent[k] = chains[k].send(waiting[k])
            except StopIteration as stop:
                results[k] = stop.value
                del waiting[k]
        flat = [value for k in sent for value in sent[k]]
        if len(flat) > 1:
            flat = list(together(*flat))
        for k in sent:
            waiting[k] = flat[: len(sent[k])]
            flat = flat[len(sent[k]) :]
    return results


def after_stages(count, chain):
    for _ in range(count):
        yield []
    return (yield from chain)


def ring_gather(ring, whole, rows):
    count = ring.count
    half = rows // 2
    out = jnp.zeros((count * rows, whole.shape[1]), whole.dtype)
    more = jnp.zeros((count, whole.shape[0] - rows, whole.shape[1]), whole.dtype)

    def put(arrays, piece, offset, start=0):
        out, more = arrays
        device = ring.device_at(offset)
        kept = min(piece.shape[0], rows - start)
        out = lax.dynamic_update_slice_in_dim(out, piece[:kept], device * rows + start, 0)
        if piece.shape[0] > kept:
            more = lax.dynamic_update_index_in_dim(more, piece[kept:], device, 0)
        return (out, more)

    arrays = put((out, more), whole, 0)
    ahead = behind = whole
    for step in range(1, count // 2):
        ahead, behind = yield [ring.send(ahead, 1), ring.send(behind, -1)]
        arrays = put(arrays, ahead, -step)
        arrays = put(arrays, behind, step)
    ahead, behind = yield [ring.send(ahead[:half], 1), ring.send(behind[half:], -1)]
    arrays = put(arrays, ahead, -(count // 2))
    return put(arrays, behind, count // 2, half)


def ring_scatter(ring, *parts):
    count = ring.count
    rows = parts[0].shape[0] // count
    half = rows // 2

    def piece(offset, start=0, size=rows):
        first = ring.device_at(offset) * rows + start
        return jnp.concatenate(
            [lax.dynamic_slice_in_dim(part, first, size, 0).astype(jnp.float32) for part in parts],
            axis=1,
        )

    far = count // 2
    ahead = piece(far, 0, half).astype(jnp.bfloat16)
    behind = piece(far, half, rows - half).astype(jnp.bfloat16)
    for offset in range(far - 1, -1, -1):
        ahead, behind = yield [ring.send(ahead, 1), ring.send(behind, -1)]
        ahead, behind = (ahead.astype(jnp.float32), behind.astype(jnp.float32))
        if offset == far - 1:
            ahead, behind = (
                jnp.concatenate([ahead, jnp.zeros_like(behind)], axis=0),
                jnp.concatenate([jnp.zeros_like(ahead), behind], axis=0),
            )
        if offset:
            ahead = (ahead + piece(offset)).astype(jnp.bfloat16)
            behind = (behind + piece(-offset)).astype(jnp.bfloat16)
    return ahead + behind + piece(0)


def core_swap(block):
    count = lax.axis_size("tensor")
    return lax.ppermute(block, "tensor", [(k, k ^ 1) for k in range(count)])


def chip_shift(block, step):
    count = lax.axis_size("tensor")
    return lax.ppermute(block, "tensor", [(k, (k + 2 * step) % count) for k in range(count)])


def tensor_parts(block):
    chips = lax.axis_size("tensor") // 2
    mate, *others = yield [core_swap(block)] + [chip_shift(block, k) for k in range(1, chips)]
    mates = yield [core_swap(other) for other in others]
    parts = [block, mate]
    for other, beside in zip(others, mates):
        parts += [other, beside]
    return parts


def in_order(parts):
    chips = len(parts) // 2
    mine = lax.axis_index("tensor")
    flipped = mine % 2 == 1
    pairs = []
    for chip in range(chips):
        first, second = (parts[2 * chip], parts[2 * chip + 1])
        pairs.append((jnp.where(flipped, second, first), jnp.where(flipped, first, second)))
    out = []
    for chip in range(chips):
        back = (mine // 2 + chips - chip) % chips
        for core in range(2):
            value = pairs[0][core]
            for step in range(1, chips):
                value = jnp.where(back == step, pairs[step][core], value)
            out.append(value)
    return out


def seq_gather(values):
    parts = yield from tensor_parts(values)
    return jnp.concatenate(parts, axis=0)


def tensor_scatter(pick):
    chips = lax.axis_size("tensor") // 2
    places = [2 * (chips - step) for step in range(1, chips)]
    mate, *others = yield [core_swap(pick(place + 1)) for place in [0] + places]
    merged = [
        (pick(place).astype(jnp.float32) + other.astype(jnp.float32)).astype(jnp.bfloat16)
        for place, other in zip(places, others)
    ]
    received = yield [chip_shift(value, k + 1) for k, value in enumerate(merged)]
    total = pick(0).astype(jnp.float32) + mate.astype(jnp.float32)
    for other in received:
        total = total + other.astype(jnp.float32)
    return total


def seq_reduce(lowered):
    rows = lowered.shape[0] // lax.axis_size("tensor")
    return tensor_scatter(lambda place: lowered[place * rows : (place + 1) * rows])


def width_total(values):
    chips = lax.axis_size("tensor") // 2
    blocks = values.reshape(chips, 2, -1)
    blocks = blocks + core_swap(blocks)[:, ::-1]
    total = blocks
    for step in range(1, chips):
        total = total + jnp.roll(chip_shift(blocks, step), step, axis=0)
    return total.reshape(values.shape)


def exchange(blocks, axes):
    return lax.all_to_all(blocks, axes, 0, 0, tiled=False)


def dp_scatter(values):
    blocks = values.astype(jnp.bfloat16).reshape((lax.axis_size("dp"), -1) + values.shape[1:])
    return jnp.sum(exchange(blocks, "dp").astype(jnp.float32), axis=0)


def run(chain):
    return lockstep(chain)[0]


def local(
    layer_input,
    out_grad,
    segment_ids,
    valid_mask,
    doc_start,
    norm_gains,
    conv_weight,
    conv_bias,
    mixer_gain,
    shared_proj,
    step_bias,
    decay_log,
    skip_gain,
    mamba_gate,
    mamba_input,
    mamba_step,
    query_proj,
    mamba_out,
    attention_out,
    swiglu_gate,
    swiglu_up,
    swiglu_down,
):
    tensor_position = lax.axis_index("tensor")
    dp_count = lax.axis_size("dp")
    tensor_count = lax.axis_size("tensor")
    device = lax.axis_index("dp") * tensor_count + tensor_position
    ring = Ring(dp_count)
    local_width = mamba_gate.shape[1]
    query_width = query_proj.shape[1]
    head_local = mamba_step.shape[1]
    hidden_width = swiglu_gate.shape[1]
    query_slice = query_width // HEAD_SIZE
    slab = 2 * HEAD_SIZE
    wide = -(-local_width // slab) * slab
    early_width = wide + slab
    block_rows = layer_input.shape[0]
    tokens_per_group = block_rows * tensor_count
    seq_count = tokens_per_group // SEQUENCE_TOKENS
    channel_start = tensor_position * local_width
    head_start = tensor_position * head_local
    channels = conv_weight.shape[1] * dp_count * tensor_count

    def padded(values, columns):
        return jnp.pad(values, ((0, 0), (0, columns - values.shape[1])))

    def placed(rows_in, columns, start):
        whole = jnp.zeros((rows_in.shape[0], columns), rows_in.dtype)
        return lax.dynamic_update_slice_in_dim(whole, rows_in, start, 1)

    device_count = dp_count * tensor_count
    rows_in = mamba_gate.shape[0]
    shared_rows = shared_proj.shape[0]
    small = jnp.concatenate(
        [norm_gains.reshape(-1), conv_weight.reshape(-1), conv_bias, mixer_gain]
    )
    small_width = -(-small.shape[0] // 128) * 128
    if small_width > shared_proj.shape[1]:
        raise ValueError("small parameters")
    small = jnp.pad(small, (0, shared_proj.shape[1] - small.shape[0]))
    small = jnp.pad(small[None], ((0, 7), (0, 0)))
    common = lax.all_gather(jnp.concatenate([shared_proj, small], axis=0), "tensor", axis=0)
    shared_own = common[:, :shared_rows].reshape(rows_in, -1)
    small_own = common[:, shared_rows, :small_width].reshape(1, -1)
    valid_f = valid_mask.astype(jnp.float32)
    out_cot = out_grad.astype(jnp.float32) * valid_f[:, None]
    layer_input, shared_own = together(layer_input, shared_own)
    block = pack(
        rows_in,
        (
            (mamba_gate, wide, False),
            (query_proj, slab, False),
            (mamba_out, local_width, True),
            (attention_out, query_width, True),
            (mamba_input, wide, False),
            (mamba_step, slab, False),
            (shared_own, shared_proj.shape[1], False),
        ),
        jnp.broadcast_to(small_own, (8, small_own.shape[1])),
    )

    def prepared():
        spots, gate, up, down = yield [doc_start, swiglu_gate, swiglu_up, swiglu_down]
        position = jnp.tile(jnp.arange(SEQUENCE_TOKENS, dtype=jnp.int32), seq_count) - spots
        ffn_block = pack(
            rows_in,
            ((gate, hidden_width, False), (up, hidden_width, False), (down, hidden_width, True)),
        )
        ffn_blocks = jnp.broadcast_to(ffn_block[None], (dp_count,) + ffn_block.shape)
        cosines, sines, ffn_blocks = yield [*rope_rows(position), ffn_blocks]
        return (ffn_blocks, cosines, sines)

    x_full, (w_in, small_all), ffn_grad_in, waited = lockstep(
        seq_gather(layer_input),
        ring_gather(ring, block, rows_in),
        after_stages(1, seq_gather(out_cot.astype(jnp.bfloat16))),
        prepared(),
    )
    ffn_blocks, cosine_table, sine_table = waited
    w_in, ffn_grad_in, ffn_blocks = together(w_in, ffn_grad_in, ffn_blocks)
    w_ffn = exchange(ffn_blocks, "dp").reshape(D, -1)
    shared_at = w_in.shape[1] - shared_proj.shape[1]
    late_at = early_width + local_width + query_width
    w_out = w_in[:, early_width:late_at]
    gains_f, conv_f, mixer_gain_f = unpack(
        small_all[:, 0],
        tensor_count,
        small_width,
        (
            (2, norm_gains.shape[1]),
            (CONV + 1, conv_weight.shape[1]),
            (1, mixer_gain.shape[0]),
        ),
    )
    tokens_f = layer_input.astype(jnp.float32)
    scale_one = rms_scale(tokens_f)
    first_full, early_act, late_act, common_act = project(
        x_full,
        gains_f,
        (
            (w_in, early_width, 0),
            (w_in, early_width, late_at),
            (w_in, shared_proj.shape[1], shared_at),
        ),
        block_rows,
    )
    taps = jnp.concatenate(
        [lax.dynamic_slice_in_dim(conv_f, channel_start, local_width, 1), conv_f[:, DSSM:]], axis=1
    )
    own_gain = lax.dynamic_slice_in_dim(mixer_gain_f[0], channel_start, local_width, 0)
    own_bias = lax.dynamic_slice_in_dim(step_bias, head_start, head_local, 0)
    own_decay = lax.dynamic_slice_in_dim(decay_log, head_start, head_local, 0)
    own_skip = lax.dynamic_slice_in_dim(skip_gain, head_start, head_local, 0)
    params = jnp.pad(
        jnp.stack([own_bias, -jnp.exp(own_decay)], axis=0), ((0, 6), (0, slab - head_local))
    )
    skip_row = jnp.broadcast_to(jnp.repeat(own_skip, HEAD_SIZE)[None], (8, local_width))
    doc = doc_start[:, None]
    kv = (tensor_position * query_slice // (QUERY_HEADS // KEY_VALUE_HEADS)).astype(jnp.int32)[None]
    device_ids = jnp.arange(tensor_count, dtype=jnp.int32)
    chip_count = tensor_count // 2
    block_order = (tensor_position // 2 + chip_count - device_ids // 2) % chip_count * 2 + (
        tensor_position + device_ids
    ) % 2

    mamba_y, square_rows, kept_states = mamba_forward(
        block_order, block_rows, early_act, late_act, common_act, doc, taps, params, skip_row
    )
    attended, query_rot, key_rot, value_low, log_total = attention_forward(
        kv, block_order, block_rows, early_act, common_act, cosine_table, sine_table, doc
    )
    square_sum = width_total(square_rows[0])
    gate_scale = lax.rsqrt(square_sum / DSSM + EPS)[:, None]
    gate_z = early_act[:, :local_width]
    sigmoid_z = jax.nn.sigmoid(gate_z)
    silu_z = gate_z * sigmoid_z
    gated_y = mamba_y * silu_z
    normed_b = (gated_y * gate_scale * own_gain).astype(jnp.bfloat16)
    mixed_b = jnp.concatenate([normed_b, attended[:, :query_width]], axis=1)
    mixer_part = product_nt(mixed_b, w_out).astype(jnp.bfloat16)
    mixer_sum = run(seq_reduce(mixer_part))

    middle = tokens_f + mixer_sum
    scale_two = rms_scale(middle)
    second_b = (middle * scale_two * gains_f[1]).astype(jnp.bfloat16)
    ffn_in = run(seq_gather(second_b))
    gate_up_grad, hidden_b, second_part, ffn_part = feed_forward(
        ffn_in, ffn_grad_in, w_ffn, block_rows
    )
    ffn_in, ffn_grad_in, second_part, mixed_b = together(ffn_in, ffn_grad_in, second_part, mixed_b)
    second_grad = run(seq_reduce(second_part))
    ffn_w_grad = weight_grads(((ffn_in, gate_up_grad), (ffn_grad_in, hidden_b)))
    second_value_grad, gain_two_grad = norm_back(middle, scale_two, gains_f[1], second_grad)
    middle_grad = out_cot + second_value_grad
    middle_grad, ffn_w_grad = together(middle_grad, ffn_w_grad)

    gathered = seq_gather(middle_grad.astype(jnp.bfloat16))
    mate, *others = next(gathered)
    mate, ffn_w_grad = together(mate, ffn_w_grad)
    ffn_w_grad = dp_scatter(ffn_w_grad)
    mixer_grad_full = run(resumed(gathered, [mate, *others]))
    ffn_part, mixer_grad_full = together(ffn_part, mixer_grad_full)
    mixed_grad = product(mixer_grad_full, w_out)
    normed_grad = mixed_grad[:, :local_width]
    scaled_normed = normed_grad * own_gain
    inner_sum = width_total(jnp.sum(scaled_normed * gated_y, axis=1))
    attended_grad, attended_at = (mixed_grad, local_width // slab)
    if local_width % slab or query_width != slab:
        attended_grad, attended_at = (padded(mixed_grad[:, local_width:], slab), 0)
    dq, dkv = attention_backward(
        kv,
        block_order,
        block_rows,
        query_rot,
        key_rot,
        value_low,
        cosine_table,
        sine_table,
        doc,
        log_total,
        attended_grad,
        attended_at,
    )
    own_gain_grad = jnp.sum(normed_grad * gated_y * gate_scale, axis=0)
    gated_grad = (
        gate_scale * scaled_normed
        - gated_y * (gate_scale * gate_scale * gate_scale) * (inner_sum / DSSM)[:, None]
    )
    mamba_y_grad = gated_grad * silu_z
    gate_z_grad = (gated_grad * mamba_y * sigmoid_z * (1.0 + gate_z * (1.0 - sigmoid_z))).astype(
        jnp.bfloat16
    )
    early_grad = jnp.concatenate([padded(gate_z_grad, wide), dq], axis=1)
    early_w_grad, first_early, gain_one_early = weight_grads(
        ((mixer_grad_full, mixed_b), (first_full, early_grad)), (w_in, 0)
    )
    early_ring = ring_scatter(ring, early_w_grad)
    early_sent = next(early_ring)
    ffn_out = run(seq_reduce(ffn_part))
    mamba_y_grad, first_early = together(mamba_y_grad, first_early)
    late_grad, taps_grad, params_grad = mamba_backward(
        block_order,
        block_rows,
        late_act,
        common_act,
        doc,
        taps,
        params,
        skip_row,
        mamba_y,
        mamba_y_grad,
        dkv,
        kept_states,
    )

    late_grad, ffn_w_grad, *early_sent = together(late_grad, ffn_w_grad, *early_sent)
    gate_w_grad = ffn_w_grad[:, :hidden_width]
    up_w_grad = ffn_w_grad[:, hidden_width : 2 * hidden_width]
    down_w_grad = ffn_w_grad[:, 2 * hidden_width :].T
    early_sent = early_ring.send(early_sent)
    back = (w_in, late_at // late_grad.shape[1])
    if late_at % late_grad.shape[1]:
        back = (w_in[:, late_at:], 0)
    late_w_grad, first_part, gain_one_late = weight_grads(
        ((first_full, late_grad),), back, first_early
    )
    def summed(taps_grad, params_grad, gain_one_late, ffn_out):
        taps_grad, params_grad, gain_one_late, ffn_out = yield [
            taps_grad,
            params_grad,
            gain_one_late,
            ffn_out,
        ]
        result_b, stat_terms = finish(valid_f[:, None], layer_input, mixer_sum, middle, ffn_out)
        gain_one_grad = (gain_one_early + gain_one_late)[:, 0] / gains_f[0]
        heads = jnp.concatenate(
            [
                placed(params_grad[:3, :head_local], slab, head_start),
                padded(stat_terms[:6, 0][None], slab),
            ],
            axis=0,
        )
        conv_rows = jnp.concatenate(
            [
                placed(taps_grad[: CONV + 1, :local_width], DSSM, channel_start),
                taps_grad[: CONV + 1, local_width:],
            ],
            axis=1,
        )
        sums = gather_sums(
            device_count,
            (
                jnp.stack([gain_one_grad, gain_two_grad], axis=0),
                conv_rows,
                placed(own_gain_grad[None], DSSM, channel_start),
            ),
            ((2, norm_gains.shape[1]), (CONV + 1, conv_weight.shape[1]), (1, mixer_gain.shape[0])),
            heads,
            (MH, MH, MH, 6),
        )
        (sums,) = yield [sums]
        (got,) = yield [exchange(sums, ("dp", "tensor"))]
        outputs = spread_sums(
            got,
            (
                (2, norm_gains.shape[1]),
                (CONV, conv_weight.shape[1]),
                (1, conv_weight.shape[1]),
                (1, mixer_gain.shape[0]),
                (1, MH),
                (1, MH),
                (1, MH),
                (1, 6),
            ),
        )
        stats = outputs[-1][0]
        return (yield list(outputs[:-1]) + [jnp.sqrt(stats[:5] / (stats[5] * D)), result_b])

    def finished(part):
        first_grad = yield from seq_reduce(part)
        first_value_grad, _ = norm_back(tokens_f, scale_one, gains_f[0], first_grad)
        return (yield [middle_grad + first_value_grad])

    late_total, early_total, (input_grad,), outputs = lockstep(
        ring_scatter(ring, late_w_grad),
        resumed(early_ring, early_sent),
        after_stages(1, finished(first_part)),
        summed(taps_grad, params_grad, gain_one_late, ffn_out),
    )
    shared_total = late_total[:, early_width:].astype(jnp.bfloat16)
    places = [
        ((tensor_position // 2 + chip_count - place // 2) % chip_count) * 2
        + (tensor_position + place) % 2
        for place in range(tensor_count)
    ]
    shared_proj_grad = run(
        tensor_scatter(
            lambda place: lax.dynamic_slice_in_dim(
                shared_total, places[place] * shared_rows, shared_rows, 0
            )
        )
    )
    mamba_out_grad = early_total[:, :local_width].T
    attend_out_grad = early_total[:, local_width : local_width + query_width].T
    early_at = local_width + query_width
    gate_proj_grad = early_total[:, early_at : early_at + local_width]
    query_proj_grad = early_total[:, early_at + wide : early_at + wide + query_width]
    input_proj_grad = late_total[:, :local_width]
    step_proj_grad = late_total[:, wide : wide + head_local]
    gains_grad, conv_w_grad, conv_b_grad, gain_full_grad, bias_total, decay_total, skip_total, rms, result_b = outputs
    return (
        result_b,
        input_grad,
        gains_grad,
        conv_w_grad,
        conv_b_grad[0],
        gain_full_grad[0],
        shared_proj_grad,
        bias_total[0],
        decay_total[0],
        skip_total[0],
        gate_proj_grad,
        input_proj_grad,
        step_proj_grad,
        query_proj_grad,
        mamba_out_grad,
        attend_out_grad,
        gate_w_grad,
        up_w_grad,
        down_w_grad,
        rms,
    )


def solution(mesh):
    in_specs = (
        P(("dp", "tensor"), None),
        P(("dp", "tensor"), None),
        P("dp"),
        P(("dp", "tensor")),
        P("dp"),
        P(None, ("dp", "tensor")),
        P(None, ("dp", "tensor")),
        P(("dp", "tensor")),
        P(("dp", "tensor")),
        P(("dp", "tensor"), None),
        P(),
        P(),
        P(),
        P("dp", "tensor"),
        P("dp", "tensor"),
        P("dp", "tensor"),
        P("dp", "tensor"),
        P("tensor", "dp"),
        P("tensor", "dp"),
        P("dp", "tensor"),
        P("dp", "tensor"),
        P("tensor", "dp"),
    )
    out_specs = (
        P(("dp", "tensor"), None),
        P(("dp", "tensor"), None),
        P(None, ("dp", "tensor")),
        P(None, ("dp", "tensor")),
        P(("dp", "tensor")),
        P(("dp", "tensor")),
        P(("dp", "tensor"), None),
        P(),
        P(),
        P(),
        P("dp", "tensor"),
        P("dp", "tensor"),
        P("dp", "tensor"),
        P("dp", "tensor"),
        P("tensor", "dp"),
        P("tensor", "dp"),
        P("dp", "tensor"),
        P("dp", "tensor"),
        P("tensor", "dp"),
        P(),
    )
    return jax.shard_map(local, mesh=mesh, in_specs=in_specs, out_specs=out_specs, check_vma=False)
```
